32 devices in a mesh: row: 8 (over z, core), col: 4 (over y, x).
Axes of the slice: x: 2, y: 2, z: 4, core: 2. Of those that a mesh axis runs over, the one named last changes fastest.
Arguments:
- hidden: bfloat16 [16384, 2560], P(('row', 'col')), may hold values from -6 to 6
- in_gain: bfloat16 [2560], P('col'), may hold values from 0.5 to 1.5
- w_gate: bfloat16 [2560, 5120], P('row', 'col'), may hold values from -0.125 to 0.125
- w_value: bfloat16 [2560, 5120], P('row', 'col'), may hold values from -0.125 to 0.125
- w_bc: bfloat16 [2560, 256], P('row', 'col'), may hold values from -0.125 to 0.125
- w_step: bfloat16 [2560, 80], P('row', 'col'), may hold values from -0.125 to 0.125
- conv_value: float32 [4, 5120], P(None, 'col'), may hold values from -3 to 3
- conv_value_bias: float32 [5120], P('col'), may hold values from -0.5 to 0.5
- conv_bc: float32 [4, 256], P(None, 'col'), may hold values from -3 to 3
- conv_bc_bias: float32 [256], P('col'), may hold values from -0.5 to 0.5
- step_bias: float32 [80], P('col'), may hold values from -6 to -2
- decay_log: float32 [80], P('col'), may hold values from 0 to 2.5
- skip_gain: float32 [80], P('col'), may hold values from 0.5 to 1.5
- norm_gain: float32 [5120], P('col'), may hold values from 0.5 to 1.5
- w_out: bfloat16 [5120, 2560], P('col', 'row'), may hold values from -0.078125 to 0.078125
- grad_out: bfloat16 [16384, 2560], P(('row', 'col')), may hold values from -6 to 6
Outputs:
- out: bfloat16 [16384, 2560], P(('row', 'col'))
- grad_hidden: float32 [16384, 2560], P(('row', 'col'))
- grad_in_gain: float32 [2560], P('col')
- grad_w_gate: float32 [2560, 5120], P('row', 'col')
- grad_w_value: float32 [2560, 5120], P('row', 'col')
- grad_w_bc: float32 [2560, 256], P('row', 'col')
- grad_w_step: float32 [2560, 80], P('row', 'col')
- grad_conv_value: float32 [4, 5120], P(None, 'col')
- grad_conv_value_bias: float32 [5120], P('col')
- grad_conv_bc: float32 [4, 256], P(None, 'col')
- grad_conv_bc_bias: float32 [256], P('col')
- grad_step_bias: float32 [80], P('col')
- grad_decay_log: float32 [80], P('col')
- grad_skip_gain: float32 [80], P('col')
- grad_norm_gain: float32 [5120], P('col')
- grad_w_out: float32 [5120, 2560], P('col', 'row')
The draws below stay inside these ranges and needn't reach their ends.
All inputs are finite; a program needn't handle non-finite values.
Results may differ from the reference program's by a relative error of at most 0.018.
Values may be sent and summed in bfloat16 or wider, within the bound.
No kernel may reach another device: no remote copies, remote signals or barrier semaphores. Data moves between devices by JAX's collectives and lax.ppermute only.
A program may use at most 256 MiB of HBM per device.

```python
import jax
import jax.numpy as jnp
from jax import lax

D = 2560
H = 80
P_SIZE = 64
N = 128
E = 5120
K = 4
GROUP = 256
ROW_TOK = 2048
TOKENS = 16384
N_ROW = 8


def block_scale(key, shape, cuts, least, top_value):
    def one(axis_at, shards_of):
        steps = jax.random.uniform(jax.random.fold_in(jax.random.fold_in(key, 6), axis_at), (shards_of,), jnp.float32, least / len(cuts), top_value / len(cuts))
        return jnp.repeat(jnp.exp(steps), shape[axis_at] // shards_of).reshape((-1,) + (1,) * (len(shape) - axis_at - 1))

    loudness = one(*cuts[0])
    for cut in cuts[1:]:
        loudness = loudness * one(*cut)
    return loudness


def noise(key, dims, width, most, split=(), held_as=jnp.bfloat16):
    factor_of = block_scale(key, dims, split, -0.22, 0.18) if split else 1.0
    values = jax.random.normal(key, dims, jnp.float32) * width * factor_of
    return jnp.minimum(jnp.maximum(values, -most), most).astype(held_as)


def setup_inputs(seed: int = 0) -> dict:
    keys = jax.random.split(jax.random.key(seed), 17)
    hidden = noise(keys[0], (TOKENS, D), 1.0, 6.0, ((0, 32),))
    in_gain = jnp.clip(1.0 + 0.1 * jax.random.normal(keys[1], (D,), jnp.float32), 0.5, 1.5).astype(jnp.bfloat16)
    w_gate = noise(keys[2], (D, E), D ** -0.5, 0.125, ((0, 8), (1, 4)))
    w_value = noise(keys[3], (D, E), D ** -0.5, 0.125, ((0, 8), (1, 4)))
    w_bc = noise(keys[4], (D, 2 * N), D ** -0.5, 0.125, ((0, 8), (1, 4)))
    w_step = noise(keys[5], (D, H), D ** -0.5, 0.125, ((0, 8), (1, 4)))
    conv_value = noise(keys[6], (K, E), K ** -0.5, 3.0, ((1, 4),), jnp.float32)
    conv_value_bias = jnp.clip(jax.random.uniform(keys[7], (E,), jnp.float32, -0.5, 0.5) * block_scale(keys[7], (E,), ((0, 4),), -0.4, 0.0), -0.5, 0.5)
    conv_bc = noise(keys[8], (K, 2 * N), K ** -0.5, 3.0, ((1, 4),), jnp.float32)
    conv_bc_bias = jnp.clip(jax.random.uniform(keys[9], (2 * N,), jnp.float32, -0.5, 0.5) * block_scale(keys[9], (2 * N,), ((0, 4),), -0.4, 0.0), -0.5, 0.5)
    step_bias = jnp.clip(-6.0 + 4.0 * jax.random.uniform(keys[10], (H,), jnp.float32) ** block_scale(keys[10], (H,), ((0, 4),), -0.2, 0.2), -6.0, -2.0)
    decay_log = jnp.clip(2.5 * jax.random.uniform(keys[11], (H,), jnp.float32) ** block_scale(keys[11], (H,), ((0, 4),), -0.2, 0.2), 0.0, 2.5)
    skip_gain = jnp.clip(0.5 + 1.0 * jax.random.uniform(keys[12], (H,), jnp.float32) ** block_scale(keys[12], (H,), ((0, 4),), -0.2, 0.2), 0.5, 1.5)
    norm_gain = jnp.clip(1.0 + 0.1 * jax.random.normal(keys[13], (E,), jnp.float32), 0.5, 1.5)
    w_out = noise(keys[14], (E, D), E ** -0.5, 0.078125, ((0, 4), (1, 8)))
    grad_out = noise(keys[15], (TOKENS, D), 1.0, 6.0, ((0, 32),))
    return dict(hidden=hidden, in_gain=in_gain, w_gate=w_gate, w_value=w_value, w_bc=w_bc, w_step=w_step, conv_value=conv_value, conv_value_bias=conv_value_bias, conv_bc=conv_bc, conv_bc_bias=conv_bc_bias, step_bias=step_bias, decay_log=decay_log, skip_gain=skip_gain, norm_gain=norm_gain, w_out=w_out, grad_out=grad_out)


EPSILON = 1e-05
HIGH = lax.Precision.HIGHEST

@jax.custom_vjp
def low(v):
    return lax.optimization_barrier(v.astype(jnp.bfloat16)).astype(jnp.float32)

@jax.custom_vjp
def low_back(v):
    return v

def low_keep(v):
    return (low(v), None)

def low_pass(kept, grad):
    return (grad,)

def back_keep(v):
    return (v, None)

def back_low(kept, grad):
    return (low(grad),)
low.defvjp(low_keep, low_pass)
low_back.defvjp(back_keep, back_low)

def swish(value_in):
    return value_in * jax.nn.sigmoid(value_in)

def causal_conv(values, taps, offsets):
    tap_count = taps.shape[0]
    length = values.shape[0]
    padded = jnp.pad(values, ((tap_count - 1, 0), (0, 0)))
    summed = offsets[None, :] + taps[0][None, :] * padded[0:length]
    for offset in range(1, tap_count):
        summed = summed + taps[offset][None, :] * padded[offset:offset + length]
    return summed

def block_scan(inner_vals, step_sizes, decay_rates, b_rows, c_rows, skips, block_len):
    length, head_num, head_dim = inner_vals.shape
    blocks = length // block_len
    state_dim = b_rows.shape[1]
    causal = jnp.tril(jnp.ones((block_len, block_len), inner_vals.dtype))
    split_vals = inner_vals.reshape(blocks, block_len, head_num, head_dim)
    split_steps = step_sizes.reshape(blocks, block_len, head_num)
    split_b = b_rows.reshape(blocks, block_len, state_dim)
    split_c = c_rows.reshape(blocks, block_len, state_dim)

    def block_step(carried, pieces):
        values_in, steps_here, b_here, c_here = pieces
        log_sums = jnp.cumsum(steps_here * decay_rates[None, :], axis=0)
        gaps = log_sums[:, None, :] - log_sums[None, :, :]
        decays = jnp.exp(jnp.where(causal[:, :, None] > 0, gaps, 0.0)) * causal[:, :, None]
        scores = jnp.dot(c_here, b_here.T, precision=HIGH)
        mixing = scores[:, :, None] * decays * steps_here[None, :, :]
        inside = jnp.einsum('tsh,shp->thp', mixing, values_in, precision=HIGH)
        across = jnp.einsum('tn,hpn->thp', c_here, carried, precision=HIGH) * jnp.exp(log_sums)[:, :, None]
        block_end = log_sums[-1]
        carry_weight = jnp.exp(block_end[None, :] - log_sums) * steps_here
        updated = carried * jnp.exp(block_end)[:, None, None] + jnp.einsum('sh,shp,sn->hpn', carry_weight, values_in, b_here, precision=HIGH)
        return (updated, inside + across + skips[None, :, None] * values_in)
    start_state = jnp.zeros((head_num, head_dim, state_dim), inner_vals.dtype)
    last_state, results = lax.scan(jax.checkpoint(block_step), start_state, (split_vals, split_steps, split_b, split_c))
    return results.reshape(length, head_num, head_dim)

def layer(hidden, in_gain, w_gate, w_value, w_bc, w_step, conv_value, conv_value_bias, conv_bc, conv_bc_bias, step_bias, decay_log, skip_gain, norm_gain, w_out):

    def one_sequence(tokens):
        scaling = lax.rsqrt(lax.optimization_barrier(jnp.mean(tokens * tokens, axis=1, keepdims=True)) + EPSILON)
        normal_in = low(tokens * scaling * in_gain)
        gate_pre = low_back(jnp.dot(normal_in, w_gate, precision=HIGH))
        value_pre = low_back(jnp.dot(normal_in, w_value, precision=HIGH))
        bc_pre = low_back(jnp.dot(normal_in, w_bc, precision=HIGH))
        step_pre = low_back(jnp.dot(normal_in, w_step, precision=HIGH))
        inner_vals = swish(causal_conv(value_pre, conv_value, conv_value_bias))
        state_in = low(swish(causal_conv(bc_pre, conv_bc, conv_bc_bias)))
        step_sizes = jax.nn.softplus(step_pre + step_bias)
        decay_rates = -jnp.exp(decay_log)
        heads_out = block_scan(inner_vals.reshape(ROW_TOK, H, P_SIZE), step_sizes, decay_rates, state_in[:, :N], state_in[:, N:], skip_gain, GROUP)
        gated_vals = heads_out.reshape(ROW_TOK, E) * swish(gate_pre)
        gated_scale = lax.rsqrt(lax.optimization_barrier(jnp.mean(gated_vals * gated_vals, axis=1, keepdims=True)) + EPSILON)
        normed = low(gated_vals * gated_scale * norm_gain)
        return tokens + jnp.dot(normed, w_out, precision=HIGH)
    sequences = hidden.reshape(N_ROW, ROW_TOK, D)
    return lax.map(jax.checkpoint(one_sequence), sequences).reshape(TOKENS, D)

def reference(hidden, in_gain, w_gate, w_value, w_bc, w_step, conv_value, conv_value_bias, conv_bc, conv_bc_bias, step_bias, decay_log, skip_gain, norm_gain, w_out, grad_out):
    floats = tuple((array.astype(jnp.float32) for array in (hidden, in_gain, w_gate, w_value, w_bc, w_step, conv_value, conv_value_bias, conv_bc, conv_bc_bias, step_bias, decay_log, skip_gain, norm_gain, w_out)))
    result, pullback = jax.vjp(layer, *floats)
    grads = pullback(grad_out.astype(jnp.float32))
    return (result.astype(jnp.bfloat16), grads[0], grads[1], grads[2], grads[3], grads[4], grads[5], grads[6], grads[7], grads[8], grads[9], grads[10], grads[11], grads[12], grads[13], grads[14])
```

```python
import functools
import jax
import jax.numpy as jnp
from jax import lax
from jax.experimental import pallas as pl
from jax.experimental.pallas import tpu as pltpu
from jax.sharding import PartitionSpec as P

P_SIZE = 64
N = 128
Q = 128
LANES = 128
NEG = -1e30
HIGH = lax.Precision.HIGHEST
F32 = jnp.float32
BF16 = jnp.bfloat16


def sigmoid(v):
    return 0.5 * jnp.tanh(0.5 * v) + 0.5


def nt_dot(a, b):
    return lax.dot_general(a, b, (((1,), (1,)), ((), ())), preferred_element_type=F32)


def mm(a, b):
    return jnp.dot(a, b, preferred_element_type=F32)


def mm_exact(a, b):
    return jnp.dot(a, b, precision=HIGH, preferred_element_type=F32)


def turned(m):
    return m.astype(F32).T.astype(BF16)


def pair_cols(low_half, cols, first):
    return jnp.where(low_half, cols[:, first : first + 1], cols[:, first + 1 : first + 2])


def halves(low_half, v):
    zero = jnp.zeros_like(v)
    return jnp.concatenate([jnp.where(low_half, v, zero), jnp.where(low_half, zero, v)], axis=0)


def conv_at(halo, taps_ref, bias_ref, cols, start):
    total = bias_ref[:, cols] + taps_ref[0:1, cols] * halo[start : start + Q, cols]
    for k in range(1, 4):
        total = total + taps_ref[k : k + 1, cols] * halo[start + k : start + k + Q, cols]
    return total


def scan_forward(
    seat_ref, vp_ref, bc_ref, st_ref, taps_ref, bias_ref, rate_ref, skip_ref,
    y_ref, hold_ref, state, halo, *, pairs
):
    @pl.when(pl.program_id(0) == 0)
    def _():
        state[...] = jnp.zeros_like(state)
        halo[0:8, :] = jnp.zeros_like(halo[0:8, :])

    halo[8 : 8 + Q, :] = vp_ref[...].astype(F32)
    rows = lax.broadcasted_iota(jnp.int32, (Q, Q), 0)
    lanes = lax.broadcasted_iota(jnp.int32, (Q, Q), 1)
    causal = rows >= lanes
    low_half = lanes < P_SIZE
    steps = st_ref[...]
    lam = mm_exact(causal.astype(F32), steps * rate_ref[...])
    source_t = (lam - jnp.log(steps)).T
    grown = jnp.exp(lam)
    last = lam[Q - 1 : Q, :]
    weight = jnp.exp(last - lam) * steps
    fade = jnp.exp(last)
    b_rows = bc_ref[:, :N]
    c_rows = bc_ref[:, N:]
    b_t = turned(b_rows)
    scores = nt_dot(c_rows, b_rows)
    for pair in range(pairs):
        cols = slice(pair * LANES, (pair + 1) * LANES)
        first = 2 * pair
        conv = conv_at(halo, taps_ref, bias_ref, cols, 5)
        x = conv * sigmoid(conv)
        mixing = []
        for h in (first, first + 1):
            gap = jnp.where(causal, lam[:, h : h + 1] - source_t[h : h + 1, :], NEG)
            mixing.append((scores * jnp.exp(gap)).astype(BF16))
        y = mm(jnp.concatenate(mixing, axis=1), halves(low_half, x).astype(BF16))
        held = state[:, cols]
        held_low = held.astype(BF16)
        y = y + mm(c_rows, held_low) * pair_cols(low_half, grown, first)
        y = y + skip_ref[:, cols] * x
        y_ref[:, cols] = y.astype(y_ref.dtype)
        hold_ref[0, :, cols] = held_low
        fed = (x * pair_cols(low_half, weight, first)).astype(BF16)
        state[:, cols] = held * pair_cols(low_half[0:1], fade, first) + mm(b_t, fed)
    halo[0:8, :] = halo[Q : Q + 8, :]


def scan_backward(
    seat_ref, vp_ref, before_ref, dy_ref, bc_ref, st_ref, hold_ref, taps_ref, bias_ref, rate_ref, skip_ref, pick_ref,
    dvp_ref, dbc_ref, dst_ref, gconv_ref, gdecay_ref,
    halo, gbuf, ds, ds_low, across, r_cols, w_rows, state_terms, inter_terms, fed_all, dyl_all, e_rows, *, pairs, blocks
):
    step_id = pl.program_id(0)

    @pl.when(step_id == 0)
    def _():
        ds[...] = jnp.zeros_like(ds)
        gbuf[Q : Q + 8, :] = jnp.zeros_like(gbuf[Q : Q + 8, :])
        gconv_ref[...] = jnp.zeros_like(gconv_ref)
        gdecay_ref[...] = jnp.zeros_like(gdecay_ref)
        r_cols[...] = jnp.zeros_like(r_cols)
        w_rows[...] = jnp.zeros_like(w_rows)
        e_rows[...] = jnp.zeros_like(e_rows)

    halo[16 : 16 + Q, :] = vp_ref[...].astype(F32)

    @pl.when(step_id < blocks - 1)
    def _():
        halo[0:16, :] = before_ref[...].astype(F32)

    @pl.when(step_id == blocks - 1)
    def _():
        halo[0:16, :] = jnp.zeros_like(halo[0:16, :])

    rows = lax.broadcasted_iota(jnp.int32, (Q, Q), 0)
    lanes = lax.broadcasted_iota(jnp.int32, (Q, Q), 1)
    causal = rows >= lanes
    later = lanes >= rows
    low_half = lanes < P_SIZE
    steps = st_ref[...]
    rate = rate_ref[...]
    lam = mm_exact(causal.astype(F32), steps * rate)
    lam_t = lam.T
    grown = jnp.exp(lam)
    last = lam[Q - 1 : Q, :]
    reach = jnp.exp(last - lam)
    fade = jnp.exp(last)
    b_rows = bc_ref[:, :N]
    c_rows = bc_ref[:, N:]
    c_t = turned(c_rows)
    scores_t = nt_dot(b_rows, c_rows)
    for pair in range(pairs):
        cols = slice(pair * LANES, (pair + 1) * LANES)
        first = 2 * pair
        conv = conv_at(halo, taps_ref, bias_ref, cols, 13)
        gate = sigmoid(conv)
        x = conv * gate
        dy = dy_ref[:, cols]
        dy_wide = dy.astype(F32)
        q_t = nt_dot(halves(low_half, x).astype(BF16), dy)
        mixing = []
        crossed = None
        for at, h in enumerate((first, first + 1)):
            step_col = steps[:, h : h + 1]
            decay = jnp.exp(jnp.where(later, lam_t[h : h + 1, :] - lam[:, h : h + 1], NEG))
            seen = decay * q_t[at * Q : (at + 1) * Q]
            stepped = seen * step_col
            crossed = stepped if crossed is None else crossed + stepped
            r_cols[:, h : h + 1] = jnp.sum(seen * scores_t, axis=1, keepdims=True)
            w_rows[h : h + 1, :] = jnp.sum(stepped * scores_t, axis=0, keepdims=True)
            mixing.append((decay * scores_t).astype(BF16))
        if pair == 0:
            across[...] = crossed
        else:
            across[...] += crossed
        dx = mm(jnp.concatenate(mixing, axis=1), halves(low_half, dy_wide).astype(BF16))
        d_state = ds[:, cols]
        d_state_low = d_state.astype(BF16)
        ds_low[:, cols] = d_state_low
        step_pair = pair_cols(low_half, steps, first)
        reach_pair = pair_cols(low_half, reach, first)
        carried = reach_pair * mm(b_rows, d_state_low)
        dx = step_pair * (dx + carried) + skip_ref[:, cols] * dy_wide
        state_terms[:, cols] = (x * carried).astype(BF16)
        fed_all[:, cols] = (x * (reach_pair * step_pair)).astype(BF16)
        held = hold_ref[0, :, cols]
        dyl = dy_wide * pair_cols(low_half, grown, first)
        dyl_low = dyl.astype(BF16)
        dyl_all[:, cols] = dyl_low
        inter_terms[:, cols] = (dyl * mm(c_rows, held)).astype(BF16)
        e_rows[0:1, cols] = jnp.sum(d_state * held.astype(F32), axis=0, keepdims=True)
        ds[:, cols] = d_state * pair_cols(low_half[0:1], fade, first) + mm(c_t, dyl_low)
        g = dx * (gate * (1.0 + conv * (1.0 - gate)))
        gbuf[0:Q, cols] = g
        for k in range(4):
            gconv_ref[k : k + 1, cols] += jnp.sum(g * halo[13 + k : 13 + k + Q, cols], axis=0, keepdims=True)
        gconv_ref[4:5, cols] += jnp.sum(g, axis=0, keepdims=True)
        gconv_ref[5:6, cols] += jnp.sum(dy_wide * x, axis=0, keepdims=True)
        d_pre = taps_ref[3:4, cols] * g
        for k in range(1, 4):
            d_pre = d_pre + taps_ref[3 - k : 4 - k, cols] * gbuf[k : k + Q, cols]
        dvp_ref[:, cols] = d_pre.astype(dvp_ref.dtype)
        gbuf[Q : Q + 8, cols] = g[0:8]
    if dvp_ref.shape[1] > pairs * LANES:
        dvp_ref[:, pairs * LANES :] = jnp.zeros_like(dvp_ref[:, pairs * LANES :])
    cross = across[...]
    d_b = mm(cross.astype(BF16), c_rows) + nt_dot(fed_all[...], ds_low[...])
    d_c = mm(turned(cross), b_rows) + nt_dot(dyl_all[...], hold_ref[0])
    dbc_ref[:, :N] = d_b.astype(dbc_ref.dtype)
    dbc_ref[:, N:] = d_c.astype(dbc_ref.dtype)
    pick = pick_ref[...]
    from_state = mm(state_terms[...], pick)
    from_carry = mm(inter_terms[...], pick)
    e_high = e_rows[...].astype(BF16)
    e_rest = (e_rows[...] - e_high.astype(F32)).astype(BF16)
    through = (mm(e_high, pick) + mm(e_rest, pick))[0:1]
    r_all = r_cols[...]
    d_lam = w_rows[...].T - steps * r_all + from_carry
    d_log = (
        mm_exact(later.astype(F32), d_lam)
        + mm_exact((rows > lanes).astype(F32), steps * from_state)
        + fade * through
    )
    dst_ref[...] = r_all + from_state + rate * d_log
    gdecay_ref[...] += jnp.sum(steps * d_log, axis=0, keepdims=True)


def chunk_of(i, seat, per):
    return (lax.div(i, per) ^ seat[0]) * per + lax.rem(i, per)


def run_forward(seat, pre, states_in, steps, taps, bias, rate, skip, shards):
    tokens = steps.shape[0]
    width = taps.shape[1]
    blocks = tokens // Q
    per = blocks // shards
    fixed = lambda i, seat: (0, 0)
    plain = lambda i, seat: (i, 0)
    moved = lambda i, seat: (chunk_of(i, seat, per), 0)
    return pl.pallas_call(
        functools.partial(scan_forward, pairs=width // LANES),
        out_shape=(
            jax.ShapeDtypeStruct((tokens, width), BF16),
            jax.ShapeDtypeStruct((blocks, N, width), BF16),
        ),
        grid_spec=pltpu.PrefetchScalarGridSpec(
            num_scalar_prefetch=1,
            grid=(blocks,),
            in_specs=[
                pl.BlockSpec((Q, width), moved),
                pl.BlockSpec((Q, 2 * N), plain),
                pl.BlockSpec((Q, LANES), plain),
                pl.BlockSpec((4, width), fixed),
                pl.BlockSpec((1, width), fixed),
                pl.BlockSpec((1, LANES), fixed),
                pl.BlockSpec((1, width), fixed),
            ],
            out_specs=[
                pl.BlockSpec((Q, width), moved),
                pl.BlockSpec((1, N, width), lambda i, seat: (i, 0, 0)),
            ],
            scratch_shapes=[pltpu.VMEM((N, width), F32), pltpu.VMEM((Q + 8, width), F32)],
        ),
        cost_estimate=pl.CostEstimate(
            flops=tokens * width * 1200, bytes_accessed=tokens * width * 10, transcendentals=tokens * width * 3
        ),
        name="scan_forward",
    )(seat, pre, states_in, steps, taps, bias, rate, skip)


def run_backward(seat, pre, dy, states_in, steps, held, taps, bias, rate, skip, pick, shards, out_width):
    tokens = steps.shape[0]
    width = taps.shape[1]
    blocks = tokens // Q
    per = blocks // shards
    fixed = lambda i, seat: (0, 0)
    plain = lambda i, seat: (blocks - 1 - i, 0)
    moved = lambda i, seat: (chunk_of(blocks - 1 - i, seat, per), 0)

    def before(i, seat):
        chunk = jnp.maximum(blocks - 2 - i, 0)
        return (chunk_of(chunk, seat, per) * (Q // 16) + Q // 16 - 1, 0)

    return pl.pallas_call(
        functools.partial(scan_backward, pairs=width // LANES, blocks=blocks),
        out_shape=(
            jax.ShapeDtypeStruct((tokens, out_width), BF16),
            jax.ShapeDtypeStruct((tokens, 2 * N), BF16),
            jax.ShapeDtypeStruct((tokens, LANES), F32),
            jax.ShapeDtypeStruct((8, width), F32),
            jax.ShapeDtypeStruct((1, LANES), F32),
        ),
        grid_spec=pltpu.PrefetchScalarGridSpec(
            num_scalar_prefetch=1,
            grid=(blocks,),
            in_specs=[
                pl.BlockSpec((Q, width), moved),
                pl.BlockSpec((16, width), before),
                pl.BlockSpec((Q, width), moved),
                pl.BlockSpec((Q, 2 * N), plain),
                pl.BlockSpec((Q, LANES), plain),
                pl.BlockSpec((1, N, width), lambda i, seat: (blocks - 1 - i, 0, 0)),
                pl.BlockSpec((4, width), fixed),
                pl.BlockSpec((1, width), fixed),
                pl.BlockSpec((1, LANES), fixed),
                pl.BlockSpec((1, width), fixed),
                pl.BlockSpec((width, LANES), fixed),
            ],
            out_specs=[
                pl.BlockSpec((Q, out_width), moved),
                pl.BlockSpec((Q, 2 * N), plain),
                pl.BlockSpec((Q, LANES), plain),
                pl.BlockSpec((8, width), fixed),
                pl.BlockSpec((1, LANES), fixed),
            ],
            scratch_shapes=[
                pltpu.VMEM((Q + 16, width), F32),
                pltpu.VMEM((Q + 8, width), F32),
                pltpu.VMEM((N, width), F32),
                pltpu.VMEM((N, width), BF16),
                pltpu.VMEM((Q, Q), F32),
                pltpu.VMEM((Q, LANES), F32),
                pltpu.VMEM((LANES, Q), F32),
                pltpu.VMEM((Q, width), BF16),
                pltpu.VMEM((Q, width), BF16),
                pltpu.VMEM((Q, width), BF16),
                pltpu.VMEM((Q, width), BF16),
                pltpu.VMEM((8, width), F32),
            ],
        ),
        cost_estimate=pl.CostEstimate(
            flops=tokens * width * 3000, bytes_accessed=tokens * width * 14, transcendentals=tokens * width * 4
        ),
        name="scan_backward",
    )(seat, pre, pre, dy, states_in, steps, held, taps, bias, rate, skip, pick)


EPSILON = 1e-05


def swish(v):
    return v * sigmoid(v)


def tn_dot(a, b):
    return lax.dot_general(a, b, (((0,), (0,)), ((), ())), preferred_element_type=F32)


def causal_conv(values, taps, offsets):
    tap_count = taps.shape[0]
    length = values.shape[0]
    padded = jnp.pad(values, ((tap_count - 1, 0), (0, 0)))
    summed = offsets[None, :] + taps[0][None, :] * padded[0:length]
    for offset in range(1, tap_count):
        summed = summed + taps[offset][None, :] * padded[offset : offset + length]
    return summed


def swap(v, bit, axis="col"):
    size = lax.axis_size(axis)
    return lax.ppermute(v, axis, [(i, i ^ bit) for i in range(size)])


def row_sum(v):
    bit = 1
    while bit < lax.axis_size("row"):
        v = v + swap(v, bit, "row")
        bit *= 2
    return v


class Square:
    shards = 4

    def __init__(self):
        self.place = lax.axis_index("col")
        self.x = lax.rem(self.place, 2) == 1
        self.y = lax.div(self.place, 2) == 1
        self.seat = jnp.reshape(self.place, (1,)).astype(jnp.int32)

    def settle(self, v):
        parts = v.reshape((2, 2, v.shape[0] // 4) + v.shape[1:])
        parts = jnp.where(self.y, parts[::-1], parts)
        parts = jnp.where(self.x, parts[:, ::-1], parts)
        return parts.reshape(v.shape)

    def gather(self, v):
        half = v.shape[0] // 2
        from_x = swap(v, 1)
        from_y = swap(v, 2)
        return [v, from_x, from_y, swap(from_x[:half], 2), swap(from_y[half:], 1)]

    def gather_flat(self, v):
        return self.settle(jnp.concatenate(self.gather(v)))

    def token_sum(self, v):
        parts = v.reshape(2, 2, -1)
        parts = parts + swap(parts, 1)[:, ::-1]
        parts = parts + swap(parts, 2)[::-1]
        return parts.reshape(v.shape)

    def total(self, v):
        v = v + swap(v, 1)
        return v + swap(v, 2)

    def scatter(self, piece_of):
        far = piece_of(3).astype(BF16)
        half = far.shape[0] // 2
        beside = piece_of(1)
        above = piece_of(2)
        across_x = swap(far[:half], 1).astype(F32)
        across_y = swap(far[half:], 2).astype(F32)
        x_top = swap(beside[:half].astype(BF16), 1)
        y_low = swap(above[half:].astype(BF16), 2)
        own = piece_of(0)
        x_low = swap((beside[half:] + across_y).astype(BF16), 1)
        y_top = swap((above[:half] + across_x).astype(BF16), 2)
        top = own[:half] + x_top.astype(F32) + y_top.astype(F32)
        low = own[half:] + x_low.astype(F32) + y_low.astype(F32)
        return jnp.concatenate([top, low])

    def gather_states(self, s):
        pair = jnp.concatenate([s, swap(s, 1)], axis=1)
        other = swap(pair, 2)
        return jnp.concatenate([jnp.where(self.y, other, pair), jnp.where(self.y, pair, other)], axis=1)

    def scatter_states(self, d):
        first, second = d[:, :N], d[:, N:]
        kept = jnp.where(self.y, second, first).astype(F32)
        kept = kept + swap(jnp.where(self.y, first, second), 2).astype(F32)
        half = N // 2
        return kept[:, :half] + swap(kept[:, half:].astype(BF16), 1).astype(F32)

    def own_slice(self, v):
        width = v.shape[0] // 4
        return lax.dynamic_slice(v, (self.place * width,), (width,))


class Line:
    shards = 1

    def __init__(self):
        self.seat = jnp.zeros((1,), jnp.int32)

    def settle(self, v):
        return v

    def gather(self, v):
        return [lax.all_gather(v, "col", axis=0, tiled=True)]

    def gather_flat(self, v):
        return lax.all_gather(v, "col", axis=0, tiled=True)

    def token_sum(self, v):
        return lax.psum(v, "col")

    def total(self, v):
        return lax.psum(v, "col")

    def scatter(self, piece_of):
        return lax.psum_scatter(
            piece_of(None).astype(BF16), "col", scatter_dimension=0, tiled=True
        ).astype(F32)

    def gather_states(self, s):
        return lax.all_gather(s, "col", axis=1, tiled=True)

    def scatter_states(self, d):
        return lax.psum_scatter(d.astype(BF16), "col", scatter_dimension=1, tiled=True).astype(F32)

    def own_slice(self, v):
        width = v.shape[0] // lax.axis_size("col")
        return lax.dynamic_slice(v, (lax.axis_index("col") * width,), (width,))


def widened(v, width):
    return v if v.shape[-1] == width else jnp.pad(v, [(0, 0)] * (v.ndim - 1) + [(0, width - v.shape[-1])])


def row_scatter(v):
    return lax.psum_scatter(v.astype(BF16), "row", scatter_dimension=0, tiled=True).astype(F32)


def body(
    hidden,
    in_gain,
    w_gate,
    w_value,
    w_bc,
    w_step,
    conv_value,
    conv_value_bias,
    conv_bc,
    conv_bc_bias,
    step_bias,
    decay_log,
    skip_gain,
    norm_gain,
    w_out,
    grad_out,
):
    lines = Square() if lax.axis_size("col") == 4 else Line()
    heads = step_bias.shape[0]
    channels = w_value.shape[1]
    inner_width = lax.axis_size("col") * channels
    bc_width = w_bc.shape[1]
    wide = -(-channels // LANES) * LANES
    full_width = wide + LANES
    step_at = wide + bc_width
    piece_rows = hidden.shape[0]

    def rows_of(v, piece):
        return v if piece is None else v[piece * piece_rows : (piece + 1) * piece_rows]

    w_cat = lax.all_gather(
        widened(jnp.concatenate([widened(w_value, wide), w_bc, w_step], axis=1), full_width),
        "row", axis=0, tiled=True,
    )
    w_gate_full = lax.all_gather(w_gate, "row", axis=0, tiled=True)
    w_out_t = lax.all_gather(w_out.T, "row", axis=0, tiled=True)
    full_gain = lines.gather_flat(in_gain).astype(F32)

    def normalized(rows):
        rows = rows.astype(F32)
        scale = lax.rsqrt(jnp.mean(rows * rows, axis=1, keepdims=True) + EPSILON)
        return (rows * scale * full_gain).astype(BF16)

    normal_in = jnp.concatenate([normalized(piece) for piece in lines.gather(hidden)])
    grad_full = jnp.concatenate(lines.gather(grad_out))

    pre = mm(normal_in, w_cat)
    bc_pre = lines.settle(pre[:, wide : wide + bc_width])
    step_sum = lines.settle(pre[:, step_at : step_at + heads]) + step_bias

    def state_branch(pre_vals, conv_weight, conv_offset):
        return swish(causal_conv(pre_vals, conv_weight, conv_offset))

    state_local, state_back = jax.vjp(state_branch, bc_pre, conv_bc, conv_bc_bias)
    states = lines.gather_states(state_local.astype(BF16))
    steps = widened(jax.nn.softplus(step_sum), LANES)
    rate = widened(-jnp.exp(decay_log), LANES)[None]
    skip = widened(jnp.repeat(skip_gain, P_SIZE), wide)[None]
    taps = widened(conv_value, wide)
    offsets = widened(conv_value_bias, wide)[None]
    pick = (jnp.arange(wide)[:, None] // P_SIZE == jnp.arange(LANES)[None]).astype(BF16)
    heads_out, held = run_forward(lines.seat, pre, states, steps, taps, offsets, rate, skip, lines.shards)

    gate_pre = mm(normal_in, w_gate_full).astype(BF16)
    ho = heads_out[:, :channels].astype(F32)
    gate = gate_pre.astype(F32)
    gated = ho * swish(gate)
    squares = lines.token_sum(jnp.sum(gated * gated, axis=1))
    mix = lax.rsqrt(squares / inner_width + EPSILON)[:, None]
    normed = (gated * mix * norm_gain).astype(BF16)

    branch_out = lines.scatter(lambda piece: nt_dot(rows_of(normed, piece), w_out_t))
    result = (hidden.astype(F32) + branch_out).astype(BF16)

    d_normed = mm(grad_full, w_out_t).astype(BF16).astype(F32)
    scaled = d_normed * norm_gain
    dots = lines.token_sum(jnp.sum(gated * scaled, axis=1))[:, None]
    g_out_t = row_scatter(tn_dot(grad_full, normed))
    d_gated = mix * scaled - gated * (mix * mix * mix * dots / inner_width)
    g_norm_gain = jnp.sum(d_normed * gated * mix, axis=0)
    open_gate = sigmoid(gate)
    d_heads = (d_gated * gate * open_gate).astype(BF16)
    d_gate = (d_gated * ho * (open_gate * (1.0 + gate * (1.0 - open_gate)))).astype(BF16)
    g_gate_part = tn_dot(normal_in, d_gate).astype(BF16)
    g_gate = row_scatter(g_gate_part)

    d_cat, d_states, d_steps, g_conv, g_decay = run_backward(
        lines.seat, pre, widened(d_heads, wide), states, steps, held, taps, offsets, rate, skip, pick,
        lines.shards, full_width,
    )
    d_bc_pre, g_conv_bc, g_conv_bc_bias = state_back(lines.scatter_states(d_states))
    d_step = d_steps[:, :heads] * sigmoid(step_sum)
    small = lines.settle(widened(jnp.concatenate([d_bc_pre, d_step], axis=1), LANES)).astype(BF16)
    d_cat = lax.dynamic_update_slice(d_cat, small, (0, wide))
    g_cat_part = tn_dot(normal_in, d_cat).astype(BF16)
    g_cat = row_scatter(g_cat_part)

    d_rows = lines.scatter(
        lambda piece: nt_dot(rows_of(d_gate, piece), w_gate_full) + nt_dot(rows_of(d_cat, piece), w_cat)
    )
    tokens = hidden.astype(F32)
    scale = lax.rsqrt(jnp.mean(tokens * tokens, axis=1, keepdims=True) + EPSILON)
    scaled_rows = d_rows * full_gain
    grad_hidden = grad_out.astype(F32) + scale * (
        scaled_rows - tokens * (scale * scale * jnp.mean(tokens * scaled_rows, axis=1, keepdims=True))
    )

    g_in_gain = (
        jnp.sum(w_gate_full.astype(F32) * g_gate_part.astype(F32), axis=1)
        + jnp.sum(w_cat.astype(F32) * g_cat_part.astype(F32), axis=1)
    ) / full_gain
    g_in_gain = row_sum(lines.own_slice(lines.total(g_in_gain)))
    parts = (
        g_conv[:4, :channels],
        g_conv[4, :channels],
        g_conv_bc,
        g_conv_bc_bias,
        jnp.sum(d_step, axis=0),
        (g_decay * rate)[0, :heads],
        jnp.sum(g_conv[5, :channels].reshape(heads, P_SIZE), axis=1),
        g_norm_gain,
    )
    packed = row_sum(jnp.concatenate([part.reshape(-1) for part in parts]))
    summed = []
    at = 0
    for part in parts:
        summed.append(packed[at : at + part.size].reshape(part.shape))
        at += part.size
    return (
        result,
        grad_hidden,
        g_in_gain,
        g_gate,
        g_cat[:, :channels],
        g_cat[:, wide : wide + bc_width],
        g_cat[:, step_at : step_at + heads],
        *summed,
        g_out_t.T,
    )


def solution(mesh):
    over_tokens = P(("row", "col"), None)
    square = P("row", "col")
    across = P(None, "col")
    vector = P("col")
    return jax.shard_map(
        body,
        mesh=mesh,
        in_specs=(
            over_tokens, vector, square, square, square, square, across, vector, across, vector,
            vector, vector, vector, vector, P("col", "row"), over_tokens,
        ),
        out_specs=(
            over_tokens, over_tokens, vector, square, square, square, square, across, vector, across,
            vector, vector, vector, vector, vector, P("col", "row"),
        ),
        check_vma=False,
    )
```

```python
import functools
import jax
import jax.numpy as jnp
from jax import lax
from jax.experimental import pallas as pl
from jax.experimental.pallas import tpu as pltpu
from jax.experimental.layout import Layout, with_layout_constraint
from jax.sharding import PartitionSpec as P


P_SIZE = 64
N = 128
Q = 128
LANES = 128
NEG = -1e30
HIGH = lax.Precision.HIGHEST
F32 = jnp.float32
BF16 = jnp.bfloat16


def sigmoid(v):
    return 0.5 * jnp.tanh(0.5 * v) + 0.5


def nt_dot(a, b):
    return lax.dot_general(a, b, (((1,), (1,)), ((), ())), preferred_element_type=F32)


def mm(a, b):
    return jnp.dot(a, b, preferred_element_type=F32)


def mm_exact(a, b):
    return jnp.dot(a, b, precision=HIGH, preferred_element_type=F32)


def turned(m):
    return m.astype(F32).T.astype(BF16)


def pair_cols(low_half, cols, first):
    return jnp.where(low_half, cols[:, first : first + 1], cols[:, first + 1 : first + 2])


def halves(low_half, v):
    zero = jnp.zeros_like(v)
    return jnp.concatenate([jnp.where(low_half, v, zero), jnp.where(low_half, zero, v)], axis=0)


def conv_at(halo, taps_ref, bias_ref, cols, start):
    total = bias_ref[:, cols] + taps_ref[0:1, cols] * halo[start : start + Q, cols]
    for k in range(1, 4):
        total = total + taps_ref[k : k + 1, cols] * halo[start + k : start + k + Q, cols]
    return total


def scan_forward(
    seat_ref, vp_ref, bc_ref, st_ref, taps_ref, bias_ref, rate_ref, skip_ref,
    y_ref, hold_ref, state, halo, *, pairs
):
    @pl.when(pl.program_id(0) == 0)
    def _():
        state[...] = jnp.zeros_like(state)
        halo[0:8, :] = jnp.zeros_like(halo[0:8, :])

    halo[8 : 8 + Q, :] = vp_ref[...].astype(F32)
    rows = lax.broadcasted_iota(jnp.int32, (Q, Q), 0)
    lanes = lax.broadcasted_iota(jnp.int32, (Q, Q), 1)
    causal = rows >= lanes
    low_half = lanes < P_SIZE
    steps = st_ref[...]
    lam = mm_exact(causal.astype(F32), steps * rate_ref[...])
    source_t = (lam - jnp.log(steps)).T
    grown = jnp.exp(lam)
    last = lam[Q - 1 : Q, :]
    weight = jnp.exp(last - lam) * steps
    fade = jnp.exp(last)
    b_rows = bc_ref[:, :N]
    c_rows = bc_ref[:, N:]
    b_t = turned(b_rows)
    scores = nt_dot(c_rows, b_rows)
    for pair in range(pairs):
        cols = slice(pair * LANES, (pair + 1) * LANES)
        first = 2 * pair
        conv = conv_at(halo, taps_ref, bias_ref, cols, 5)
        x = conv * sigmoid(conv)
        mixing = []
        for h in (first, first + 1):
            gap = jnp.where(causal, lam[:, h : h + 1] - source_t[h : h + 1, :], NEG)
            mixing.append((scores * jnp.exp(gap)).astype(BF16))
        y = mm(jnp.concatenate(mixing, axis=1), halves(low_half, x).astype(BF16))
        held = state[:, cols]
        held_low = held.astype(BF16)
        y = y + mm(c_rows, held_low) * pair_cols(low_half, grown, first)
        y = y + skip_ref[:, cols] * x
        y_ref[:, cols] = y.astype(y_ref.dtype)
        hold_ref[0, :, cols] = held_low
        fed = (x * pair_cols(low_half, weight, first)).astype(BF16)
        state[:, cols] = held * pair_cols(low_half[0:1], fade, first) + mm(b_t, fed)
    halo[0:8, :] = halo[Q : Q + 8, :]


def scan_backward(
    seat_ref, vp_ref, before_ref, dy_ref, bc_ref, st_ref, hold_ref, taps_ref, bias_ref, rate_ref, skip_ref, pick_ref,
    dvp_ref, dbc_ref, dst_ref, gconv_ref, gdecay_ref,
    halo, gbuf, ds, ds_low, across, r_cols, w_rows, state_terms, inter_terms, fed_all, dyl_all, e_rows, *, pairs, blocks
):
    step_id = pl.program_id(0)

    @pl.when(step_id == 0)
    def _():
        ds[...] = jnp.zeros_like(ds)
        gbuf[Q : Q + 8, :] = jnp.zeros_like(gbuf[Q : Q + 8, :])
        gconv_ref[...] = jnp.zeros_like(gconv_ref)
        gdecay_ref[...] = jnp.zeros_like(gdecay_ref)
        r_cols[...] = jnp.zeros_like(r_cols)
        w_rows[...] = jnp.zeros_like(w_rows)
        e_rows[...] = jnp.zeros_like(e_rows)

    halo[16 : 16 + Q, :] = vp_ref[...].astype(F32)

    @pl.when(step_id < blocks - 1)
    def _():
        halo[0:16, :] = before_ref[...].astype(F32)

    @pl.when(step_id == blocks - 1)
    def _():
        halo[0:16, :] = jnp.zeros_like(halo[0:16, :])

    rows = lax.broadcasted_iota(jnp.int32, (Q, Q), 0)
    lanes = lax.broadcasted_iota(jnp.int32, (Q, Q), 1)
    causal = rows >= lanes
    later = lanes >= rows
    low_half = lanes < P_SIZE
    steps = st_ref[...]
    rate = rate_ref[...]
    lam = mm_exact(causal.astype(F32), steps * rate)
    lam_t = lam.T
    grown = jnp.exp(lam)
    last = lam[Q - 1 : Q, :]
    reach = jnp.exp(last - lam)
    fade = jnp.exp(last)
    b_rows = bc_ref[:, :N]
    c_rows = bc_ref[:, N:]
    c_t = turned(c_rows)
    scores_t = nt_dot(b_rows, c_rows)
    for pair in range(pairs):
        cols = slice(pair * LANES, (pair + 1) * LANES)
        first = 2 * pair
        conv = conv_at(halo, taps_ref, bias_ref, cols, 13)
        gate = sigmoid(conv)
        x = conv * gate
        dy = dy_ref[:, cols]
        dy_wide = dy.astype(F32)
        q_t = nt_dot(halves(low_half, x).astype(BF16), dy)
        mixing = []
        crossed = None
        for at, h in enumerate((first, first + 1)):
            step_col = steps[:, h : h + 1]
            decay = jnp.exp(jnp.where(later, lam_t[h : h + 1, :] - lam[:, h : h + 1], NEG))
            seen = decay * q_t[at * Q : (at + 1) * Q]
            stepped = seen * step_col
            crossed = stepped if crossed is None else crossed + stepped
            r_cols[:, h : h + 1] = jnp.sum(seen * scores_t, axis=1, keepdims=True)
            w_rows[h : h + 1, :] = jnp.sum(stepped * scores_t, axis=0, keepdims=True)
            mixing.append((decay * scores_t).astype(BF16))
        if pair == 0:
            across[...] = crossed
        else:
            across[...] += crossed
        dx = mm(jnp.concatenate(mixing, axis=1), halves(low_half, dy_wide).astype(BF16))
        d_state = ds[:, cols]
        d_state_low = d_state.astype(BF16)
        ds_low[:, cols] = d_state_low
        step_pair = pair_cols(low_half, steps, first)
        reach_pair = pair_cols(low_half, reach, first)
        carried = reach_pair * mm(b_rows, d_state_low)
        dx = step_pair * (dx + carried) + skip_ref[:, cols] * dy_wide
        state_terms[:, cols] = (x * carried).astype(BF16)
        fed_all[:, cols] = (x * (reach_pair * step_pair)).astype(BF16)
        held = hold_ref[0, :, cols]
        dyl = dy_wide * pair_cols(low_half, grown, first)
        dyl_low = dyl.astype(BF16)
        dyl_all[:, cols] = dyl_low
        inter_terms[:, cols] = (dyl * mm(c_rows, held)).astype(BF16)
        e_rows[0:1, cols] = jnp.sum(d_state * held.astype(F32), axis=0, keepdims=True)
        ds[:, cols] = d_state * pair_cols(low_half[0:1], fade, first) + mm(c_t, dyl_low)
        g = dx * (gate * (1.0 + conv * (1.0 - gate)))
        gbuf[0:Q, cols] = g
        for k in range(4):
            gconv_ref[k : k + 1, cols] += jnp.sum(g * halo[13 + k : 13 + k + Q, cols], axis=0, keepdims=True)
        gconv_ref[4:5, cols] += jnp.sum(g, axis=0, keepdims=True)
        gconv_ref[5:6, cols] += jnp.sum(dy_wide * x, axis=0, keepdims=True)
        d_pre = taps_ref[3:4, cols] * g
        for k in range(1, 4):
            d_pre = d_pre + taps_ref[3 - k : 4 - k, cols] * gbuf[k : k + Q, cols]
        dvp_ref[:, cols] = d_pre.astype(dvp_ref.dtype)
        gbuf[Q : Q + 8, cols] = g[0:8]
    if dvp_ref.shape[1] > pairs * LANES:
        dvp_ref[:, pairs * LANES :] = jnp.zeros_like(dvp_ref[:, pairs * LANES :])
    cross = across[...]
    d_b = mm(cross.astype(BF16), c_rows) + nt_dot(fed_all[...], ds_low[...])
    d_c = mm(turned(cross), b_rows) + nt_dot(dyl_all[...], hold_ref[0])
    dbc_ref[:, :N] = d_b.astype(dbc_ref.dtype)
    dbc_ref[:, N:] = d_c.astype(dbc_ref.dtype)
    pick = pick_ref[...]
    from_state = mm(state_terms[...], pick)
    from_carry = mm(inter_terms[...], pick)
    e_high = e_rows[...].astype(BF16)
    e_rest = (e_rows[...] - e_high.astype(F32)).astype(BF16)
    through = (mm(e_high, pick) + mm(e_rest, pick))[0:1]
    r_all = r_cols[...]
    d_lam = w_rows[...].T - steps * r_all + from_carry
    d_log = (
        mm_exact(later.astype(F32), d_lam)
        + mm_exact((rows > lanes).astype(F32), steps * from_state)
        + fade * through
    )
    dst_ref[...] = r_all + from_state + rate * d_log
    gdecay_ref[...] += jnp.sum(steps * d_log, axis=0, keepdims=True)


def chunk_of(i, seat, per):
    return (lax.div(i, per) ^ seat[0]) * per + lax.rem(i, per)


def run_forward(seat, pre, states_in, steps, taps, bias, rate, skip, shards):
    tokens = steps.shape[0]
    width = taps.shape[1]
    blocks = tokens // Q
    per = blocks // shards
    fixed = lambda i, seat: (0, 0)
    plain = lambda i, seat: (i, 0)
    moved = lambda i, seat: (chunk_of(i, seat, per), 0)
    return pl.pallas_call(
        functools.partial(scan_forward, pairs=width // LANES),
        out_shape=(
            jax.ShapeDtypeStruct((tokens, width), BF16),
            jax.ShapeDtypeStruct((blocks, N, width), BF16),
        ),
        grid_spec=pltpu.PrefetchScalarGridSpec(
            num_scalar_prefetch=1,
            grid=(blocks,),
            in_specs=[
                pl.BlockSpec((Q, width), moved),
                pl.BlockSpec((Q, 2 * N), plain),
                pl.BlockSpec((Q, LANES), plain),
                pl.BlockSpec((4, width), fixed),
                pl.BlockSpec((1, width), fixed),
                pl.BlockSpec((1, LANES), fixed),
                pl.BlockSpec((1, width), fixed),
            ],
            out_specs=[
                pl.BlockSpec((Q, width), moved),
                pl.BlockSpec((1, N, width), lambda i, seat: (i, 0, 0)),
            ],
            scratch_shapes=[pltpu.VMEM((N, width), F32), pltpu.VMEM((Q + 8, width), F32)],
        ),
        cost_estimate=pl.CostEstimate(
            flops=tokens * width * 1200, bytes_accessed=tokens * width * 10, transcendentals=tokens * width * 3
        ),
        name="scan_forward",
    )(seat, pre, states_in, steps, taps, bias, rate, skip)


def run_backward(seat, pre, dy, states_in, steps, held, taps, bias, rate, skip, pick, shards, out_width):
    tokens = steps.shape[0]
    width = taps.shape[1]
    blocks = tokens // Q
    per = blocks // shards
    fixed = lambda i, seat: (0, 0)
    plain = lambda i, seat: (blocks - 1 - i, 0)
    moved = lambda i, seat: (chunk_of(blocks - 1 - i, seat, per), 0)

    def before(i, seat):
        chunk = jnp.maximum(blocks - 2 - i, 0)
        return (chunk_of(chunk, seat, per) * (Q // 16) + Q // 16 - 1, 0)

    return pl.pallas_call(
        functools.partial(scan_backward, pairs=width // LANES, blocks=blocks),
        out_shape=(
            jax.ShapeDtypeStruct((tokens, out_width), BF16),
            jax.ShapeDtypeStruct((tokens, 2 * N), BF16),
            jax.ShapeDtypeStruct((tokens, LANES), F32),
            jax.ShapeDtypeStruct((8, width), F32),
            jax.ShapeDtypeStruct((1, LANES), F32),
        ),
        grid_spec=pltpu.PrefetchScalarGridSpec(
            num_scalar_prefetch=1,
            grid=(blocks,),
            in_specs=[
                pl.BlockSpec((Q, width), moved),
                pl.BlockSpec((16, width), before),
                pl.BlockSpec((Q, width), moved),
                pl.BlockSpec((Q, 2 * N), plain),
                pl.BlockSpec((Q, LANES), plain),
                pl.BlockSpec((1, N, width), lambda i, seat: (blocks - 1 - i, 0, 0)),
                pl.BlockSpec((4, width), fixed),
                pl.BlockSpec((1, width), fixed),
                pl.BlockSpec((1, LANES), fixed),
                pl.BlockSpec((1, width), fixed),
                pl.BlockSpec((width, LANES), fixed),
            ],
            out_specs=[
                pl.BlockSpec((Q, out_width), moved),
                pl.BlockSpec((Q, 2 * N), plain),
                pl.BlockSpec((Q, LANES), plain),
                pl.BlockSpec((8, width), fixed),
                pl.BlockSpec((1, LANES), fixed),
            ],
            scratch_shapes=[
                pltpu.VMEM((Q + 16, width), F32),
                pltpu.VMEM((Q + 8, width), F32),
                pltpu.VMEM((N, width), F32),
                pltpu.VMEM((N, width), BF16),
                pltpu.VMEM((Q, Q), F32),
                pltpu.VMEM((Q, LANES), F32),
                pltpu.VMEM((LANES, Q), F32),
                pltpu.VMEM((Q, width), BF16),
                pltpu.VMEM((Q, width), BF16),
                pltpu.VMEM((Q, width), BF16),
                pltpu.VMEM((Q, width), BF16),
                pltpu.VMEM((8, width), F32),
            ],
        ),
        cost_estimate=pl.CostEstimate(
            flops=tokens * width * 3000, bytes_accessed=tokens * width * 14, transcendentals=tokens * width * 4
        ),
        name="scan_backward",
    )(seat, pre, pre, dy, states_in, steps, held, taps, bias, rate, skip, pick)


EPSILON = 1e-05


def swish(v):
    return v * sigmoid(v)


def tn_dot(a, b):
    return lax.dot_general(a, b, (((0,), (0,)), ((), ())), preferred_element_type=F32)


def fill_kernel(x_ref, w_ref, *refs):
    refs[-1][...] = mm(x_ref[...], w_ref[...])


def run_fill(x, w, into, rows, first, block):
    depth, width = w.shape
    return pl.pallas_call(
        fill_kernel,
        out_shape=jax.ShapeDtypeStruct((rows, width), F32),
        grid=(x.shape[0] // block,),
        in_specs=[
            pl.BlockSpec((block, depth), lambda i: (i, 0)),
            pl.BlockSpec((depth, width), lambda i: (0, 0), pipeline_mode=pl.Buffered(1)),
        ]
        + [pl.BlockSpec(memory_space=pl.ANY)] * len(into),
        out_specs=pl.BlockSpec((block, width), lambda i: (i + first, 0)),
        input_output_aliases={2: 0} if into else {},
        cost_estimate=pl.CostEstimate(
            flops=2 * x.shape[0] * depth * width,
            bytes_accessed=2 * (x.shape[0] + width) * depth + 4 * x.shape[0] * width,
            transcendentals=0,
        ),
        name="value_product",
    )(x, w, *into)


def split_kernel(x_ref, w_ref, *out_refs):
    rows = out_refs[0].shape[0]
    for at, out_ref in enumerate(out_refs):
        out_ref[...] = nt_dot(x_ref[at * rows : (at + 1) * rows], w_ref[...]).astype(BF16)


def run_split(x, w, parts, block):
    tokens, depth = x.shape
    width = w.shape[0]
    rows = tokens // parts
    return pl.pallas_call(
        split_kernel,
        out_shape=[jax.ShapeDtypeStruct((rows, width), BF16)] * parts,
        grid=(width // block,),
        in_specs=[
            pl.BlockSpec((tokens, depth), lambda i: (0, 0), pipeline_mode=pl.Buffered(1)),
            pl.BlockSpec((block, depth), lambda i: (i, 0)),
        ],
        out_specs=[pl.BlockSpec((rows, block), lambda i: (0, i))] * parts,
        cost_estimate=pl.CostEstimate(
            flops=2 * tokens * depth * width, bytes_accessed=2 * (tokens + width) * depth + 2 * tokens * width, transcendentals=0
        ),
        name="split_product",
    )(x, w)


def rows_kernel(gate_ref, value_ref, small_ref, w_gate_ref, w_cat_ref, top_ref, low_ref):
    wide = value_ref.shape[1]
    rows = top_ref.shape[0]
    for at, out_ref in enumerate((top_ref, low_ref)):
        here = slice(at * rows, (at + 1) * rows)
        total = nt_dot(gate_ref[here], w_gate_ref[...])
        total = total + nt_dot(value_ref[here], w_cat_ref[:, :wide])
        total = total + nt_dot(small_ref[here], w_cat_ref[:, wide:])
        out_ref[...] = total.astype(BF16)


def run_rows(piece, d_gate, d_value, d_small, w_gate, w_cat, rows, block):
    width = w_gate.shape[0]
    depth = w_gate.shape[1] + w_cat.shape[1]
    mine = lambda i: (piece, 0)
    once = pl.Buffered(1)
    return pl.pallas_call(
        rows_kernel,
        out_shape=[jax.ShapeDtypeStruct((rows // 2, width), BF16)] * 2,
        grid=(width // block,),
        in_specs=[
            pl.BlockSpec((rows, d_gate.shape[1]), mine, pipeline_mode=once),
            pl.BlockSpec((rows, d_value.shape[1]), mine, pipeline_mode=once),
            pl.BlockSpec((rows, d_small.shape[1]), mine, pipeline_mode=once),
            pl.BlockSpec((block, w_gate.shape[1]), lambda i: (i, 0)),
            pl.BlockSpec((block, w_cat.shape[1]), lambda i: (i, 0)),
        ],
        out_specs=[pl.BlockSpec((rows // 2, block), lambda i: (0, i))] * 2,
        cost_estimate=pl.CostEstimate(
            flops=2 * rows * depth * width, bytes_accessed=2 * (rows + width) * depth + 2 * rows * width, transcendentals=0
        ),
        name="rows_product",
    )(d_gate, d_value, d_small, w_gate, w_cat)


def causal_conv(values, taps, offsets):
    tap_count = taps.shape[0]
    length = values.shape[0]
    padded = jnp.pad(values, ((tap_count - 1, 0), (0, 0)))
    summed = offsets[None, :] + taps[0][None, :] * padded[0:length]
    for offset in range(1, tap_count):
        summed = summed + taps[offset][None, :] * padded[offset : offset + length]
    return summed


def swap(v, bit, axis="col"):
    size = lax.axis_size(axis)
    return lax.ppermute(v, axis, [(i, i ^ bit) for i in range(size)])


def row_sum(v):
    bit = 1
    while bit < lax.axis_size("row"):
        v = v + swap(v, bit, "row")
        bit *= 2
    return v


class Square:
    shards = 4

    def __init__(self):
        self.place = lax.axis_index("col")
        self.x = lax.rem(self.place, 2) == 1
        self.y = lax.div(self.place, 2) == 1
        self.seat = jnp.reshape(self.place, (1,)).astype(jnp.int32)

    def settle(self, v):
        parts = v.reshape((2, 2, v.shape[0] // 4) + v.shape[1:])
        parts = jnp.where(self.y, parts[::-1], parts)
        parts = jnp.where(self.x, parts[:, ::-1], parts)
        return parts.reshape(v.shape)

    def gather_begin(self, v):
        return [v, swap(v, 1), swap(v, 2)]

    def gather_end(self, pieces):
        half = pieces[0].shape[0] // 2
        return pieces + [swap(pieces[1][:half], 2), swap(pieces[2][half:], 1)]

    def gather_flat(self, v):
        return self.settle(jnp.concatenate([v, swap(v, 1), swap(v, 2), swap(v, 3)]))

    def token_sum(self, v):
        parts = v.reshape(2, 2, -1)
        parts = parts + swap(parts, 1)[:, ::-1]
        parts = parts + swap(parts, 2)[::-1]
        return parts.reshape(v.shape)

    def total(self, v):
        v = v + swap(v, 1)
        return v + swap(v, 2)

    def scatter_begin(self, halves_of):
        top, low, x_top, x_low, y_top, y_low, far_top, far_low = halves_of
        came = []
        for part, bit in ((far_top, 1), (far_low, 2), (x_top, 1), (y_low, 2)):
            came.append(swap(part, bit))
        return [x_low, y_top, top, low], came

    def scatter_relay(self, kept, came):
        beside, above, top, low = kept
        across_x, across_y, x_top, y_low = came
        x_low = (beside.astype(F32) + across_y.astype(F32)).astype(BF16)
        y_top = (above.astype(F32) + across_x.astype(F32)).astype(BF16)
        return [x_low, y_top], [top, low, x_top, y_low]

    def scatter_end(self, sent, came):
        x_low = swap(sent[0], 1)
        y_top = swap(sent[1], 2)
        top, low, x_top, y_low = (v.astype(F32) for v in came)
        return jnp.concatenate([top + x_top + y_top.astype(F32), low + x_low.astype(F32) + y_low])

    def gather_states(self, s):
        pair = jnp.concatenate([s, swap(s, 1)], axis=1)
        other = jnp.concatenate([swap(s, 2), swap(s, 3)], axis=1)
        return jnp.concatenate([jnp.where(self.y, other, pair), jnp.where(self.y, pair, other)], axis=1)

    def split_states(self, d):
        first, second = d[:, :N], d[:, N:]
        kept = jnp.where(self.y, second, first)
        given = jnp.where(self.y, first, second)
        half = N // 2
        return [kept[:, :half], kept[:, half:], given[:, :half], given[:, half:]]

    def scatter_states(self, parts):
        own = parts[0].astype(F32)
        for bit in (1, 2, 3):
            came = swap(parts[bit], bit)
            own = own + came.astype(F32)
        return own

    def own_slice(self, v):
        width = v.shape[0] // 4
        return lax.dynamic_slice(v, (self.place * width,), (width,))


class Line:
    shards = 1

    def __init__(self):
        self.seat = jnp.zeros((1,), jnp.int32)

    def settle(self, v):
        return v

    def gather_begin(self, v):
        return [lax.all_gather(v, "col", axis=0, tiled=True)]

    def gather_end(self, pieces):
        return pieces

    def gather_flat(self, v):
        return lax.all_gather(v, "col", axis=0, tiled=True)

    def token_sum(self, v):
        return lax.psum(v, "col")

    def total(self, v):
        return lax.psum(v, "col")

    def scatter_begin(self, halves_of):
        return [], list(halves_of)

    def scatter_relay(self, kept, came):
        return came, []

    def scatter_end(self, sent, came):
        return lax.psum_scatter(sent[0], "col", scatter_dimension=0, tiled=True).astype(F32)

    def gather_states(self, s):
        return lax.all_gather(s, "col", axis=1, tiled=True)

    def split_states(self, d):
        return [d]

    def scatter_states(self, parts):
        return lax.psum_scatter(parts[0].astype(BF16), "col", scatter_dimension=1, tiled=True).astype(F32)

    def own_slice(self, v):
        width = v.shape[0] // lax.axis_size("col")
        return lax.dynamic_slice(v, (lax.axis_index("col") * width,), (width,))


def widened(v, width):
    return v if v.shape[-1] == width else jnp.pad(v, [(0, 0)] * (v.ndim - 1) + [(0, width - v.shape[-1])])


def tied(*values):
    return lax.optimization_barrier(values)


def row_major(v):
    return with_layout_constraint(v, Layout(major_to_minor=(0, 1)))


def row_scatter_small(v):
    bit = lax.axis_size("row") // 2
    place = lax.axis_index("row")
    while bit:
        half = v.shape[0] // 2
        upper = lax.rem(lax.div(place, bit), 2) == 1
        kept = jnp.where(upper, v[half:], v[:half])
        given = jnp.where(upper, v[:half], v[half:])
        v = kept + swap(given.astype(BF16), bit, "row").astype(F32)
        bit //= 2
    return v


def row_scatter(v):
    return lax.psum_scatter(v.astype(BF16), "row", scatter_dimension=0, tiled=True).astype(F32)


def body(
    hidden,
    in_gain,
    w_gate,
    w_value,
    w_bc,
    w_step,
    conv_value,
    conv_value_bias,
    conv_bc,
    conv_bc_bias,
    step_bias,
    decay_log,
    skip_gain,
    norm_gain,
    w_out,
    grad_out,
):
    lines = Square() if lax.axis_size("col") == 4 else Line()
    heads = step_bias.shape[0]
    channels = w_value.shape[1]
    inner_width = lax.axis_size("col") * channels
    bc_width = w_bc.shape[1]
    wide = -(-channels // LANES) * LANES
    full_width = wide + LANES
    step_at = wide + bc_width
    piece_rows = hidden.shape[0]

    w_cat = lax.all_gather(
        widened(jnp.concatenate([widened(w_value, wide), w_bc, w_step], axis=1), full_width),
        "row", axis=0, tiled=True,
    )
    w_gate_full = lax.all_gather(w_gate, "row", axis=0, tiled=True)
    w_out_t = lax.all_gather(w_out.T, "row", axis=0, tiled=True)
    full_gain = lines.gather_flat(in_gain).astype(F32)

    def normalized(rows):
        rows = rows.astype(F32)
        scale = lax.rsqrt(jnp.mean(rows * rows, axis=1, keepdims=True) + EPSILON)
        return (rows * scale * full_gain).astype(BF16)

    hidden_pieces = lines.gather_end(lines.gather_begin(hidden))
    near = jnp.concatenate([normalized(piece) for piece in hidden_pieces[:3]])
    far = [normalized(piece) for piece in hidden_pieces[3:]]
    grad_source, _ = tied(grad_out, hidden_pieces[-1])
    grad_pieces = lines.gather_begin(grad_source)

    if far:
        far = jnp.concatenate(far)
        tokens_here = near.shape[0] + far.shape[0]
        pre = run_fill(near, w_cat, (), tokens_here, 0, 256)
        pre = run_fill(far, w_cat, (pre,), tokens_here, near.shape[0] // 256, 256)
        normal_in = jnp.concatenate([near, far])
    else:
        normal_in = near
        pre = mm(normal_in, w_cat)
    bc_pre = lines.settle(pre[:, wide : wide + bc_width])
    step_sum = lines.settle(pre[:, step_at : step_at + heads]) + step_bias

    def state_branch(pre_vals, conv_weight, conv_offset):
        return swish(causal_conv(pre_vals, conv_weight, conv_offset))

    state_local, state_back = jax.vjp(state_branch, bc_pre, conv_bc, conv_bc_bias)
    states = lines.gather_states(state_local.astype(BF16))
    steps = widened(jax.nn.softplus(step_sum), LANES)
    rate = widened(-jnp.exp(decay_log), LANES)[None]
    skip = widened(jnp.repeat(skip_gain, P_SIZE), wide)[None]
    taps = widened(conv_value, wide)
    offsets = widened(conv_value_bias, wide)[None]
    pick = (jnp.arange(wide)[:, None] // P_SIZE == jnp.arange(LANES)[None]).astype(BF16)
    heads_out, held = run_forward(lines.seat, pre, states, steps, taps, offsets, rate, skip, lines.shards)

    heads_out, *grad_pieces = tied(heads_out, *grad_pieces)
    grad_pieces = lines.gather_end(grad_pieces)
    gate_pre = mm(normal_in, w_gate_full).astype(BF16)
    ho = heads_out[:, :channels].astype(F32)
    gate = gate_pre.astype(F32)
    gated = ho * swish(gate)
    squares = lines.token_sum(jnp.sum(gated * gated, axis=1))
    mix = lax.rsqrt(squares / inner_width + EPSILON)[:, None]
    normed = (gated * mix * norm_gain).astype(BF16)
    normed, *grad_pieces = tied(normed, *grad_pieces)
    grad_full = jnp.concatenate(grad_pieces)

    g_out_part = row_major(tn_dot(grad_full, normed).astype(BF16))
    w_out_t, g_out_part = tied(w_out_t, g_out_part)
    g_out_t = row_scatter(g_out_part)
    d_normed = mm(grad_full, w_out_t).astype(BF16).astype(F32)
    scaled = d_normed * norm_gain
    dots = jnp.sum(gated * scaled, axis=1)
    w_out_t, dots = tied(w_out_t, dots)
    if lines.shards == 4:
        out_parts = run_split(normed, w_out_t, 8, 512)
    else:
        out_parts = [nt_dot(normed, w_out_t).astype(BF16)]
    kept, came = lines.scatter_begin(out_parts)
    dots = lines.token_sum(dots)[:, None]
    d_gated = mix * scaled - gated * (mix * mix * mix * dots / inner_width)
    g_norm_gain = jnp.sum(d_normed * gated * mix, axis=0)
    open_gate = sigmoid(gate)
    d_heads = (d_gated * gate * open_gate).astype(BF16)
    d_gate = (d_gated * ho * (open_gate * (1.0 + gate * (1.0 - open_gate)))).astype(BF16)
    g_gate_part = row_major(tn_dot(normal_in, d_gate).astype(BF16))
    sent, came = lines.scatter_relay(kept, came)
    d_heads, g_gate_part, *sent = tied(d_heads, g_gate_part, *sent)
    g_gate = row_scatter(g_gate_part)

    d_value, d_states, d_steps, g_conv, g_decay = run_backward(
        lines.seat, pre, widened(d_heads, wide), states, steps, held, taps, offsets, rate, skip, pick,
        lines.shards, wide,
    )
    state_parts = lines.split_states(d_states)
    normal_in, *state_parts = tied(normal_in, *state_parts)
    g_value_part = row_major(tn_dot(normal_in, d_value).astype(BF16))
    g_value = row_scatter(g_value_part)
    branch_out = lines.scatter_end(sent, came)
    result = (hidden.astype(F32) + branch_out).astype(BF16)
    d_state_local, result, g_value_part = tied(lines.scatter_states(state_parts), result, g_value_part)
    d_bc_pre, g_conv_bc, g_conv_bc_bias = state_back(d_state_local)
    d_step = d_steps[:, :heads] * sigmoid(step_sum)
    small = lines.settle(widened(jnp.concatenate([d_bc_pre, d_step], axis=1), LANES)).astype(BF16)
    small, d_value, g_value_part = tied(small, d_value, g_value_part)
    if lines.shards == 4:
        pieces = {}
        turn = d_value
        for piece in (3, 1, 2, 0):
            pieces[piece] = run_rows(piece, d_gate, turn, small, w_gate_full, w_cat, piece_rows, 512)
            turn, last_part = tied(turn, pieces[piece][0])
        row_parts = [half for piece in range(4) for half in pieces[piece]]
    else:
        d_cat = jnp.concatenate([d_value, small], axis=1)
        row_parts = [(nt_dot(d_gate, w_gate_full) + nt_dot(d_cat, w_cat)).astype(BF16)]
    sent, came = lines.scatter_relay(*lines.scatter_begin(row_parts))
    parts = (
        g_conv[:4, :channels],
        g_conv[4, :channels],
        g_conv_bc,
        g_conv_bc_bias,
        jnp.sum(d_step, axis=0),
        (g_decay * rate)[0, :heads],
        jnp.sum(g_conv[5, :channels].reshape(heads, P_SIZE), axis=1),
        g_norm_gain,
    )
    packed = jnp.concatenate([part.reshape(-1) for part in parts])
    packed, last_part, normal_in, g_gate_part, g_value_part, *sent = tied(
        packed, row_parts[0], normal_in, g_gate_part, g_value_part, *sent
    )
    d_rows = lines.scatter_end(sent, came)
    packed = row_sum(packed)
    g_small_part = tn_dot(normal_in, small)
    g_small = row_scatter_small(g_small_part)
    tokens = hidden.astype(F32)
    scale = lax.rsqrt(jnp.mean(tokens * tokens, axis=1, keepdims=True) + EPSILON)
    scaled_rows = d_rows * full_gain
    grad_hidden = grad_out.astype(F32) + scale * (
        scaled_rows - tokens * (scale * scale * jnp.mean(tokens * scaled_rows, axis=1, keepdims=True))
    )

    g_in_gain = gain_sums(w_gate_full, g_gate_part, w_cat, g_value_part, g_small_part) / full_gain
    g_in_gain = row_sum(lines.own_slice(lines.total(g_in_gain)))
    summed = []
    at = 0
    for part in parts:
        summed.append(packed[at : at + part.size].reshape(part.shape))
        at += part.size
    return (
        result,
        grad_hidden,
        g_in_gain,
        g_gate,
        g_value[:, :channels],
        g_small[:, :bc_width],
        g_small[:, bc_width : bc_width + heads],
        *summed,
        g_out_t.T,
    )


def gain_sums(w_gate, g_gate, w_cat, g_value, g_small):
    wide = g_value.shape[1]
    return (
        jnp.sum(w_gate.astype(F32) * g_gate.astype(F32), axis=1)
        + jnp.sum(w_cat[:, :wide].astype(F32) * g_value.astype(F32), axis=1)
        + jnp.sum(w_cat[:, wide:].astype(F32) * g_small, axis=1)
    )


def solution(mesh):
    over_tokens = P(("row", "col"), None)
    square = P("row", "col")
    across = P(None, "col")
    vector = P("col")
    return jax.shard_map(
        body,
        mesh=mesh,
        in_specs=(
            over_tokens, vector, square, square, square, square, across, vector, across, vector,
            vector, vector, vector, vector, P("col", "row"), over_tokens,
        ),
        out_specs=(
            over_tokens, over_tokens, vector, square, square, square, square, across, vector, across,
            vector, vector, vector, vector, vector, P("col", "row"),
        ),
        check_vma=False,
    )
```

```python
import functools
import jax
import jax.numpy as jnp
from jax import lax
from jax.experimental import pallas as pl
from jax.experimental.pallas import tpu as pltpu
from jax.experimental.layout import Layout, with_layout_constraint
from jax.sharding import PartitionSpec as P


P_SIZE = 64
N = 128
Q = 128
LANES = 128
NEG = -1e30
HIGH = lax.Precision.HIGHEST
F32 = jnp.float32
BF16 = jnp.bfloat16


def sigmoid(v):
    return 0.5 * jnp.tanh(0.5 * v) + 0.5


def nt_dot(a, b):
    return lax.dot_general(a, b, (((1,), (1,)), ((), ())), preferred_element_type=F32)


def mm(a, b):
    return jnp.dot(a, b, preferred_element_type=F32)


def mm_exact(a, b):
    return jnp.dot(a, b, precision=HIGH, preferred_element_type=F32)


def turned(m):
    return m.astype(F32).T.astype(BF16)


def pair_cols(low_half, cols, first):
    return jnp.where(low_half, cols[:, first : first + 1], cols[:, first + 1 : first + 2])


def halves(low_half, v):
    zero = jnp.zeros_like(v)
    return jnp.concatenate([jnp.where(low_half, v, zero), jnp.where(low_half, zero, v)], axis=0)


def shifts(first_row, count, step):
    rows = lax.broadcasted_iota(jnp.int32, (count * Q, Q + 16), 0)
    lanes = lax.broadcasted_iota(jnp.int32, (count * Q, Q + 16), 1)
    part = lax.div(rows, Q)
    return (lanes == first_row + step * part + lax.rem(rows, Q)).astype(F32).astype(BF16)


def open_chunk(taps_ref, back_ref, prior, vp_ref, cols):
    now = vp_ref[:, cols]
    moved = mm(back_ref[...], jnp.concatenate([prior[:, cols], now], axis=0))
    seen = [moved[k * Q : (k + 1) * Q] for k in range(3)] + [now.astype(F32)]
    half = taps_ref[4:5, cols] + taps_ref[0:1, cols] * seen[0]
    for k in range(1, 4):
        half = half + taps_ref[k : k + 1, cols] * seen[k]
    return seen, half, jnp.tanh(half)


def scan_forward(
    seat_ref, vp_ref, bc_ref, st_ref, taps_ref, rate_ref, skip_ref,
    y_ref, hold_ref, state, halo, shut, *, pairs
):
    rows = lax.broadcasted_iota(jnp.int32, (Q, Q), 0)
    lanes = lax.broadcasted_iota(jnp.int32, (Q, Q), 1)

    @pl.when(pl.program_id(0) == 0)
    def _():
        state[...] = jnp.zeros_like(state)
        halo[0:8, :] = jnp.zeros_like(halo[0:8, :])
        shut[...] = jnp.where(rows >= lanes, 0.0, NEG)

    halo[8 : 8 + Q, :] = vp_ref[...].astype(F32)
    low_half = lanes < P_SIZE
    steps = st_ref[...]
    lam = mm_exact((rows >= lanes).astype(F32), steps * rate_ref[...])
    source_t = (lam - jnp.log(steps)).T
    grown = jnp.exp(lam)
    last = lam[Q - 1 : Q, :]
    weight = jnp.exp(last - lam) * steps
    fade = jnp.exp(last)
    b_rows = bc_ref[:, :N]
    c_rows = bc_ref[:, N:]
    b_t = turned(b_rows)
    scores = nt_dot(c_rows, b_rows)
    for pair in range(pairs):
        cols = slice(pair * LANES, (pair + 1) * LANES)
        first = 2 * pair
        half = taps_ref[4:5, cols] + taps_ref[0:1, cols] * halo[5 : 5 + Q, cols]
        for k in range(1, 4):
            half = half + taps_ref[k : k + 1, cols] * halo[5 + k : 5 + k + Q, cols]
        x = half * jnp.tanh(half) + half
        mixing = []
        for h in (first, first + 1):
            gap = lam[:, h : h + 1] - source_t[h : h + 1, :] + shut[...]
            mixing.append((scores * jnp.exp(gap)).astype(BF16))
        y = mm(jnp.concatenate(mixing, axis=1), halves(low_half, x).astype(BF16))
        held = state[:, cols]
        held_low = held.astype(BF16)
        y = y + mm(c_rows, held_low) * pair_cols(low_half, grown, first)
        y = y + skip_ref[:, cols] * x
        y_ref[:, cols] = y.astype(y_ref.dtype)
        hold_ref[0, :, cols] = held_low
        fed = (x * pair_cols(low_half, weight, first)).astype(BF16)
        state[:, cols] = held * pair_cols(low_half[0:1], fade, first) + mm(b_t, fed)
    halo[0:8, :] = halo[Q : Q + 8, :]


def scan_backward(
    seat_ref, vp_ref, before_ref, dy_ref, bc_ref, st_ref, hold_ref, taps_ref, rate_ref, skip_ref, pick_ref,
    dvp_ref, dbc_ref, dst_ref, gconv_ref, gdecay_ref,
    prior, g_next, back, ahead, shut, ds, ds_low, across, w_cols, w_rows, state_terms, inter_terms, fed_all, dyl_all,
    e_rows, *, pairs, blocks
):
    step_id = pl.program_id(0)
    rows = lax.broadcasted_iota(jnp.int32, (Q, Q), 0)
    lanes = lax.broadcasted_iota(jnp.int32, (Q, Q), 1)

    @pl.when(step_id == 0)
    def _():
        ds[...] = jnp.zeros_like(ds)
        g_next[...] = jnp.zeros_like(g_next)
        gconv_ref[...] = jnp.zeros_like(gconv_ref)
        gdecay_ref[...] = jnp.zeros_like(gdecay_ref)
        w_cols[...] = jnp.zeros_like(w_cols)
        w_rows[...] = jnp.zeros_like(w_rows)
        e_rows[...] = jnp.zeros_like(e_rows)
        back[...] = shifts(13, 3, 1)
        ahead[...] = shifts(1, 3, 1)
        shut[...] = jnp.where(lanes >= rows, 0.0, NEG)

    @pl.when(step_id < blocks - 1)
    def _():
        prior[...] = before_ref[...]

    @pl.when(step_id == blocks - 1)
    def _():
        prior[...] = jnp.zeros_like(prior)

    low_half = lanes < P_SIZE
    steps = st_ref[...]
    rate = rate_ref[...]
    lam = mm_exact((rows >= lanes).astype(F32), steps * rate)
    lam_t = lam.T
    source = lam - jnp.log(steps)
    grown = jnp.exp(lam)
    last = lam[Q - 1 : Q, :]
    weight = jnp.exp(last - lam) * steps
    fade = jnp.exp(last)
    b_rows = bc_ref[:, :N]
    c_rows = bc_ref[:, N:]
    c_t = turned(c_rows)
    scores_t = nt_dot(b_rows, c_rows)
    for pair in range(pairs):
        cols = slice(pair * LANES, (pair + 1) * LANES)
        first = 2 * pair
        seen, half, bend = open_chunk(taps_ref, back, prior, vp_ref, cols)
        x = half * bend + half
        dy = dy_ref[:, cols]
        dy_wide = dy.astype(F32)
        q_t = nt_dot(halves(low_half, x).astype(BF16), dy)
        mixing = []
        crossed = None
        for at, h in enumerate((first, first + 1)):
            decay = jnp.exp(lam_t[h : h + 1, :] - source[:, h : h + 1] + shut[...])
            stepped = decay * q_t[at * Q : (at + 1) * Q]
            crossed = stepped if crossed is None else crossed + stepped
            both = stepped * scores_t
            w_cols[:, h : h + 1] = jnp.sum(both, axis=1, keepdims=True)
            w_rows[h : h + 1, :] = jnp.sum(both, axis=0, keepdims=True)
            mixing.append((decay * scores_t).astype(BF16))
        if pair == 0:
            across[...] = crossed
        else:
            across[...] += crossed
        dx = mm(jnp.concatenate(mixing, axis=1), halves(low_half, dy_wide).astype(BF16))
        d_state = ds[:, cols]
        d_state_low = d_state.astype(BF16)
        ds_low[:, cols] = d_state_low
        weight_pair = pair_cols(low_half, weight, first)
        carried = weight_pair * mm(b_rows, d_state_low)
        dx = dx + carried + skip_ref[:, cols] * dy_wide
        state_terms[:, cols] = (x * carried).astype(BF16)
        fed_all[:, cols] = (x * weight_pair).astype(BF16)
        held = hold_ref[0, :, cols]
        dyl = dy_wide * pair_cols(low_half, grown, first)
        dyl_low = dyl.astype(BF16)
        dyl_all[:, cols] = dyl_low
        inter_terms[:, cols] = (dyl * mm(c_rows, held)).astype(BF16)
        e_rows[0:1, cols] = jnp.sum(d_state * held.astype(F32), axis=0, keepdims=True)
        ds[:, cols] = d_state * pair_cols(low_half[0:1], fade, first) + mm(c_t, dyl_low)
        g = dx * ((0.5 + 0.5 * bend) * (1.0 + half * (1.0 - bend)))
        for k in range(4):
            gconv_ref[k : k + 1, cols] += jnp.sum(g * seen[k], axis=0, keepdims=True)
        gconv_ref[4:5, cols] += jnp.sum(g, axis=0, keepdims=True)
        gconv_ref[5:6, cols] += jnp.sum(dy_wide * x, axis=0, keepdims=True)
        g_low = g.astype(BF16)
        moved = mm(ahead[...], jnp.concatenate([g_low, g_next[:, cols]], axis=0))
        d_pre = taps_ref[3:4, cols] * g
        for k in range(3):
            d_pre = d_pre + taps_ref[2 - k : 3 - k, cols] * moved[k * Q : (k + 1) * Q]
        dvp_ref[:, cols] = (2.0 * d_pre).astype(dvp_ref.dtype)
        g_next[:, cols] = g_low[0:16]
    cross = across[...]
    d_b = mm(cross.astype(BF16), c_rows) + nt_dot(fed_all[...], ds_low[...])
    d_c = mm(turned(cross), b_rows) + nt_dot(dyl_all[...], hold_ref[0])
    dbc_ref[:, :N] = d_b.astype(dbc_ref.dtype)
    dbc_ref[:, N:] = d_c.astype(dbc_ref.dtype)
    pick = pick_ref[...]
    from_state = mm(state_terms[...], pick)
    from_carry = mm(inter_terms[...], pick)
    e_high = e_rows[...].astype(BF16)
    e_rest = (e_rows[...] - e_high.astype(F32)).astype(BF16)
    through = (mm(e_high, pick) + mm(e_rest, pick))[0:1]
    w_all = w_cols[...]
    d_lam = w_rows[...].T - w_all + from_carry
    d_log = (
        mm_exact((lanes >= rows).astype(F32), d_lam)
        + mm_exact((rows > lanes).astype(F32), from_state)
        + fade * through
    )
    dst_ref[...] = (w_all + from_state) / jnp.maximum(steps, 1e-37) + rate * d_log
    gdecay_ref[...] += jnp.sum(steps * d_log, axis=0, keepdims=True)


def chunk_of(i, seat, per):
    return (lax.div(i, per) ^ seat[0]) * per + lax.rem(i, per)


def run_forward(seat, pre, states_in, steps, taps, rate, skip, shards):
    tokens = steps.shape[0]
    width = taps.shape[1]
    blocks = tokens // Q
    per = blocks // shards
    fixed = lambda i, seat: (0, 0)
    plain = lambda i, seat: (i, 0)
    moved = lambda i, seat: (chunk_of(i, seat, per), 0)
    return pl.pallas_call(
        functools.partial(scan_forward, pairs=width // LANES),
        out_shape=(
            jax.ShapeDtypeStruct((tokens, width), BF16),
            jax.ShapeDtypeStruct((blocks, N, width), BF16),
        ),
        grid_spec=pltpu.PrefetchScalarGridSpec(
            num_scalar_prefetch=1,
            grid=(blocks,),
            in_specs=[
                pl.BlockSpec((Q, width), moved),
                pl.BlockSpec((Q, 2 * N), plain),
                pl.BlockSpec((Q, LANES), plain),
                pl.BlockSpec((8, width), fixed),
                pl.BlockSpec((1, LANES), fixed),
                pl.BlockSpec((1, width), fixed),
            ],
            out_specs=[
                pl.BlockSpec((Q, width), moved),
                pl.BlockSpec((1, N, width), lambda i, seat: (i, 0, 0)),
            ],
            scratch_shapes=[
                pltpu.VMEM((N, width), F32),
                pltpu.VMEM((Q + 8, width), F32),
                pltpu.VMEM((Q, Q), F32),
            ],
        ),
        cost_estimate=pl.CostEstimate(
            flops=tokens * width * 1200, bytes_accessed=tokens * width * 10, transcendentals=tokens * width * 3
        ),
        name="scan_forward",
    )(seat, pre, states_in, steps, taps, rate, skip)


def run_backward(seat, pre, dy, states_in, steps, held, taps, rate, skip, pick, shards):
    tokens = steps.shape[0]
    width = taps.shape[1]
    blocks = tokens // Q
    per = blocks // shards
    fixed = lambda i, seat: (0, 0)
    plain = lambda i, seat: (blocks - 1 - i, 0)
    moved = lambda i, seat: (chunk_of(blocks - 1 - i, seat, per), 0)

    def before(i, seat):
        chunk = jnp.maximum(blocks - 2 - i, 0)
        return (chunk_of(chunk, seat, per) * (Q // 16) + Q // 16 - 1, 0)

    return pl.pallas_call(
        functools.partial(scan_backward, pairs=width // LANES, blocks=blocks),
        out_shape=(
            jax.ShapeDtypeStruct((tokens, width), BF16),
            jax.ShapeDtypeStruct((tokens, 2 * N), BF16),
            jax.ShapeDtypeStruct((tokens, LANES), F32),
            jax.ShapeDtypeStruct((8, width), F32),
            jax.ShapeDtypeStruct((1, LANES), F32),
        ),
        grid_spec=pltpu.PrefetchScalarGridSpec(
            num_scalar_prefetch=1,
            grid=(blocks,),
            in_specs=[
                pl.BlockSpec((Q, width), moved),
                pl.BlockSpec((16, width), before),
                pl.BlockSpec((Q, width), moved),
                pl.BlockSpec((Q, 2 * N), plain),
                pl.BlockSpec((Q, LANES), plain),
                pl.BlockSpec((1, N, width), lambda i, seat: (blocks - 1 - i, 0, 0)),
                pl.BlockSpec((8, width), fixed),
                pl.BlockSpec((1, LANES), fixed),
                pl.BlockSpec((1, width), fixed),
                pl.BlockSpec((width, LANES), fixed),
            ],
            out_specs=[
                pl.BlockSpec((Q, width), moved),
                pl.BlockSpec((Q, 2 * N), plain),
                pl.BlockSpec((Q, LANES), plain),
                pl.BlockSpec((8, width), fixed),
                pl.BlockSpec((1, LANES), fixed),
            ],
            scratch_shapes=[
                pltpu.VMEM((16, width), BF16),
                pltpu.VMEM((16, width), BF16),
                pltpu.VMEM((3 * Q, Q + 16), BF16),
                pltpu.VMEM((3 * Q, Q + 16), BF16),
                pltpu.VMEM((Q, Q), F32),
                pltpu.VMEM((N, width), F32),
                pltpu.VMEM((N, width), BF16),
                pltpu.VMEM((Q, Q), F32),
                pltpu.VMEM((Q, LANES), F32),
                pltpu.VMEM((LANES, Q), F32),
                pltpu.VMEM((Q, width), BF16),
                pltpu.VMEM((Q, width), BF16),
                pltpu.VMEM((Q, width), BF16),
                pltpu.VMEM((Q, width), BF16),
                pltpu.VMEM((8, width), F32),
            ],
        ),
        cost_estimate=pl.CostEstimate(
            flops=tokens * width * 3000, bytes_accessed=tokens * width * 14, transcendentals=tokens * width * 4
        ),
        name="scan_backward",
    )(seat, pre, pre, dy, states_in, steps, held, taps, rate, skip, pick)


EPSILON = 1e-05


def swish(v):
    return v * sigmoid(v)


def tn_dot(a, b):
    return lax.dot_general(a, b, (((0,), (0,)), ((), ())), preferred_element_type=F32)


def fill_kernel(x_ref, w_ref, *refs):
    value_ref, small_ref = refs[-2:]
    wide = value_ref.shape[1]
    small_ref[...] = mm(x_ref[...], w_ref[:, wide:])
    value_ref[...] = mm(x_ref[...], w_ref[:, :wide]).astype(BF16)


def run_fill(x, w, into, rows, first, block):
    depth, width = w.shape
    wide = width - LANES
    place = lambda i: (i + first, 0)
    return pl.pallas_call(
        fill_kernel,
        out_shape=(jax.ShapeDtypeStruct((rows, wide), BF16), jax.ShapeDtypeStruct((rows, LANES), F32)),
        grid=(x.shape[0] // block,),
        in_specs=[
            pl.BlockSpec((block, depth), lambda i: (i, 0)),
            pl.BlockSpec((depth, width), lambda i: (0, 0), pipeline_mode=pl.Buffered(1)),
        ]
        + [pl.BlockSpec(memory_space=pl.ANY)] * len(into),
        out_specs=(pl.BlockSpec((block, wide), place), pl.BlockSpec((block, LANES), place)),
        input_output_aliases={2: 0, 3: 1} if into else {},
        cost_estimate=pl.CostEstimate(
            flops=2 * x.shape[0] * depth * width,
            bytes_accessed=2 * (x.shape[0] + width) * (depth + width),
            transcendentals=0,
        ),
        name="value_product",
    )(x, w, *into)


def split_kernel(x_ref, w_ref, *out_refs):
    rows = out_refs[0].shape[0]
    for at, out_ref in enumerate(out_refs):
        out_ref[...] = nt_dot(x_ref[at * rows : (at + 1) * rows], w_ref[...]).astype(BF16)


def run_split(x, w, parts, block):
    tokens, depth = x.shape
    width = w.shape[0]
    rows = tokens // parts
    return pl.pallas_call(
        split_kernel,
        out_shape=[jax.ShapeDtypeStruct((rows, width), BF16)] * parts,
        grid=(width // block,),
        in_specs=[
            pl.BlockSpec((tokens, depth), lambda i: (0, 0), pipeline_mode=pl.Buffered(1)),
            pl.BlockSpec((block, depth), lambda i: (i, 0)),
        ],
        out_specs=[pl.BlockSpec((rows, block), lambda i: (0, i))] * parts,
        cost_estimate=pl.CostEstimate(
            flops=2 * tokens * depth * width, bytes_accessed=2 * (tokens + width) * depth + 2 * tokens * width, transcendentals=0
        ),
        name="split_product",
    )(x, w)


def rows_kernel(gate_ref, value_ref, small_ref, w_gate_ref, w_cat_ref, top_ref, low_ref):
    wide = value_ref.shape[1]
    rows = top_ref.shape[0]
    for at, out_ref in enumerate((top_ref, low_ref)):
        here = slice(at * rows, (at + 1) * rows)
        total = nt_dot(gate_ref[here], w_gate_ref[...])
        total = total + nt_dot(value_ref[here], w_cat_ref[:, :wide])
        total = total + nt_dot(small_ref[here], w_cat_ref[:, wide:])
        out_ref[...] = total.astype(BF16)


def run_rows(piece, d_gate, d_value, d_small, w_gate, w_cat, rows, block):
    width = w_gate.shape[0]
    depth = w_gate.shape[1] + w_cat.shape[1]
    mine = lambda i: (piece, 0)
    once = pl.Buffered(1)
    return pl.pallas_call(
        rows_kernel,
        out_shape=[jax.ShapeDtypeStruct((rows // 2, width), BF16)] * 2,
        grid=(width // block,),
        in_specs=[
            pl.BlockSpec((rows, d_gate.shape[1]), mine, pipeline_mode=once),
            pl.BlockSpec((rows, d_value.shape[1]), mine, pipeline_mode=once),
            pl.BlockSpec((rows, d_small.shape[1]), mine, pipeline_mode=once),
            pl.BlockSpec((block, w_gate.shape[1]), lambda i: (i, 0)),
            pl.BlockSpec((block, w_cat.shape[1]), lambda i: (i, 0)),
        ],
        out_specs=[pl.BlockSpec((rows // 2, block), lambda i: (0, i))] * 2,
        cost_estimate=pl.CostEstimate(
            flops=2 * rows * depth * width, bytes_accessed=2 * (rows + width) * depth + 2 * rows * width, transcendentals=0
        ),
        name="rows_product",
    )(d_gate, d_value, d_small, w_gate, w_cat)


def causal_conv(values, taps, offsets):
    tap_count = taps.shape[0]
    length = values.shape[0]
    padded = jnp.pad(values, ((tap_count - 1, 0), (0, 0)))
    summed = offsets[None, :] + taps[0][None, :] * padded[0:length]
    for offset in range(1, tap_count):
        summed = summed + taps[offset][None, :] * padded[offset : offset + length]
    return summed


def swap(v, bit, axis="col"):
    size = lax.axis_size(axis)
    return lax.ppermute(v, axis, [(i, i ^ bit) for i in range(size)])


def row_sum(v):
    bit = 1
    while bit < lax.axis_size("row"):
        v = v + swap(v, bit, "row")
        bit *= 2
    return v


class Square:
    shards = 4

    def __init__(self):
        self.place = lax.axis_index("col")
        self.x = lax.rem(self.place, 2) == 1
        self.y = lax.div(self.place, 2) == 1
        self.seat = jnp.reshape(self.place, (1,)).astype(jnp.int32)

    def settle(self, v):
        parts = v.reshape((2, 2, v.shape[0] // 4) + v.shape[1:])
        parts = jnp.where(self.y, parts[::-1], parts)
        parts = jnp.where(self.x, parts[:, ::-1], parts)
        return parts.reshape(v.shape)

    def gather_whole(self, v):
        from_x, from_y = swap(v, 1), swap(v, 2)
        half = v.shape[0] // 2
        relay_y = swap(from_x[:half], 2)
        relay_x = swap(from_y[half:], 1)
        return [v, from_x, from_y, relay_y, relay_x]

    def gather_top(self, v):
        half = v.shape[0] // 2
        top, low = v[:half], v[half:]
        return [v, low, swap(top, 1), swap(top, 2)]

    def gather_low(self, parts):
        v, low, x_top, y_top = parts
        x_low, y_low = swap(low, 1), swap(low, 2)
        relay_y = swap(x_top, 2)
        return [v, x_top, x_low, y_top, y_low, relay_y, swap(y_low, 1)]

    def gather_flat(self, v):
        others = [swap(v, bit) for bit in (1, 2, 3)]
        return self.settle(jnp.concatenate([v] + others))

    def token_sum(self, v):
        parts = v.reshape(2, 2, -1)
        parts = parts + swap(parts, 1)[:, ::-1]
        parts = parts + swap(parts, 2)[::-1]
        return parts.reshape(v.shape)

    def total(self, v):
        v = v + swap(v, 1)
        return v + swap(v, 2)

    def scatter_begin(self, halves_of):
        top, low, x_top, x_low, y_top, y_low, far_top, far_low = halves_of
        came = []
        for part, bit in ((far_top, 1), (far_low, 2), (x_top, 1), (y_low, 2)):
            came.append(swap(part, bit))
        return [x_low, y_top, top, low], came

    def scatter_relay(self, kept, came):
        beside, above, top, low = kept
        across_x, across_y, x_top, y_low = came
        x_low = (beside.astype(F32) + across_y.astype(F32)).astype(BF16)
        y_top = (above.astype(F32) + across_x.astype(F32)).astype(BF16)
        return [x_low, y_top], [top, low, x_top, y_low]

    def scatter_end(self, sent, came):
        x_low = swap(sent[0], 1)
        y_top = swap(sent[1], 2)
        top, low, x_top, y_low = (v.astype(F32) for v in came)
        return jnp.concatenate([top + x_top + y_top.astype(F32), low + x_low.astype(F32) + y_low])

    def gather_states(self, s):
        pair = jnp.concatenate([s, swap(s, 1)], axis=1)
        other = jnp.concatenate([swap(s, 2), swap(s, 3)], axis=1)
        return jnp.concatenate([jnp.where(self.y, other, pair), jnp.where(self.y, pair, other)], axis=1)

    def split_states(self, d):
        first, second = d[:, :N], d[:, N:]
        kept = jnp.where(self.y, second, first)
        given = jnp.where(self.y, first, second)
        half = N // 2
        return [kept[:, :half], kept[:, half:], given[:, :half], given[:, half:]]

    def scatter_states(self, parts):
        own = parts[0].astype(F32)
        for bit in (1, 2, 3):
            came = swap(parts[bit], bit)
            own = own + came.astype(F32)
        return own

    def own_slice(self, v):
        width = v.shape[0] // 4
        return lax.dynamic_slice(v, (self.place * width,), (width,))


class Line:
    shards = 1

    def __init__(self):
        self.seat = jnp.zeros((1,), jnp.int32)

    def settle(self, v):
        return v

    def gather_whole(self, v):
        return [lax.all_gather(v, "col", axis=0, tiled=True)]

    def gather_top(self, v):
        return self.gather_whole(v)

    def gather_low(self, parts):
        return parts

    def gather_flat(self, v):
        return lax.all_gather(v, "col", axis=0, tiled=True)

    def token_sum(self, v):
        return lax.psum(v, "col")

    def total(self, v):
        return lax.psum(v, "col")

    def scatter_begin(self, halves_of):
        return [], list(halves_of)

    def scatter_relay(self, kept, came):
        return came, []

    def scatter_end(self, sent, came):
        return lax.psum_scatter(sent[0], "col", scatter_dimension=0, tiled=True).astype(F32)

    def gather_states(self, s):
        return lax.all_gather(s, "col", axis=1, tiled=True)

    def split_states(self, d):
        return [d]

    def scatter_states(self, parts):
        return lax.psum_scatter(parts[0].astype(BF16), "col", scatter_dimension=1, tiled=True).astype(F32)

    def own_slice(self, v):
        width = v.shape[0] // lax.axis_size("col")
        return lax.dynamic_slice(v, (lax.axis_index("col") * width,), (width,))


def widened(v, width):
    return v if v.shape[-1] == width else jnp.pad(v, [(0, 0)] * (v.ndim - 1) + [(0, width - v.shape[-1])])


def tied(*values):
    return lax.optimization_barrier(values)


def row_major(v):
    return with_layout_constraint(v, Layout(major_to_minor=(0, 1)))


def row_scatter_small(v):
    bit = lax.axis_size("row") // 2
    place = lax.axis_index("row")
    while bit:
        half = v.shape[0] // 2
        upper = lax.rem(lax.div(place, bit), 2) == 1
        kept = jnp.where(upper, v[half:], v[:half])
        given = jnp.where(upper, v[:half], v[half:])
        v = kept + swap(given.astype(BF16), bit, "row").astype(F32)
        bit //= 2
    return v


def row_scatter(v):
    return lax.psum_scatter(v.astype(BF16), "row", scatter_dimension=0, tiled=True).astype(F32)


def body(
    hidden,
    in_gain,
    w_gate,
    w_value,
    w_bc,
    w_step,
    conv_value,
    conv_value_bias,
    conv_bc,
    conv_bc_bias,
    step_bias,
    decay_log,
    skip_gain,
    norm_gain,
    w_out,
    grad_out,
):
    lines = Square() if lax.axis_size("col") == 4 else Line()
    heads = step_bias.shape[0]
    channels = w_value.shape[1]
    inner_width = lax.axis_size("col") * channels
    bc_width = w_bc.shape[1]
    wide = -(-channels // LANES) * LANES
    full_width = wide + LANES
    piece_rows = hidden.shape[0]

    w_cat = lax.all_gather(
        widened(jnp.concatenate([widened(w_value, wide), w_bc, w_step], axis=1), full_width),
        "row", axis=0, tiled=True,
    )
    w_gate_full = lax.all_gather(w_gate, "row", axis=0, tiled=True)
    w_out_t = lax.all_gather(w_out.T, "row", axis=0, tiled=True)
    full_gain = lines.gather_flat(in_gain).astype(F32)

    def normalized(rows):
        rows = rows.astype(F32)
        scale = lax.rsqrt(jnp.mean(rows * rows, axis=1, keepdims=True) + EPSILON)
        return (rows * scale * full_gain).astype(BF16)

    hidden_pieces = lines.gather_whole(hidden)
    near = jnp.concatenate([normalized(piece) for piece in hidden_pieces[:3]])
    far = [normalized(piece) for piece in hidden_pieces[3:]]
    grad_source, _ = tied(grad_out, hidden_pieces[-1])
    grad_pieces = lines.gather_top(grad_source)

    if far:
        far = jnp.concatenate(far)
        tokens_here = near.shape[0] + far.shape[0]
        filled = run_fill(near, w_cat, (), tokens_here, 0, 256)
        pre, pre_small = run_fill(far, w_cat, filled, tokens_here, near.shape[0] // 256, 256)
        normal_in = jnp.concatenate([near, far])
    else:
        normal_in = near
        pre = mm(normal_in, w_cat[:, :wide]).astype(BF16)
        pre_small = mm(normal_in, w_cat[:, wide:])
    bc_pre = lines.settle(pre_small[:, :bc_width])
    step_sum = lines.settle(pre_small[:, bc_width : bc_width + heads]) + step_bias

    def state_branch(pre_vals, conv_weight, conv_offset):
        return swish(causal_conv(pre_vals, conv_weight, conv_offset))

    state_local, state_back = jax.vjp(state_branch, bc_pre, conv_bc, conv_bc_bias)
    states = lines.gather_states(state_local.astype(BF16))
    steps = widened(jax.nn.softplus(step_sum), LANES)
    rate = widened(-jnp.exp(decay_log), LANES)[None]
    skip = widened(jnp.repeat(skip_gain, P_SIZE), wide)[None]
    taps = 0.5 * jnp.concatenate([conv_value, conv_value_bias[None], jnp.zeros((3, channels), F32)])
    taps = widened(taps, wide)
    pick = (jnp.arange(wide)[:, None] // P_SIZE == jnp.arange(LANES)[None]).astype(BF16)
    states, *grad_pieces = tied(states, *grad_pieces)
    grad_pieces = lines.gather_low(grad_pieces)
    heads_out, held = run_forward(lines.seat, pre, states, steps, taps, rate, skip, lines.shards)

    gate_pre = mm(normal_in, w_gate_full).astype(BF16)
    ho = heads_out[:, :channels].astype(F32)
    gate = gate_pre.astype(F32)
    gated = ho * swish(gate)
    squares = jnp.sum(gated * gated, axis=1)
    squares = lines.token_sum(squares)
    mix = lax.rsqrt(squares / inner_width + EPSILON)[:, None]
    normed = (gated * mix * norm_gain).astype(BF16)
    normed, *grad_pieces = tied(normed, *grad_pieces)
    grad_full = jnp.concatenate(grad_pieces)

    g_out_part = row_major(tn_dot(grad_full, normed).astype(BF16))
    w_out_t, g_out_part = tied(w_out_t, g_out_part)
    g_out_t = row_scatter(g_out_part)
    d_normed = mm(grad_full, w_out_t).astype(BF16).astype(F32)
    scaled = d_normed * norm_gain
    dots = jnp.sum(gated * scaled, axis=1)
    w_out_t, dots = tied(w_out_t, dots)
    if lines.shards == 4:
        out_parts = run_split(normed, w_out_t, 8, 512)
    else:
        out_parts = [nt_dot(normed, w_out_t).astype(BF16)]
    kept, came = lines.scatter_begin(out_parts)
    dots = lines.token_sum(dots)[:, None]
    d_gated = mix * scaled - gated * (mix * mix * mix * dots / inner_width)
    g_norm_gain = jnp.sum(d_normed * gated * mix, axis=0)
    open_gate = sigmoid(gate)
    d_heads = (d_gated * gate * open_gate).astype(BF16)
    d_gate = (d_gated * ho * (open_gate * (1.0 + gate * (1.0 - open_gate)))).astype(BF16)
    g_gate_part = row_major(tn_dot(normal_in, d_gate).astype(BF16))
    sent, came = lines.scatter_relay(kept, came)
    d_heads, g_gate_part, *sent = tied(d_heads, g_gate_part, *sent)
    g_gate_sent, g_out_t = tied(g_gate_part, g_out_t)
    g_gate = row_scatter(g_gate_sent)

    d_value, d_states, d_steps, g_conv, g_decay = run_backward(
        lines.seat, pre, widened(d_heads, wide), states, steps, held, taps, rate, skip, pick, lines.shards
    )
    state_parts = lines.split_states(d_states)
    normal_in, *state_parts = tied(normal_in, *state_parts)
    g_value_part = row_major(tn_dot(normal_in, d_value).astype(BF16))
    g_value_sent, g_gate = tied(g_value_part, g_gate)
    g_value = row_scatter(g_value_sent)
    branch_out = lines.scatter_end(sent, came)
    result = (hidden.astype(F32) + branch_out).astype(BF16)
    d_state_local, result, g_value_part = tied(lines.scatter_states(state_parts), result, g_value_part)
    d_bc_pre, g_conv_bc, g_conv_bc_bias = state_back(d_state_local)
    d_step = d_steps[:, :heads] * sigmoid(step_sum)
    small = lines.settle(widened(jnp.concatenate([d_bc_pre, d_step], axis=1), LANES)).astype(BF16)
    small, d_value, g_value_part = tied(small, d_value, g_value_part)
    if lines.shards == 4:
        pieces = {}
        turn = d_value
        for piece in (3, 1, 2, 0):
            pieces[piece] = run_rows(piece, d_gate, turn, small, w_gate_full, w_cat, piece_rows, 512)
            turn, last_part = tied(turn, pieces[piece][0])
        row_parts = [half for piece in range(4) for half in pieces[piece]]
    else:
        d_cat = jnp.concatenate([d_value, small], axis=1)
        row_parts = [(nt_dot(d_gate, w_gate_full) + nt_dot(d_cat, w_cat)).astype(BF16)]
    sent, came = lines.scatter_relay(*lines.scatter_begin(row_parts))
    parts = (
        g_conv[:4, :channels],
        g_conv[4, :channels],
        g_conv_bc,
        g_conv_bc_bias,
        jnp.sum(d_step, axis=0),
        (g_decay * rate)[0, :heads],
        jnp.sum(g_conv[5, :channels].reshape(heads, P_SIZE), axis=1),
        g_norm_gain,
    )
    packed = jnp.concatenate([part.reshape(-1) for part in parts])
    packed, last_part, normal_in, g_gate_part, g_value_part, *sent = tied(
        packed, row_parts[0], normal_in, g_gate_part, g_value_part, *sent
    )
    d_rows = lines.scatter_end(sent, came)
    packed = row_sum(packed)
    g_small_part = tn_dot(normal_in, small)
    g_small = row_scatter_small(g_small_part)
    tokens = hidden.astype(F32)
    scale = lax.rsqrt(jnp.mean(tokens * tokens, axis=1, keepdims=True) + EPSILON)
    scaled_rows = d_rows * full_gain
    grad_hidden = grad_out.astype(F32) + scale * (
        scaled_rows - tokens * (scale * scale * jnp.mean(tokens * scaled_rows, axis=1, keepdims=True))
    )

    g_in_gain = gain_sums(w_gate_full, g_gate_part, w_cat, g_value_part, g_small_part) / full_gain
    g_in_gain = row_sum(lines.own_slice(lines.total(g_in_gain)))
    summed = []
    at = 0
    for part in parts:
        summed.append(packed[at : at + part.size].reshape(part.shape))
        at += part.size
    return (
        result,
        grad_hidden,
        g_in_gain,
        g_gate,
        g_value[:, :channels],
        g_small[:, :bc_width],
        g_small[:, bc_width : bc_width + heads],
        *summed,
        g_out_t.T,
    )


def gain_sums(w_gate, g_gate, w_cat, g_value, g_small):
    wide = g_value.shape[1]
    return (
        jnp.sum(w_gate.astype(F32) * g_gate.astype(F32), axis=1)
        + jnp.sum(w_cat[:, :wide].astype(F32) * g_value.astype(F32), axis=1)
        + jnp.sum(w_cat[:, wide:].astype(F32) * g_small, axis=1)
    )


def solution(mesh):
    over_tokens = P(("row", "col"), None)
    square = P("row", "col")
    across = P(None, "col")
    vector = P("col")
    return jax.shard_map(
        body,
        mesh=mesh,
        in_specs=(
            over_tokens, vector, square, square, square, square, across, vector, across, vector,
            vector, vector, vector, vector, P("col", "row"), over_tokens,
        ),
        out_specs=(
            over_tokens, over_tokens, vector, square, square, square, square, across, vector, across,
            vector, vector, vector, vector, vector, P("col", "row"),
        ),
        check_vma=False,
    )
```

```python
import functools
import jax
import jax.numpy as jnp
from jax import lax
from jax.experimental import pallas as pl
from jax.experimental.pallas import tpu as pltpu
from jax.experimental.layout import Layout, with_layout_constraint
from jax.sharding import PartitionSpec as P


P_SIZE = 64
N = 128
Q = 128
LANES = 128
NEG = -1e30
HIGH = lax.Precision.HIGHEST
F32 = jnp.float32
BF16 = jnp.bfloat16


def sigmoid(v):
    return 0.5 * jnp.tanh(0.5 * v) + 0.5


def nt_dot(a, b):
    return lax.dot_general(a, b, (((1,), (1,)), ((), ())), preferred_element_type=F32)


def mm(a, b):
    return jnp.dot(a, b, preferred_element_type=F32)


def mm_exact(a, b):
    return jnp.dot(a, b, precision=HIGH, preferred_element_type=F32)


def turned(m):
    return m.astype(F32).T.astype(BF16)


def pair_cols(low_half, cols, first):
    return jnp.where(low_half, cols[:, first : first + 1], cols[:, first + 1 : first + 2])


def halves(low_half, v):
    zero = jnp.zeros_like(v)
    return jnp.concatenate([jnp.where(low_half, v, zero), jnp.where(low_half, zero, v)], axis=0)


def shifts(first_row, count, step):
    rows = lax.broadcasted_iota(jnp.int32, (count * Q, Q + 16), 0)
    lanes = lax.broadcasted_iota(jnp.int32, (count * Q, Q + 16), 1)
    part = lax.div(rows, Q)
    return (lanes == first_row + step * part + lax.rem(rows, Q)).astype(F32).astype(BF16)


def open_chunk(taps_ref, back_ref, prior, vp_ref, cols):
    now = vp_ref[:, cols]
    moved = mm(back_ref[...], jnp.concatenate([prior[:, cols], now], axis=0))
    seen = [moved[k * Q : (k + 1) * Q] for k in range(3)] + [now.astype(F32)]
    half = taps_ref[4:5, cols] + taps_ref[0:1, cols] * seen[0]
    for k in range(1, 4):
        half = half + taps_ref[k : k + 1, cols] * seen[k]
    return seen, half, jnp.tanh(half)


def scan_forward(
    seat_ref, vp_ref, bc_ref, st_ref, taps_ref, rate_ref, skip_ref,
    y_ref, hold_ref, state, halo, shut, *, pairs
):
    rows = lax.broadcasted_iota(jnp.int32, (Q, Q), 0)
    lanes = lax.broadcasted_iota(jnp.int32, (Q, Q), 1)

    @pl.when(pl.program_id(0) == 0)
    def _():
        state[...] = jnp.zeros_like(state)
        halo[0:8, :] = jnp.zeros_like(halo[0:8, :])
        shut[...] = jnp.where(rows >= lanes, 0.0, NEG)

    halo[8 : 8 + Q, :] = vp_ref[...].astype(F32)
    low_half = lanes < P_SIZE
    steps = st_ref[...]
    lam = mm_exact((rows >= lanes).astype(F32), steps * rate_ref[...])
    source_t = (lam - jnp.log(steps)).T
    grown = jnp.exp(lam)
    last = lam[Q - 1 : Q, :]
    weight = jnp.exp(last - lam) * steps
    fade = jnp.exp(last)
    b_rows = bc_ref[:, :N]
    c_rows = bc_ref[:, N:]
    b_t = turned(b_rows)
    scores = nt_dot(c_rows, b_rows)
    for pair in range(pairs):
        cols = slice(pair * LANES, (pair + 1) * LANES)
        first = 2 * pair
        half = taps_ref[4:5, cols] + taps_ref[0:1, cols] * halo[5 : 5 + Q, cols]
        for k in range(1, 4):
            half = half + taps_ref[k : k + 1, cols] * halo[5 + k : 5 + k + Q, cols]
        x = half * jnp.tanh(half) + half
        mixing = []
        for h in (first, first + 1):
            gap = lam[:, h : h + 1] - source_t[h : h + 1, :] + shut[...]
            mixing.append((scores * jnp.exp(gap)).astype(BF16))
        y = mm(jnp.concatenate(mixing, axis=1), halves(low_half, x).astype(BF16))
        held = state[:, cols]
        held_low = held.astype(BF16)
        y = y + mm(c_rows, held_low) * pair_cols(low_half, grown, first)
        y = y + skip_ref[:, cols] * x
        y_ref[:, cols] = y.astype(y_ref.dtype)
        hold_ref[0, :, cols] = held_low
        fed = (x * pair_cols(low_half, weight, first)).astype(BF16)
        state[:, cols] = held * pair_cols(low_half[0:1], fade, first) + mm(b_t, fed)
    halo[0:8, :] = halo[Q : Q + 8, :]


def scan_backward(
    seat_ref, vp_ref, before_ref, dy_ref, bc_ref, st_ref, hold_ref, taps_ref, rate_ref, skip_ref, pick_ref,
    dvp_ref, dbc_ref, dst_ref, gconv_ref, gdecay_ref,
    prior, g_next, back, ahead, shut, ds, ds_low, across, w_cols, w_rows, state_terms, inter_terms, fed_all, dyl_all,
    e_rows, *, pairs, blocks
):
    step_id = pl.program_id(0)
    rows = lax.broadcasted_iota(jnp.int32, (Q, Q), 0)
    lanes = lax.broadcasted_iota(jnp.int32, (Q, Q), 1)

    @pl.when(step_id == 0)
    def _():
        ds[...] = jnp.zeros_like(ds)
        g_next[...] = jnp.zeros_like(g_next)
        gconv_ref[...] = jnp.zeros_like(gconv_ref)
        gdecay_ref[...] = jnp.zeros_like(gdecay_ref)
        w_cols[...] = jnp.zeros_like(w_cols)
        w_rows[...] = jnp.zeros_like(w_rows)
        e_rows[...] = jnp.zeros_like(e_rows)
        back[...] = shifts(13, 3, 1)
        ahead[...] = shifts(1, 3, 1)
        shut[...] = jnp.where(lanes >= rows, 0.0, NEG)

    @pl.when(step_id < blocks - 1)
    def _():
        prior[...] = before_ref[...]

    @pl.when(step_id == blocks - 1)
    def _():
        prior[...] = jnp.zeros_like(prior)

    low_half = lanes < P_SIZE
    steps = st_ref[...]
    rate = rate_ref[...]
    lam = mm_exact((rows >= lanes).astype(F32), steps * rate)
    lam_t = lam.T
    source = lam - jnp.log(steps)
    grown = jnp.exp(lam)
    last = lam[Q - 1 : Q, :]
    weight = jnp.exp(last - lam) * steps
    fade = jnp.exp(last)
    b_rows = bc_ref[:, :N]
    c_rows = bc_ref[:, N:]
    c_t = turned(c_rows)
    scores_t = nt_dot(b_rows, c_rows)
    for pair in range(pairs):
        cols = slice(pair * LANES, (pair + 1) * LANES)
        first = 2 * pair
        seen, half, bend = open_chunk(taps_ref, back, prior, vp_ref, cols)
        x = half * bend + half
        dy = dy_ref[:, cols]
        dy_wide = dy.astype(F32)
        q_t = nt_dot(halves(low_half, x).astype(BF16), dy)
        mixing = []
        crossed = None
        for at, h in enumerate((first, first + 1)):
            decay = jnp.exp(lam_t[h : h + 1, :] - source[:, h : h + 1] + shut[...])
            stepped = decay * q_t[at * Q : (at + 1) * Q]
            crossed = stepped if crossed is None else crossed + stepped
            both = stepped * scores_t
            w_cols[:, h : h + 1] = jnp.sum(both, axis=1, keepdims=True)
            w_rows[h : h + 1, :] = jnp.sum(both, axis=0, keepdims=True)
            mixing.append((decay * scores_t).astype(BF16))
        if pair == 0:
            across[...] = crossed
        else:
            across[...] += crossed
        dx = mm(jnp.concatenate(mixing, axis=1), halves(low_half, dy_wide).astype(BF16))
        d_state = ds[:, cols]
        d_state_low = d_state.astype(BF16)
        ds_low[:, cols] = d_state_low
        weight_pair = pair_cols(low_half, weight, first)
        carried = weight_pair * mm(b_rows, d_state_low)
        dx = dx + carried + skip_ref[:, cols] * dy_wide
        state_terms[:, cols] = (x * carried).astype(BF16)
        fed_all[:, cols] = (x * weight_pair).astype(BF16)
        held = hold_ref[0, :, cols]
        dyl = dy_wide * pair_cols(low_half, grown, first)
        dyl_low = dyl.astype(BF16)
        dyl_all[:, cols] = dyl_low
        inter_terms[:, cols] = (dyl * mm(c_rows, held)).astype(BF16)
        e_rows[0:1, cols] = jnp.sum(d_state * held.astype(F32), axis=0, keepdims=True)
        ds[:, cols] = d_state * pair_cols(low_half[0:1], fade, first) + mm(c_t, dyl_low)
        g = dx * ((0.5 + 0.5 * bend) * (1.0 + half * (1.0 - bend)))
        for k in range(4):
            gconv_ref[k : k + 1, cols] += jnp.sum(g * seen[k], axis=0, keepdims=True)
        gconv_ref[4:5, cols] += jnp.sum(g, axis=0, keepdims=True)
        gconv_ref[5:6, cols] += jnp.sum(dy_wide * x, axis=0, keepdims=True)
        g_low = g.astype(BF16)
        moved = mm(ahead[...], jnp.concatenate([g_low, g_next[:, cols]], axis=0))
        d_pre = taps_ref[3:4, cols] * g
        for k in range(3):
            d_pre = d_pre + taps_ref[2 - k : 3 - k, cols] * moved[k * Q : (k + 1) * Q]
        dvp_ref[:, cols] = (2.0 * d_pre).astype(dvp_ref.dtype)
        g_next[:, cols] = g_low[0:16]
    cross = across[...]
    d_b = mm(cross.astype(BF16), c_rows) + nt_dot(fed_all[...], ds_low[...])
    d_c = mm(turned(cross), b_rows) + nt_dot(dyl_all[...], hold_ref[0])
    dbc_ref[:, :N] = d_b.astype(dbc_ref.dtype)
    dbc_ref[:, N:] = d_c.astype(dbc_ref.dtype)
    pick = pick_ref[...]
    from_state = mm(state_terms[...], pick)
    from_carry = mm(inter_terms[...], pick)
    e_high = e_rows[...].astype(BF16)
    e_rest = (e_rows[...] - e_high.astype(F32)).astype(BF16)
    through = (mm(e_high, pick) + mm(e_rest, pick))[0:1]
    w_all = w_cols[...]
    d_lam = w_rows[...].T - w_all + from_carry
    d_log = (
        mm_exact((lanes >= rows).astype(F32), d_lam)
        + mm_exact((rows > lanes).astype(F32), from_state)
        + fade * through
    )
    dst_ref[...] = (w_all + from_state) / jnp.maximum(steps, 1e-37) + rate * d_log
    gdecay_ref[...] += jnp.sum(steps * d_log, axis=0, keepdims=True)


def chunk_of(i, seat, per):
    return (lax.div(i, per) ^ seat[0]) * per + lax.rem(i, per)


def run_forward(seat, pre, states_in, steps, taps, rate, skip, shards):
    tokens = steps.shape[0]
    width = taps.shape[1]
    blocks = tokens // Q
    per = blocks // shards
    fixed = lambda i, seat: (0, 0)
    plain = lambda i, seat: (i, 0)
    moved = lambda i, seat: (chunk_of(i, seat, per), 0)
    return pl.pallas_call(
        functools.partial(scan_forward, pairs=width // LANES),
        out_shape=(
            jax.ShapeDtypeStruct((tokens, width), BF16),
            jax.ShapeDtypeStruct((blocks, N, width), BF16),
        ),
        grid_spec=pltpu.PrefetchScalarGridSpec(
            num_scalar_prefetch=1,
            grid=(blocks,),
            in_specs=[
                pl.BlockSpec((Q, width), moved),
                pl.BlockSpec((Q, 2 * N), plain),
                pl.BlockSpec((Q, LANES), plain),
                pl.BlockSpec((8, width), fixed),
                pl.BlockSpec((1, LANES), fixed),
                pl.BlockSpec((1, width), fixed),
            ],
            out_specs=[
                pl.BlockSpec((Q, width), moved),
                pl.BlockSpec((1, N, width), lambda i, seat: (i, 0, 0)),
            ],
            scratch_shapes=[
                pltpu.VMEM((N, width), F32),
                pltpu.VMEM((Q + 8, width), F32),
                pltpu.VMEM((Q, Q), F32),
            ],
        ),
        cost_estimate=pl.CostEstimate(
            flops=tokens * width * 1200, bytes_accessed=tokens * width * 10, transcendentals=tokens * width * 3
        ),
        name="scan_forward",
    )(seat, pre, states_in, steps, taps, rate, skip)


def run_backward(seat, pre, dy, states_in, steps, held, taps, rate, skip, pick, shards):
    tokens = steps.shape[0]
    width = taps.shape[1]
    blocks = tokens // Q
    per = blocks // shards
    fixed = lambda i, seat: (0, 0)
    plain = lambda i, seat: (blocks - 1 - i, 0)
    moved = lambda i, seat: (chunk_of(blocks - 1 - i, seat, per), 0)

    def before(i, seat):
        chunk = jnp.maximum(blocks - 2 - i, 0)
        return (chunk_of(chunk, seat, per) * (Q // 16) + Q // 16 - 1, 0)

    return pl.pallas_call(
        functools.partial(scan_backward, pairs=width // LANES, blocks=blocks),
        out_shape=(
            jax.ShapeDtypeStruct((tokens, width), BF16),
            jax.ShapeDtypeStruct((tokens, 2 * N), BF16),
            jax.ShapeDtypeStruct((tokens, LANES), F32),
            jax.ShapeDtypeStruct((8, width), F32),
            jax.ShapeDtypeStruct((1, LANES), F32),
        ),
        grid_spec=pltpu.PrefetchScalarGridSpec(
            num_scalar_prefetch=1,
            grid=(blocks,),
            in_specs=[
                pl.BlockSpec((Q, width), moved),
                pl.BlockSpec((16, width), before),
                pl.BlockSpec((Q, width), moved),
                pl.BlockSpec((Q, 2 * N), plain),
                pl.BlockSpec((Q, LANES), plain),
                pl.BlockSpec((1, N, width), lambda i, seat: (blocks - 1 - i, 0, 0)),
                pl.BlockSpec((8, width), fixed),
                pl.BlockSpec((1, LANES), fixed),
                pl.BlockSpec((1, width), fixed),
                pl.BlockSpec((width, LANES), fixed),
            ],
            out_specs=[
                pl.BlockSpec((Q, width), moved),
                pl.BlockSpec((Q, 2 * N), plain),
                pl.BlockSpec((Q, LANES), plain),
                pl.BlockSpec((8, width), fixed),
                pl.BlockSpec((1, LANES), fixed),
            ],
            scratch_shapes=[
                pltpu.VMEM((16, width), BF16),
                pltpu.VMEM((16, width), BF16),
                pltpu.VMEM((3 * Q, Q + 16), BF16),
                pltpu.VMEM((3 * Q, Q + 16), BF16),
                pltpu.VMEM((Q, Q), F32),
                pltpu.VMEM((N, width), F32),
                pltpu.VMEM((N, width), BF16),
                pltpu.VMEM((Q, Q), F32),
                pltpu.VMEM((Q, LANES), F32),
                pltpu.VMEM((LANES, Q), F32),
                pltpu.VMEM((Q, width), BF16),
                pltpu.VMEM((Q, width), BF16),
                pltpu.VMEM((Q, width), BF16),
                pltpu.VMEM((Q, width), BF16),
                pltpu.VMEM((8, width), F32),
            ],
        ),
        cost_estimate=pl.CostEstimate(
            flops=tokens * width * 3000, bytes_accessed=tokens * width * 14, transcendentals=tokens * width * 4
        ),
        name="scan_backward",
    )(seat, pre, pre, dy, states_in, steps, held, taps, rate, skip, pick)


EPSILON = 1e-05


def swish(v):
    return v * sigmoid(v)


def tn_dot(a, b):
    return lax.dot_general(a, b, (((0,), (0,)), ((), ())), preferred_element_type=F32)


def fill_kernel(*refs, spans):
    gain_ref, w_ref = refs[len(spans) : len(spans) + 2]
    normal_ref, value_ref, small_ref = refs[-3:]
    step_id = pl.program_id(0)
    wide = value_ref.shape[1]
    for (start, stop), piece_ref in zip(spans, refs):

        @pl.when((step_id >= start) & (step_id < stop))
        def _(piece_ref=piece_ref):
            rows = piece_ref[...].astype(F32)
            scale = lax.rsqrt(jnp.mean(rows * rows, axis=1, keepdims=True) + EPSILON)
            normal_ref[...] = (rows * scale * gain_ref[...]).astype(BF16)

    small_ref[...] = mm(normal_ref[...], w_ref[:, wide:])
    value_ref[...] = mm(normal_ref[...], w_ref[:, :wide]).astype(BF16)


def run_fill(pieces, gain, w, into, rows, first, block):
    depth, width = w.shape
    wide = width - LANES
    place = lambda i: (i + first, 0)
    spans = []
    specs = []
    at = 0
    for piece in pieces:
        blocks = piece.shape[0] // block
        spans.append((at, at + blocks))
        specs.append(pl.BlockSpec((block, depth), lambda i, at=at, blocks=blocks: (jnp.clip(i - at, 0, blocks - 1), 0)))
        at += blocks
    return pl.pallas_call(
        functools.partial(fill_kernel, spans=spans),
        out_shape=(
            jax.ShapeDtypeStruct((rows, depth), BF16),
            jax.ShapeDtypeStruct((rows, wide), BF16),
            jax.ShapeDtypeStruct((rows, LANES), F32),
        ),
        grid=(at,),
        in_specs=specs
        + [
            pl.BlockSpec((1, depth), lambda i: (0, 0)),
            pl.BlockSpec((depth, width), lambda i: (0, 0), pipeline_mode=pl.Buffered(1)),
        ]
        + [pl.BlockSpec(memory_space=pl.ANY)] * len(into),
        out_specs=(
            pl.BlockSpec((block, depth), place), pl.BlockSpec((block, wide), place), pl.BlockSpec((block, LANES), place)
        ),
        input_output_aliases={len(pieces) + 2 + k: k for k in range(len(into))},
        cost_estimate=pl.CostEstimate(
            flops=2 * at * block * depth * width,
            bytes_accessed=2 * (at * block + width) * (depth + width),
            transcendentals=0,
        ),
        name="value_product",
    )(*pieces, gain, w, *into)


def split_kernel(x_ref, w_ref, *out_refs):
    rows = out_refs[0].shape[0]
    for at, out_ref in enumerate(out_refs):
        out_ref[...] = nt_dot(x_ref[at * rows : (at + 1) * rows], w_ref[...]).astype(BF16)


def run_split(x, w, parts, block):
    tokens, depth = x.shape
    width = w.shape[0]
    rows = tokens // parts
    return pl.pallas_call(
        split_kernel,
        out_shape=[jax.ShapeDtypeStruct((rows, width), BF16)] * parts,
        grid=(width // block,),
        in_specs=[
            pl.BlockSpec((tokens, depth), lambda i: (0, 0), pipeline_mode=pl.Buffered(1)),
            pl.BlockSpec((block, depth), lambda i: (i, 0)),
        ],
        out_specs=[pl.BlockSpec((rows, block), lambda i: (0, i))] * parts,
        cost_estimate=pl.CostEstimate(
            flops=2 * tokens * depth * width, bytes_accessed=2 * (tokens + width) * depth + 2 * tokens * width, transcendentals=0
        ),
        name="split_product",
    )(x, w)


def rows_kernel(gate_ref, value_ref, small_ref, w_gate_ref, w_cat_ref, top_ref, low_ref):
    wide = value_ref.shape[1]
    rows = top_ref.shape[0]
    for at, out_ref in enumerate((top_ref, low_ref)):
        here = slice(at * rows, (at + 1) * rows)
        total = nt_dot(gate_ref[here], w_gate_ref[...])
        total = total + nt_dot(value_ref[here], w_cat_ref[:, :wide])
        total = total + nt_dot(small_ref[here], w_cat_ref[:, wide:])
        out_ref[...] = total.astype(BF16)


def run_rows(piece, d_gate, d_value, d_small, w_gate, w_cat, rows, block):
    width = w_gate.shape[0]
    depth = w_gate.shape[1] + w_cat.shape[1]
    mine = lambda i: (piece, 0)
    once = pl.Buffered(1)
    return pl.pallas_call(
        rows_kernel,
        out_shape=[jax.ShapeDtypeStruct((rows // 2, width), BF16)] * 2,
        grid=(width // block,),
        in_specs=[
            pl.BlockSpec((rows, d_gate.shape[1]), mine, pipeline_mode=once),
            pl.BlockSpec((rows, d_value.shape[1]), mine, pipeline_mode=once),
            pl.BlockSpec((rows, d_small.shape[1]), mine, pipeline_mode=once),
            pl.BlockSpec((block, w_gate.shape[1]), lambda i: (i, 0)),
            pl.BlockSpec((block, w_cat.shape[1]), lambda i: (i, 0)),
        ],
        out_specs=[pl.BlockSpec((rows // 2, block), lambda i: (0, i))] * 2,
        cost_estimate=pl.CostEstimate(
            flops=2 * rows * depth * width, bytes_accessed=2 * (rows + width) * depth + 2 * rows * width, transcendentals=0
        ),
        name="rows_product",
    )(d_gate, d_value, d_small, w_gate, w_cat)


def causal_conv(values, taps, offsets):
    tap_count = taps.shape[0]
    length = values.shape[0]
    padded = jnp.pad(values, ((tap_count - 1, 0), (0, 0)))
    summed = offsets[None, :] + taps[0][None, :] * padded[0:length]
    for offset in range(1, tap_count):
        summed = summed + taps[offset][None, :] * padded[offset : offset + length]
    return summed


def swap(v, bit, axis="col"):
    size = lax.axis_size(axis)
    return lax.ppermute(v, axis, [(i, i ^ bit) for i in range(size)])


def row_sum(v):
    bit = 1
    while bit < lax.axis_size("row"):
        v = v + swap(v, bit, "row")
        bit *= 2
    return v


class Square:
    shards = 4

    def __init__(self):
        self.place = lax.axis_index("col")
        self.x = lax.rem(self.place, 2) == 1
        self.y = lax.div(self.place, 2) == 1
        self.seat = jnp.reshape(self.place, (1,)).astype(jnp.int32)

    def settle(self, v):
        parts = v.reshape((2, 2, v.shape[0] // 4) + v.shape[1:])
        parts = jnp.where(self.y, parts[::-1], parts)
        parts = jnp.where(self.x, parts[:, ::-1], parts)
        return parts.reshape(v.shape)

    def gather_whole(self, v):
        from_x, from_y = swap(v, 1), swap(v, 2)
        half = v.shape[0] // 2
        relay_y = swap(from_x[:half], 2)
        relay_x = swap(from_y[half:], 1)
        return [v, from_x, from_y, relay_y, relay_x]

    def gather_top(self, v):
        first, rest = v[: v.shape[0] // 4], v[v.shape[0] // 4 :]
        return [v, rest, swap(first, 1), swap(first, 2)]

    def gather_low(self, parts):
        v, rest, x_first, y_first = parts
        quarter = x_first.shape[0]
        x_rest, y_rest = swap(rest, 1), swap(rest, 2)
        far_first = swap(y_first, 1)
        far_middle = swap(x_rest[: 2 * quarter], 2)
        far_last = swap(y_rest[2 * quarter :], 1)
        return [v, x_first, x_rest, y_first, y_rest, far_first, far_middle, far_last]

    def gather_flat(self, v):
        others = [swap(v, bit) for bit in (1, 2, 3)]
        return self.settle(jnp.concatenate([v] + others))

    def token_sum(self, v):
        parts = v.reshape(2, 2, -1)
        parts = parts + swap(parts, 1)[:, ::-1]
        parts = parts + swap(parts, 2)[::-1]
        return parts.reshape(v.shape)

    def total(self, v):
        v = v + swap(v, 1)
        return v + swap(v, 2)

    def scatter_begin(self, halves_of):
        top, low, x_top, x_low, y_top, y_low, far_top, far_low = halves_of
        came = []
        for part, bit in ((far_top, 1), (far_low, 2), (x_top, 1), (y_low, 2)):
            came.append(swap(part, bit))
        return [x_low, y_top, top, low], came

    def scatter_relay(self, kept, came):
        beside, above, top, low = kept
        across_x, across_y, x_top, y_low = came
        x_low = (beside.astype(F32) + across_y.astype(F32)).astype(BF16)
        y_top = (above.astype(F32) + across_x.astype(F32)).astype(BF16)
        return [x_low, y_top], [top, low, x_top, y_low]

    def scatter_end(self, sent, came):
        x_low = swap(sent[0], 1)
        y_top = swap(sent[1], 2)
        top, low, x_top, y_low = (v.astype(F32) for v in came)
        return jnp.concatenate([top + x_top + y_top.astype(F32), low + x_low.astype(F32) + y_low])

    def gather_states(self, s):
        pair = jnp.concatenate([s, swap(s, 1)], axis=1)
        other = jnp.concatenate([swap(s, 2), swap(s, 3)], axis=1)
        return jnp.concatenate([jnp.where(self.y, other, pair), jnp.where(self.y, pair, other)], axis=1)

    def split_states(self, d):
        first, second = d[:, :N], d[:, N:]
        kept = jnp.where(self.y, second, first)
        given = jnp.where(self.y, first, second)
        half = N // 2
        return [kept[:, :half], kept[:, half:], given[:, :half], given[:, half:]]

    def scatter_states(self, parts):
        own = parts[0].astype(F32)
        for bit in (1, 2, 3):
            came = swap(parts[bit], bit)
            own = own + came.astype(F32)
        return own

    def own_slice(self, v):
        width = v.shape[0] // 4
        return lax.dynamic_slice(v, (self.place * width,), (width,))


class Line:
    shards = 1

    def __init__(self):
        self.seat = jnp.zeros((1,), jnp.int32)

    def settle(self, v):
        return v

    def gather_whole(self, v):
        return [lax.all_gather(v, "col", axis=0, tiled=True)]

    def gather_top(self, v):
        return self.gather_whole(v)

    def gather_low(self, parts):
        return parts

    def gather_flat(self, v):
        return lax.all_gather(v, "col", axis=0, tiled=True)

    def token_sum(self, v):
        return lax.psum(v, "col")

    def total(self, v):
        return lax.psum(v, "col")

    def scatter_begin(self, halves_of):
        return [], list(halves_of)

    def scatter_relay(self, kept, came):
        return came, []

    def scatter_end(self, sent, came):
        return lax.psum_scatter(sent[0], "col", scatter_dimension=0, tiled=True).astype(F32)

    def gather_states(self, s):
        return lax.all_gather(s, "col", axis=1, tiled=True)

    def split_states(self, d):
        return [d]

    def scatter_states(self, parts):
        return lax.psum_scatter(parts[0].astype(BF16), "col", scatter_dimension=1, tiled=True).astype(F32)

    def own_slice(self, v):
        width = v.shape[0] // lax.axis_size("col")
        return lax.dynamic_slice(v, (lax.axis_index("col") * width,), (width,))


def widened(v, width):
    return v if v.shape[-1] == width else jnp.pad(v, [(0, 0)] * (v.ndim - 1) + [(0, width - v.shape[-1])])


def tied(*values):
    return lax.optimization_barrier(values)


def row_major(v):
    return with_layout_constraint(v, Layout(major_to_minor=(0, 1)))


def row_scatter_small(v):
    bit = lax.axis_size("row") // 2
    place = lax.axis_index("row")
    while bit:
        half = v.shape[0] // 2
        upper = lax.rem(lax.div(place, bit), 2) == 1
        kept = jnp.where(upper, v[half:], v[:half])
        given = jnp.where(upper, v[:half], v[half:])
        v = kept + swap(given.astype(BF16), bit, "row").astype(F32)
        bit //= 2
    return v


def row_scatter(v):
    return lax.psum_scatter(v.astype(BF16), "row", scatter_dimension=0, tiled=True).astype(F32)


def body(
    hidden,
    in_gain,
    w_gate,
    w_value,
    w_bc,
    w_step,
    conv_value,
    conv_value_bias,
    conv_bc,
    conv_bc_bias,
    step_bias,
    decay_log,
    skip_gain,
    norm_gain,
    w_out,
    grad_out,
):
    lines = Square() if lax.axis_size("col") == 4 else Line()
    heads = step_bias.shape[0]
    channels = w_value.shape[1]
    inner_width = lax.axis_size("col") * channels
    bc_width = w_bc.shape[1]
    wide = -(-channels // LANES) * LANES
    full_width = wide + LANES
    piece_rows = hidden.shape[0]

    w_cat = lax.all_gather(
        widened(jnp.concatenate([widened(w_value, wide), w_bc, w_step], axis=1), full_width),
        "row", axis=0, tiled=True,
    )
    w_gate_full = lax.all_gather(w_gate, "row", axis=0, tiled=True)
    w_out_t = lax.all_gather(w_out.T, "row", axis=0, tiled=True)
    full_gain = lines.gather_flat(in_gain).astype(F32)

    def normalized(rows):
        rows = rows.astype(F32)
        scale = lax.rsqrt(jnp.mean(rows * rows, axis=1, keepdims=True) + EPSILON)
        return (rows * scale * full_gain).astype(BF16)

    hidden_pieces = lines.gather_whole(hidden)
    near, far = hidden_pieces[:3], hidden_pieces[3:]
    grad_source, _ = tied(grad_out, hidden_pieces[-1])
    grad_pieces = lines.gather_top(grad_source)

    if far:
        tokens_here = 4 * piece_rows
        half_rows = piece_rows // 2
        filled = run_fill(near, full_gain[None], w_cat, (), tokens_here, 0, half_rows)
        filled = run_fill(far, full_gain[None], w_cat, filled, tokens_here, 6, half_rows)
        normal_in, pre, pre_small = filled
    else:
        normal_in = normalized(near[0])
        pre = mm(normal_in, w_cat[:, :wide]).astype(BF16)
        pre_small = mm(normal_in, w_cat[:, wide:])
    bc_pre = lines.settle(pre_small[:, :bc_width])
    step_sum = lines.settle(pre_small[:, bc_width : bc_width + heads]) + step_bias

    def state_branch(pre_vals, conv_weight, conv_offset):
        return swish(causal_conv(pre_vals, conv_weight, conv_offset))

    state_local, state_back = jax.vjp(state_branch, bc_pre, conv_bc, conv_bc_bias)
    states = lines.gather_states(state_local.astype(BF16))
    steps = widened(jax.nn.softplus(step_sum), LANES)
    rate = widened(-jnp.exp(decay_log), LANES)[None]
    skip = widened(jnp.repeat(skip_gain, P_SIZE), wide)[None]
    taps = 0.5 * jnp.concatenate([conv_value, conv_value_bias[None], jnp.zeros((3, channels), F32)])
    taps = widened(taps, wide)
    pick = (jnp.arange(wide)[:, None] // P_SIZE == jnp.arange(LANES)[None]).astype(BF16)
    states, *grad_pieces[:2] = tied(states, *grad_pieces[:2])
    grad_pieces = lines.gather_low(grad_pieces)
    heads_out, held = run_forward(lines.seat, pre, states, steps, taps, rate, skip, lines.shards)

    gate_pre = mm(normal_in, w_gate_full).astype(BF16)
    ho = heads_out[:, :channels].astype(F32)
    gate = gate_pre.astype(F32)
    gated = ho * swish(gate)
    squares = jnp.sum(gated * gated, axis=1)
    squares = lines.token_sum(squares)
    mix = lax.rsqrt(squares / inner_width + EPSILON)[:, None]
    normed = (gated * mix * norm_gain).astype(BF16)
    normed, *grad_pieces = tied(normed, *grad_pieces)
    grad_full = jnp.concatenate(grad_pieces)

    g_out_part = row_major(tn_dot(grad_full, normed).astype(BF16))
    w_out_t, g_out_part = tied(w_out_t, g_out_part)
    g_out_t = row_scatter(g_out_part)
    d_normed = mm(grad_full, w_out_t).astype(BF16).astype(F32)
    scaled = d_normed * norm_gain
    dots = jnp.sum(gated * scaled, axis=1)
    w_out_t, dots = tied(w_out_t, dots)
    if lines.shards == 4:
        out_parts = run_split(normed, w_out_t, 8, 512)
    else:
        out_parts = [nt_dot(normed, w_out_t).astype(BF16)]
    kept, came = lines.scatter_begin(out_parts)
    dots = lines.token_sum(dots)[:, None]
    d_gated = mix * scaled - gated * (mix * mix * mix * dots / inner_width)
    g_norm_gain = jnp.sum(d_normed * gated * mix, axis=0)
    open_gate = sigmoid(gate)
    d_heads = (d_gated * gate * open_gate).astype(BF16)
    d_gate = (d_gated * ho * (open_gate * (1.0 + gate * (1.0 - open_gate)))).astype(BF16)
    g_gate_part = row_major(tn_dot(normal_in, d_gate).astype(BF16))
    early_sent, early_came = lines.scatter_relay(kept, came)
    d_heads, g_gate_part, *early_sent = tied(d_heads, g_gate_part, *early_sent)
    g_gate_sent, g_out_t = tied(g_gate_part, g_out_t)
    g_gate = row_scatter(g_gate_sent)

    d_value, d_states, d_steps, g_conv, g_decay = run_backward(
        lines.seat, pre, widened(d_heads, wide), states, steps, held, taps, rate, skip, pick, lines.shards
    )
    state_parts = lines.split_states(d_states)
    normal_in, *state_parts = tied(normal_in, *state_parts)
    g_value_part = row_major(tn_dot(normal_in, d_value).astype(BF16))
    g_value_sent, g_gate = tied(g_value_part, g_gate)
    g_value = row_scatter(g_value_sent)
    d_state_local, g_value_part = tied(lines.scatter_states(state_parts), g_value_part)
    d_bc_pre, g_conv_bc, g_conv_bc_bias = state_back(d_state_local)
    d_step = d_steps[:, :heads] * sigmoid(step_sum)
    small = lines.settle(widened(jnp.concatenate([d_bc_pre, d_step], axis=1), LANES)).astype(BF16)
    small, d_value, g_value_part = tied(small, d_value, g_value_part)
    if lines.shards == 4:
        pieces = {}
        turn = d_value
        for piece in (3, 1, 2, 0):
            pieces[piece] = run_rows(piece, d_gate, turn, small, w_gate_full, w_cat, piece_rows, 512)
            turn, last_part = tied(turn, pieces[piece][0])
        row_parts = [half for piece in range(4) for half in pieces[piece]]
    else:
        d_cat = jnp.concatenate([d_value, small], axis=1)
        row_parts = [(nt_dot(d_gate, w_gate_full) + nt_dot(d_cat, w_cat)).astype(BF16)]
    sent, came = lines.scatter_relay(*lines.scatter_begin(row_parts))
    parts = (
        g_conv[:4, :channels],
        g_conv[4, :channels],
        g_conv_bc,
        g_conv_bc_bias,
        jnp.sum(d_step, axis=0),
        (g_decay * rate)[0, :heads],
        jnp.sum(g_conv[5, :channels].reshape(heads, P_SIZE), axis=1),
        g_norm_gain,
    )
    sent_count = len(sent)
    last_part, normal_in, g_gate_part, g_value_part, *held_back = tied(
        row_parts[0], normal_in, g_gate_part, g_value_part, *sent, *early_came
    )
    sent, early_came = held_back[:sent_count], held_back[sent_count:]
    branch_out = lines.scatter_end(early_sent, early_came)
    result = (hidden.astype(F32) + branch_out).astype(BF16)
    d_rows = lines.scatter_end(sent, came)
    g_small_part = tn_dot(normal_in, small)
    g_small = row_scatter_small(g_small_part)
    tokens = hidden.astype(F32)
    scale = lax.rsqrt(jnp.mean(tokens * tokens, axis=1, keepdims=True) + EPSILON)
    scaled_rows = d_rows * full_gain
    grad_hidden = grad_out.astype(F32) + scale * (
        scaled_rows - tokens * (scale * scale * jnp.mean(tokens * scaled_rows, axis=1, keepdims=True))
    )

    g_in_gain = gain_sums(w_gate_full, g_gate_part, w_cat, g_value_part, g_small_part) / full_gain
    packed = row_sum(jnp.concatenate([part.reshape(-1) for part in parts] + [g_in_gain]))
    summed = []
    at = 0
    for part in parts:
        summed.append(packed[at : at + part.size].reshape(part.shape))
        at += part.size
    g_in_gain = lines.own_slice(lines.total(packed[at:]))
    return (
        result,
        grad_hidden,
        g_in_gain,
        g_gate,
        g_value[:, :channels],
        g_small[:, :bc_width],
        g_small[:, bc_width : bc_width + heads],
        *summed,
        g_out_t.T,
    )


def gain_sums(w_gate, g_gate, w_cat, g_value, g_small):
    wide = g_value.shape[1]
    return (
        jnp.sum(w_gate.astype(F32) * g_gate.astype(F32), axis=1)
        + jnp.sum(w_cat[:, :wide].astype(F32) * g_value.astype(F32), axis=1)
        + jnp.sum(w_cat[:, wide:].astype(F32) * g_small, axis=1)
    )


def solution(mesh):
    over_tokens = P(("row", "col"), None)
    square = P("row", "col")
    across = P(None, "col")
    vector = P("col")
    return jax.shard_map(
        body,
        mesh=mesh,
        in_specs=(
            over_tokens, vector, square, square, square, square, across, vector, across, vector,
            vector, vector, vector, vector, P("col", "row"), over_tokens,
        ),
        out_specs=(
            over_tokens, over_tokens, vector, square, square, square, square, across, vector, across,
            vector, vector, vector, vector, vector, P("col", "row"),
        ),
        check_vma=False,
    )
```

```python
import functools
import jax
import jax.numpy as jnp
from jax import lax
from jax.experimental import pallas as pl
from jax.experimental.pallas import tpu as pltpu
from jax.sharding import PartitionSpec as P


P_SIZE = 64
N = 128
Q = 128
LANES = 128
NEG = -1e30
HIGH = lax.Precision.HIGHEST
F32 = jnp.float32
BF16 = jnp.bfloat16


def sigmoid(v):
    return 0.5 * jnp.tanh(0.5 * v) + 0.5


def nt_dot(a, b):
    return lax.dot_general(a, b, (((1,), (1,)), ((), ())), preferred_element_type=F32)


def mm(a, b):
    return jnp.dot(a, b, preferred_element_type=F32)


def mm_exact(a, b):
    return jnp.dot(a, b, precision=HIGH, preferred_element_type=F32)


def turned(m):
    return m.astype(F32).T.astype(BF16)


def pair_cols(low_half, cols, first):
    return jnp.where(low_half, cols[:, first : first + 1], cols[:, first + 1 : first + 2])


def halves(low_half, v):
    zero = jnp.zeros_like(v)
    return jnp.concatenate([jnp.where(low_half, v, zero), jnp.where(low_half, zero, v)], axis=0)


def shifts(first_row, count, step):
    rows = lax.broadcasted_iota(jnp.int32, (count * Q, Q + 16), 0)
    lanes = lax.broadcasted_iota(jnp.int32, (count * Q, Q + 16), 1)
    part = lax.div(rows, Q)
    return (lanes == first_row + step * part + lax.rem(rows, Q)).astype(F32).astype(BF16)


def open_chunk(taps_ref, back_ref, prior, vp_ref, cols):
    now = vp_ref[:, cols]
    moved = mm(back_ref[...], jnp.concatenate([prior[:, cols], now], axis=0))
    seen = [moved[k * Q : (k + 1) * Q] for k in range(3)] + [now.astype(F32)]
    half = taps_ref[4:5, cols] + taps_ref[0:1, cols] * seen[0]
    for k in range(1, 4):
        half = half + taps_ref[k : k + 1, cols] * seen[k]
    return seen, half, jnp.tanh(half)


def scan_forward(
    seat_ref, vp_ref, bc_ref, st_ref, taps_ref, rate_ref, skip_ref,
    y_ref, hold_ref, state, halo, shut, *, pairs
):
    rows = lax.broadcasted_iota(jnp.int32, (Q, Q), 0)
    lanes = lax.broadcasted_iota(jnp.int32, (Q, Q), 1)

    @pl.when(pl.program_id(0) == 0)
    def _():
        state[...] = jnp.zeros_like(state)
        halo[0:8, :] = jnp.zeros_like(halo[0:8, :])
        shut[...] = jnp.where(rows >= lanes, 0.0, NEG)

    halo[8 : 8 + Q, :] = vp_ref[...].astype(F32)
    low_half = lanes < P_SIZE
    steps = st_ref[...]
    lam = mm_exact((rows >= lanes).astype(F32), steps * rate_ref[...])
    source_t = (lam - jnp.log(steps)).T
    grown = jnp.exp(lam)
    last = lam[Q - 1 : Q, :]
    weight = jnp.exp(last - lam) * steps
    fade = jnp.exp(last)
    b_rows = bc_ref[:, :N]
    c_rows = bc_ref[:, N:]
    b_t = turned(b_rows)
    scores = nt_dot(c_rows, b_rows)
    for pair in range(pairs):
        cols = slice(pair * LANES, (pair + 1) * LANES)
        first = 2 * pair
        half = taps_ref[4:5, cols] + taps_ref[0:1, cols] * halo[5 : 5 + Q, cols]
        for k in range(1, 4):
            half = half + taps_ref[k : k + 1, cols] * halo[5 + k : 5 + k + Q, cols]
        x = half * jnp.tanh(half) + half
        mixing = []
        for h in (first, first + 1):
            gap = lam[:, h : h + 1] - source_t[h : h + 1, :] + shut[...]
            mixing.append((scores * jnp.exp(gap)).astype(BF16))
        y = mm(jnp.concatenate(mixing, axis=1), halves(low_half, x).astype(BF16))
        held = state[:, cols]
        held_low = held.astype(BF16)
        y = y + mm(c_rows, held_low) * pair_cols(low_half, grown, first)
        y = y + skip_ref[:, cols] * x
        y_ref[:, cols] = y.astype(y_ref.dtype)
        hold_ref[0, :, cols] = held_low
        fed = (x * pair_cols(low_half, weight, first)).astype(BF16)
        state[:, cols] = held * pair_cols(low_half[0:1], fade, first) + mm(b_t, fed)
    halo[0:8, :] = halo[Q : Q + 8, :]


def scan_backward(
    seat_ref, vp_ref, before_ref, dy_ref, bc_ref, st_ref, hold_ref, taps_ref, rate_ref, skip_ref, pick_ref,
    dvp_ref, dbc_ref, dst_ref, gconv_ref, gdecay_ref,
    prior, g_next, back, ahead, shut, ds, ds_low, across, w_cols, w_rows, state_terms, inter_terms, fed_all, dyl_all,
    e_rows, *, pairs, blocks
):
    step_id = pl.program_id(0)
    rows = lax.broadcasted_iota(jnp.int32, (Q, Q), 0)
    lanes = lax.broadcasted_iota(jnp.int32, (Q, Q), 1)

    @pl.when(step_id == 0)
    def _():
        ds[...] = jnp.zeros_like(ds)
        g_next[...] = jnp.zeros_like(g_next)
        gconv_ref[...] = jnp.zeros_like(gconv_ref)
        gdecay_ref[...] = jnp.zeros_like(gdecay_ref)
        w_cols[...] = jnp.zeros_like(w_cols)
        w_rows[...] = jnp.zeros_like(w_rows)
        e_rows[...] = jnp.zeros_like(e_rows)
        back[...] = shifts(13, 3, 1)
        ahead[...] = shifts(1, 3, 1)
        shut[...] = jnp.where(lanes >= rows, 0.0, NEG)

    @pl.when(step_id < blocks - 1)
    def _():
        prior[...] = before_ref[...]

    @pl.when(step_id == blocks - 1)
    def _():
        prior[...] = jnp.zeros_like(prior)

    low_half = lanes < P_SIZE
    steps = st_ref[...]
    rate = rate_ref[...]
    lam = mm_exact((rows >= lanes).astype(F32), steps * rate)
    lam_t = lam.T
    source = lam - jnp.log(steps)
    grown = jnp.exp(lam)
    last = lam[Q - 1 : Q, :]
    weight = jnp.exp(last - lam) * steps
    fade = jnp.exp(last)
    b_rows = bc_ref[:, :N]
    c_rows = bc_ref[:, N:]
    c_t = turned(c_rows)
    scores_t = nt_dot(b_rows, c_rows)
    for pair in range(pairs):
        cols = slice(pair * LANES, (pair + 1) * LANES)
        first = 2 * pair
        seen, half, bend = open_chunk(taps_ref, back, prior, vp_ref, cols)
        x = half * bend + half
        dy = dy_ref[:, cols]
        dy_wide = dy.astype(F32)
        q_t = nt_dot(halves(low_half, x).astype(BF16), dy)
        mixing = []
        crossed = None
        for at, h in enumerate((first, first + 1)):
            decay = jnp.exp(lam_t[h : h + 1, :] - source[:, h : h + 1] + shut[...])
            stepped = decay * q_t[at * Q : (at + 1) * Q]
            crossed = stepped if crossed is None else crossed + stepped
            both = stepped * scores_t
            w_cols[:, h : h + 1] = jnp.sum(both, axis=1, keepdims=True)
            w_rows[h : h + 1, :] = jnp.sum(both, axis=0, keepdims=True)
            mixing.append((decay * scores_t).astype(BF16))
        if pair == 0:
            across[...] = crossed
        else:
            across[...] += crossed
        dx = mm(jnp.concatenate(mixing, axis=1), halves(low_half, dy_wide).astype(BF16))
        d_state = ds[:, cols]
        d_state_low = d_state.astype(BF16)
        ds_low[:, cols] = d_state_low
        weight_pair = pair_cols(low_half, weight, first)
        carried = weight_pair * mm(b_rows, d_state_low)
        dx = dx + carried + skip_ref[:, cols] * dy_wide
        state_terms[:, cols] = (x * carried).astype(BF16)
        fed_all[:, cols] = (x * weight_pair).astype(BF16)
        held = hold_ref[0, :, cols]
        dyl = dy_wide * pair_cols(low_half, grown, first)
        dyl_low = dyl.astype(BF16)
        dyl_all[:, cols] = dyl_low
        inter_terms[:, cols] = (dyl * mm(c_rows, held)).astype(BF16)
        e_rows[0:1, cols] = jnp.sum(d_state * held.astype(F32), axis=0, keepdims=True)
        ds[:, cols] = d_state * pair_cols(low_half[0:1], fade, first) + mm(c_t, dyl_low)
        g = dx * ((0.5 + 0.5 * bend) * (1.0 + half * (1.0 - bend)))
        for k in range(4):
            gconv_ref[k : k + 1, cols] += jnp.sum(g * seen[k], axis=0, keepdims=True)
        gconv_ref[4:5, cols] += jnp.sum(g, axis=0, keepdims=True)
        gconv_ref[5:6, cols] += jnp.sum(dy_wide * x, axis=0, keepdims=True)
        g_low = g.astype(BF16)
        moved = mm(ahead[...], jnp.concatenate([g_low, g_next[:, cols]], axis=0))
        d_pre = taps_ref[3:4, cols] * g
        for k in range(3):
            d_pre = d_pre + taps_ref[2 - k : 3 - k, cols] * moved[k * Q : (k + 1) * Q]
        dvp_ref[:, cols] = (2.0 * d_pre).astype(dvp_ref.dtype)
        g_next[:, cols] = g_low[0:16]
    cross = across[...]
    d_b = mm(cross.astype(BF16), c_rows) + nt_dot(fed_all[...], ds_low[...])
    d_c = mm(turned(cross), b_rows) + nt_dot(dyl_all[...], hold_ref[0])
    dbc_ref[:, :N] = d_b.astype(dbc_ref.dtype)
    dbc_ref[:, N:] = d_c.astype(dbc_ref.dtype)
    pick = pick_ref[...]
    from_state = mm(state_terms[...], pick)
    from_carry = mm(inter_terms[...], pick)
    e_high = e_rows[...].astype(BF16)
    e_rest = (e_rows[...] - e_high.astype(F32)).astype(BF16)
    through = (mm(e_high, pick) + mm(e_rest, pick))[0:1]
    w_all = w_cols[...]
    d_lam = w_rows[...].T - w_all + from_carry
    d_log = (
        mm_exact((lanes >= rows).astype(F32), d_lam)
        + mm_exact((rows > lanes).astype(F32), from_state)
        + fade * through
    )
    dst_ref[...] = (w_all + from_state) / jnp.maximum(steps, 1e-37) + rate * d_log
    gdecay_ref[...] += jnp.sum(steps * d_log, axis=0, keepdims=True)


def chunk_of(i, seat, per):
    return (lax.div(i, per) ^ seat[0]) * per + lax.rem(i, per)


def run_forward(seat, pre, states_in, steps, taps, rate, skip, shards):
    tokens = steps.shape[0]
    width = taps.shape[1]
    blocks = tokens // Q
    per = blocks // shards
    fixed = lambda i, seat: (0, 0)
    plain = lambda i, seat: (i, 0)
    moved = lambda i, seat: (chunk_of(i, seat, per), 0)
    return pl.pallas_call(
        functools.partial(scan_forward, pairs=width // LANES),
        out_shape=(
            jax.ShapeDtypeStruct((tokens, width), BF16),
            jax.ShapeDtypeStruct((blocks, N, width), BF16),
        ),
        grid_spec=pltpu.PrefetchScalarGridSpec(
            num_scalar_prefetch=1,
            grid=(blocks,),
            in_specs=[
                pl.BlockSpec((Q, width), moved),
                pl.BlockSpec((Q, 2 * N), plain),
                pl.BlockSpec((Q, LANES), plain),
                pl.BlockSpec((8, width), fixed),
                pl.BlockSpec((1, LANES), fixed),
                pl.BlockSpec((1, width), fixed),
            ],
            out_specs=[
                pl.BlockSpec((Q, width), moved),
                pl.BlockSpec((1, N, width), lambda i, seat: (i, 0, 0)),
            ],
            scratch_shapes=[
                pltpu.VMEM((N, width), F32),
                pltpu.VMEM((Q + 8, width), F32),
                pltpu.VMEM((Q, Q), F32),
            ],
        ),
        cost_estimate=pl.CostEstimate(
            flops=tokens * width * 1200, bytes_accessed=tokens * width * 10, transcendentals=tokens * width * 3
        ),
        name="scan_forward",
    )(seat, pre, states_in, steps, taps, rate, skip)


def run_backward(seat, pre, dy, states_in, steps, held, taps, rate, skip, pick, shards):
    tokens = steps.shape[0]
    width = taps.shape[1]
    blocks = tokens // Q
    per = blocks // shards
    fixed = lambda i, seat: (0, 0)
    plain = lambda i, seat: (blocks - 1 - i, 0)
    moved = lambda i, seat: (chunk_of(blocks - 1 - i, seat, per), 0)

    def before(i, seat):
        chunk = jnp.maximum(blocks - 2 - i, 0)
        return (chunk_of(chunk, seat, per) * (Q // 16) + Q // 16 - 1, 0)

    return pl.pallas_call(
        functools.partial(scan_backward, pairs=width // LANES, blocks=blocks),
        out_shape=(
            jax.ShapeDtypeStruct((tokens, width), BF16),
            jax.ShapeDtypeStruct((tokens, 2 * N), BF16),
            jax.ShapeDtypeStruct((tokens, LANES), F32),
            jax.ShapeDtypeStruct((8, width), F32),
            jax.ShapeDtypeStruct((1, LANES), F32),
        ),
        grid_spec=pltpu.PrefetchScalarGridSpec(
            num_scalar_prefetch=1,
            grid=(blocks,),
            in_specs=[
                pl.BlockSpec((Q, width), moved),
                pl.BlockSpec((16, width), before),
                pl.BlockSpec((Q, width), moved),
                pl.BlockSpec((Q, 2 * N), plain),
                pl.BlockSpec((Q, LANES), plain),
                pl.BlockSpec((1, N, width), lambda i, seat: (blocks - 1 - i, 0, 0)),
                pl.BlockSpec((8, width), fixed),
                pl.BlockSpec((1, LANES), fixed),
                pl.BlockSpec((1, width), fixed),
                pl.BlockSpec((width, LANES), fixed),
            ],
            out_specs=[
                pl.BlockSpec((Q, width), moved),
                pl.BlockSpec((Q, 2 * N), plain),
                pl.BlockSpec((Q, LANES), plain),
                pl.BlockSpec((8, width), fixed),
                pl.BlockSpec((1, LANES), fixed),
            ],
            scratch_shapes=[
                pltpu.VMEM((16, width), BF16),
                pltpu.VMEM((16, width), BF16),
                pltpu.VMEM((3 * Q, Q + 16), BF16),
                pltpu.VMEM((3 * Q, Q + 16), BF16),
                pltpu.VMEM((Q, Q), F32),
                pltpu.VMEM((N, width), F32),
                pltpu.VMEM((N, width), BF16),
                pltpu.VMEM((Q, Q), F32),
                pltpu.VMEM((Q, LANES), F32),
                pltpu.VMEM((LANES, Q), F32),
                pltpu.VMEM((Q, width), BF16),
                pltpu.VMEM((Q, width), BF16),
                pltpu.VMEM((Q, width), BF16),
                pltpu.VMEM((Q, width), BF16),
                pltpu.VMEM((8, width), F32),
            ],
        ),
        cost_estimate=pl.CostEstimate(
            flops=tokens * width * 3000, bytes_accessed=tokens * width * 14, transcendentals=tokens * width * 4
        ),
        name="scan_backward",
    )(seat, pre, pre, dy, states_in, steps, held, taps, rate, skip, pick)


EPSILON = 1e-05


def swish(v):
    return v * sigmoid(v)


def tn_dot(a, b):
    return lax.dot_general(a, b, (((0,), (0,)), ((), ())), preferred_element_type=F32)


def fill_kernel(*refs, spans):
    gain_ref, w_ref = refs[len(spans) : len(spans) + 2]
    normal_ref, value_ref, small_ref = refs[-3:]
    step_id = pl.program_id(0)
    wide = value_ref.shape[1]
    for (start, stop), piece_ref in zip(spans, refs):

        @pl.when((step_id >= start) & (step_id < stop))
        def _(piece_ref=piece_ref):
            rows = piece_ref[...].astype(F32)
            scale = lax.rsqrt(jnp.mean(rows * rows, axis=1, keepdims=True) + EPSILON)
            normal_ref[...] = (rows * scale * gain_ref[...]).astype(BF16)

    small_ref[...] = mm(normal_ref[...], w_ref[:, wide:])
    value_ref[...] = mm(normal_ref[...], w_ref[:, :wide]).astype(BF16)


def run_fill(pieces, gain, w, into, rows, first, block):
    depth, width = w.shape
    wide = width - LANES
    place = lambda i: (i + first, 0)
    spans = []
    specs = []
    at = 0
    for piece in pieces:
        blocks = piece.shape[0] // block
        spans.append((at, at + blocks))
        specs.append(pl.BlockSpec((block, depth), lambda i, at=at, blocks=blocks: (jnp.clip(i - at, 0, blocks - 1), 0)))
        at += blocks
    return pl.pallas_call(
        functools.partial(fill_kernel, spans=spans),
        out_shape=(
            jax.ShapeDtypeStruct((rows, depth), BF16),
            jax.ShapeDtypeStruct((rows, wide), BF16),
            jax.ShapeDtypeStruct((rows, LANES), F32),
        ),
        grid=(at,),
        in_specs=specs
        + [
            pl.BlockSpec((1, depth), lambda i: (0, 0)),
            pl.BlockSpec((depth, width), lambda i: (0, 0), pipeline_mode=pl.Buffered(1)),
        ]
        + [pl.BlockSpec(memory_space=pl.ANY)] * len(into),
        out_specs=(
            pl.BlockSpec((block, depth), place), pl.BlockSpec((block, wide), place), pl.BlockSpec((block, LANES), place)
        ),
        input_output_aliases={len(pieces) + 2 + k: k for k in range(len(into))},
        cost_estimate=pl.CostEstimate(
            flops=2 * at * block * depth * width,
            bytes_accessed=2 * (at * block + width) * (depth + width),
            transcendentals=0,
        ),
        name="value_product",
    )(*pieces, gain, w, *into)


def split_kernel(x_ref, w_ref, *out_refs):
    rows = out_refs[0].shape[0]
    for at, out_ref in enumerate(out_refs):
        out_ref[...] = nt_dot(x_ref[at * rows : (at + 1) * rows], w_ref[...]).astype(BF16)


def run_split(x, w, parts, block):
    tokens, depth = x.shape
    width = w.shape[0]
    rows = tokens // parts
    return pl.pallas_call(
        split_kernel,
        out_shape=[jax.ShapeDtypeStruct((rows, width), BF16)] * parts,
        grid=(width // block,),
        in_specs=[
            pl.BlockSpec((tokens, depth), lambda i: (0, 0), pipeline_mode=pl.Buffered(1)),
            pl.BlockSpec((block, depth), lambda i: (i, 0)),
        ],
        out_specs=[pl.BlockSpec((rows, block), lambda i: (0, i))] * parts,
        cost_estimate=pl.CostEstimate(
            flops=2 * tokens * depth * width, bytes_accessed=2 * (tokens + width) * depth + 2 * tokens * width, transcendentals=0
        ),
        name="split_product",
    )(x, w)


def rows_kernel(*refs):
    w_gate_ref, w_cat_ref = refs[6:8]
    wide = refs[2].shape[1]
    for at in range(2):
        gate_ref, value_ref, small_ref = refs[at:6:2]
        total = nt_dot(gate_ref[...], w_gate_ref[...])
        total = total + nt_dot(value_ref[...], w_cat_ref[:, :wide])
        total = total + nt_dot(small_ref[...], w_cat_ref[:, wide:])
        refs[8 + at][...] = total.astype(BF16)


def run_rows(blocks, d_gate, d_value, d_small, w_gate, w_cat, rows, block):
    width = w_gate.shape[0]
    depth = w_gate.shape[1] + w_cat.shape[1]
    given = [v for v in (d_gate, d_value, d_small) for _ in blocks]
    specs = [
        pl.BlockSpec((rows, v.shape[1]), lambda i, at=at: (at, 0), pipeline_mode=pl.Buffered(1))
        for v in (d_gate, d_value, d_small)
        for at in blocks
    ]
    return pl.pallas_call(
        rows_kernel,
        out_shape=[jax.ShapeDtypeStruct((rows, width), BF16)] * 2,
        grid=(width // block,),
        in_specs=specs
        + [
            pl.BlockSpec((block, w_gate.shape[1]), lambda i: (i, 0)),
            pl.BlockSpec((block, w_cat.shape[1]), lambda i: (i, 0)),
        ],
        out_specs=[pl.BlockSpec((rows, block), lambda i: (0, i))] * 2,
        cost_estimate=pl.CostEstimate(
            flops=4 * rows * depth * width, bytes_accessed=2 * (2 * rows + width) * depth + 4 * rows * width, transcendentals=0
        ),
        name="rows_product",
    )(*given, w_gate, w_cat)


def turned_kernel(a_ref, b_ref, out_ref):
    out_ref[...] = tn_dot(a_ref[...], b_ref[...]).astype(BF16)


def run_turned(a, b, block):
    tokens, depth = a.shape
    width = b.shape[1]
    return pl.pallas_call(
        turned_kernel,
        out_shape=jax.ShapeDtypeStruct((depth, width), BF16),
        grid=(depth // block,),
        in_specs=[
            pl.BlockSpec((tokens, block), lambda i: (0, i)),
            pl.BlockSpec((tokens, width), lambda i: (0, 0), pipeline_mode=pl.Buffered(1)),
        ],
        out_specs=pl.BlockSpec((block, width), lambda i: (i, 0)),
        cost_estimate=pl.CostEstimate(
            flops=2 * tokens * depth * width, bytes_accessed=2 * (tokens * (depth + width) + depth * width), transcendentals=0
        ),
        name="weight_product",
    )(a, b)


def causal_conv(values, taps, offsets):
    tap_count = taps.shape[0]
    length = values.shape[0]
    padded = jnp.pad(values, ((tap_count - 1, 0), (0, 0)))
    summed = offsets[None, :] + taps[0][None, :] * padded[0:length]
    for offset in range(1, tap_count):
        summed = summed + taps[offset][None, :] * padded[offset : offset + length]
    return summed


def swap(v, bit, axis="col"):
    size = lax.axis_size(axis)
    return lax.ppermute(v, axis, [(i, i ^ bit) for i in range(size)])


def row_sum(v):
    bit = 1
    while bit < lax.axis_size("row"):
        v = v + swap(v, bit, "row")
        bit *= 2
    return v


class Square:
    shards = 4

    def __init__(self):
        self.place = lax.axis_index("col")
        self.x = lax.rem(self.place, 2) == 1
        self.y = lax.div(self.place, 2) == 1
        self.seat = jnp.reshape(self.place, (1,)).astype(jnp.int32)

    def settle(self, v):
        parts = v.reshape((2, 2, v.shape[0] // 4) + v.shape[1:])
        parts = jnp.where(self.y, parts[::-1], parts)
        parts = jnp.where(self.x, parts[:, ::-1], parts)
        return parts.reshape(v.shape)

    def gather_whole(self, v):
        from_x, from_y = swap(v, 1), swap(v, 2)
        half = v.shape[0] // 2
        relay_y = swap(from_x[:half], 2)
        relay_x = swap(from_y[half:], 1)
        return [v, from_x, from_y, relay_y, relay_x]

    def gather_top(self, v):
        first, rest = v[: v.shape[0] // 4], v[v.shape[0] // 4 :]
        return [v, rest, swap(first, 1), swap(first, 2)]

    def gather_low(self, parts):
        v, rest, x_first, y_first = parts
        quarter = x_first.shape[0]
        x_rest, y_rest = swap(rest, 1), swap(rest, 2)
        far_first = swap(y_first, 1)
        far_middle = swap(x_rest[: 2 * quarter], 2)
        far_last = swap(y_rest[2 * quarter :], 1)
        return [v, x_first, x_rest, y_first, y_rest, far_first, far_middle, far_last]

    def gather_flat(self, v):
        others = [swap(v, bit) for bit in (1, 2, 3)]
        return self.settle(jnp.concatenate([v] + others))

    def token_sum(self, v):
        parts = v.reshape(2, 2, -1)
        parts = parts + swap(parts, 1)[:, ::-1]
        parts = parts + swap(parts, 2)[::-1]
        return parts.reshape(v.shape)

    def total(self, v):
        v = v + swap(v, 1)
        return v + swap(v, 2)

    def scatter_far(self, far_top, far_low):
        return swap(far_top, 1), swap(far_low, 2)

    def scatter_near(self, x_top, y_low):
        return swap(x_top, 1), swap(y_low, 2)

    def scatter_add(self, x_low, y_top, far_came):
        across_x, across_y = far_came
        return [
            (x_low.astype(F32) + across_y.astype(F32)).astype(BF16),
            (y_top.astype(F32) + across_x.astype(F32)).astype(BF16),
        ]

    def scatter_end(self, sent, own, near_came):
        x_low, y_top = swap(sent[0], 1), swap(sent[1], 2)
        top, low, x_top, y_low = (v.astype(F32) for v in (*own, *near_came))
        return jnp.concatenate([top + x_top + y_top.astype(F32), low + x_low.astype(F32) + y_low])

    def dense_swap(self, v, bit):
        half, width = v.shape[0] // 2, v.shape[1]
        came = swap(jnp.concatenate([v[:half], v[half:]], axis=1), bit)
        return jnp.concatenate([came[:, :width], came[:, width:]])

    def gather_states(self, s):
        pair = jnp.concatenate([s, self.dense_swap(s, 1)], axis=1)
        other = jnp.concatenate([self.dense_swap(s, 2), self.dense_swap(s, 3)], axis=1)
        return jnp.concatenate([jnp.where(self.y, other, pair), jnp.where(self.y, pair, other)], axis=1)

    def split_states(self, d):
        first, second = d[:, :N], d[:, N:]
        kept = jnp.where(self.y, second, first)
        given = jnp.where(self.y, first, second)
        half = N // 2
        return [kept[:, :half], kept[:, half:], given[:, :half], given[:, half:]]

    def scatter_states(self, parts):
        own = parts[0].astype(F32)
        for bit in (1, 2, 3):
            own = own + self.dense_swap(parts[bit], bit).astype(F32)
        return own

    def own_slice(self, v):
        width = v.shape[0] // 4
        return lax.dynamic_slice(v, (self.place * width,), (width,))


class Line:
    shards = 1

    def __init__(self):
        self.seat = jnp.zeros((1,), jnp.int32)

    def settle(self, v):
        return v

    def gather_whole(self, v):
        return [lax.all_gather(v, "col", axis=0, tiled=True)]

    def gather_top(self, v):
        return self.gather_whole(v)

    def gather_low(self, parts):
        return parts

    def gather_flat(self, v):
        return lax.all_gather(v, "col", axis=0, tiled=True)

    def token_sum(self, v):
        return lax.psum(v, "col")

    def total(self, v):
        return lax.psum(v, "col")

    def scatter_whole(self, v):
        return lax.psum_scatter(v, "col", scatter_dimension=0, tiled=True).astype(F32)

    def gather_states(self, s):
        return lax.all_gather(s, "col", axis=1, tiled=True)

    def split_states(self, d):
        return [d]

    def scatter_states(self, parts):
        return lax.psum_scatter(parts[0].astype(BF16), "col", scatter_dimension=1, tiled=True).astype(F32)

    def own_slice(self, v):
        width = v.shape[0] // lax.axis_size("col")
        return lax.dynamic_slice(v, (lax.axis_index("col") * width,), (width,))


def widened(v, width):
    return v if v.shape[-1] == width else jnp.pad(v, [(0, 0)] * (v.ndim - 1) + [(0, width - v.shape[-1])])


def tied(*values):
    return lax.optimization_barrier(values)


def row_scatter_small(v):
    bit = lax.axis_size("row") // 2
    place = lax.axis_index("row")
    while bit:
        half = v.shape[0] // 2
        upper = lax.rem(lax.div(place, bit), 2) == 1
        kept = jnp.where(upper, v[half:], v[:half])
        given = jnp.where(upper, v[:half], v[half:])
        v = kept + swap(given.astype(BF16), bit, "row").astype(F32)
        bit //= 2
    return v


def row_scatter(v):
    return lax.psum_scatter(v, "row", scatter_dimension=0, tiled=True)


def body(
    hidden,
    in_gain,
    w_gate,
    w_value,
    w_bc,
    w_step,
    conv_value,
    conv_value_bias,
    conv_bc,
    conv_bc_bias,
    step_bias,
    decay_log,
    skip_gain,
    norm_gain,
    w_out,
    grad_out,
):
    lines = Square() if lax.axis_size("col") == 4 else Line()
    heads = step_bias.shape[0]
    channels = w_value.shape[1]
    inner_width = lax.axis_size("col") * channels
    bc_width = w_bc.shape[1]
    wide = -(-channels // LANES) * LANES
    full_width = wide + LANES
    piece_rows = hidden.shape[0]

    w_cat = lax.all_gather(
        widened(jnp.concatenate([widened(w_value, wide), w_bc, w_step], axis=1), full_width),
        "row", axis=0, tiled=True,
    )
    w_gate_full = lax.all_gather(w_gate, "row", axis=0, tiled=True)
    w_out_t = lax.all_gather(w_out.T, "row", axis=0, tiled=True)
    full_gain = lines.gather_flat(in_gain).astype(F32)

    def weight_grad(a, b):
        return run_turned(a, b, 256) if lines.shards == 4 else tn_dot(a, b).astype(BF16)

    def normalized(rows):
        rows = rows.astype(F32)
        scale = lax.rsqrt(jnp.mean(rows * rows, axis=1, keepdims=True) + EPSILON)
        return (rows * scale * full_gain).astype(BF16)

    hidden_pieces = lines.gather_whole(hidden)
    grad_source, hidden_pieces[-1] = tied(grad_out, hidden_pieces[-1])
    grad_pieces = lines.gather_top(grad_source)
    near, far = hidden_pieces[:3], hidden_pieces[3:]

    if far:
        tokens_here = 4 * piece_rows
        half_rows = piece_rows // 2
        filled = run_fill(near, full_gain[None], w_cat, (), tokens_here, 0, half_rows)
        filled = run_fill(far, full_gain[None], w_cat, filled, tokens_here, 6, half_rows)
        normal_in, pre, pre_small = filled
    else:
        normal_in = normalized(near[0])
        pre = mm(normal_in, w_cat[:, :wide]).astype(BF16)
        pre_small = mm(normal_in, w_cat[:, wide:])
    bc_pre = lines.settle(pre_small[:, :bc_width])
    step_sum = lines.settle(pre_small[:, bc_width : bc_width + heads]) + step_bias

    def state_branch(pre_vals, conv_weight, conv_offset):
        return swish(causal_conv(pre_vals, conv_weight, conv_offset))

    state_local, state_back = jax.vjp(state_branch, bc_pre, conv_bc, conv_bc_bias)
    states = lines.gather_states(state_local.astype(BF16))
    steps = widened(jax.nn.softplus(step_sum), LANES)
    rate = widened(-jnp.exp(decay_log), LANES)[None]
    skip = widened(jnp.repeat(skip_gain, P_SIZE), wide)[None]
    taps = 0.5 * jnp.concatenate([conv_value, conv_value_bias[None], jnp.zeros((3, channels), F32)])
    taps = widened(taps, wide)
    pick = (jnp.arange(wide)[:, None] // P_SIZE == jnp.arange(LANES)[None]).astype(BF16)
    states, *grad_pieces[:2] = tied(states, *grad_pieces[:2])
    grad_pieces = lines.gather_low(grad_pieces)
    heads_out, held = run_forward(lines.seat, pre, states, steps, taps, rate, skip, lines.shards)

    gate_pre = mm(normal_in, w_gate_full).astype(BF16)
    ho = heads_out[:, :channels].astype(F32)
    gate = gate_pre.astype(F32)
    gated = ho * swish(gate)
    squares = jnp.sum(gated * gated, axis=1)
    squares = lines.token_sum(squares)
    mix = lax.rsqrt(squares / inner_width + EPSILON)[:, None]
    normed = (gated * mix * norm_gain).astype(BF16)
    normed, *grad_pieces = tied(normed, *grad_pieces)
    grad_full = jnp.concatenate(grad_pieces)

    g_out_part = weight_grad(grad_full, normed)
    w_out_t, g_out_part = tied(w_out_t, g_out_part)
    g_out_t = row_scatter(g_out_part)
    d_normed = mm(grad_full, w_out_t).astype(BF16).astype(F32)
    scaled = d_normed * norm_gain
    dots = jnp.sum(gated * scaled, axis=1)
    w_out_t, dots = tied(w_out_t, dots)
    if lines.shards == 4:
        out_parts = run_split(normed, w_out_t, 8, 512)
        early_far = lines.scatter_far(*out_parts[6:])
        early_near = lines.scatter_near(out_parts[2], out_parts[5])
    else:
        branch_out = lines.scatter_whole(nt_dot(normed, w_out_t).astype(BF16))
    dots = lines.token_sum(dots)[:, None]
    d_gated = mix * scaled - gated * (mix * mix * mix * dots / inner_width)
    g_norm_gain = jnp.sum(d_normed * gated * mix, axis=0)
    open_gate = sigmoid(gate)
    d_heads = (d_gated * gate * open_gate).astype(BF16)
    d_gate = (d_gated * ho * (open_gate * (1.0 + gate * (1.0 - open_gate)))).astype(BF16)
    g_gate_part = weight_grad(normal_in, d_gate)
    if lines.shards == 4:
        early_sent = lines.scatter_add(out_parts[3], out_parts[4], early_far)
        d_heads, g_gate_part, *early_sent = tied(d_heads, g_gate_part, *early_sent)
    g_gate_sent, g_out_t = tied(g_gate_part, g_out_t)
    g_gate = row_scatter(g_gate_sent)

    d_value, d_states, d_steps, g_conv, g_decay = run_backward(
        lines.seat, pre, widened(d_heads, wide), states, steps, held, taps, rate, skip, pick, lines.shards
    )
    state_parts = lines.split_states(d_states)
    normal_in, *state_parts = tied(normal_in, *state_parts)
    g_value_part = weight_grad(normal_in, d_value)
    g_value_sent, g_gate = tied(g_value_part, g_gate)
    g_value = row_scatter(g_value_sent)
    d_state_local, g_value_part = tied(lines.scatter_states(state_parts), g_value_part)
    d_bc_pre, g_conv_bc, g_conv_bc_bias = state_back(d_state_local)
    d_step = d_steps[:, :heads] * sigmoid(step_sum)
    small = lines.settle(widened(jnp.concatenate([d_bc_pre, d_step], axis=1), LANES)).astype(BF16)
    small, d_value, g_value_part = tied(small, d_value, g_value_part)
    parts = (
        g_conv[:4, :channels],
        g_conv[4, :channels],
        g_conv_bc,
        g_conv_bc_bias,
        jnp.sum(d_step, axis=0),
        (g_decay * rate)[0, :heads],
        jnp.sum(g_conv[5, :channels].reshape(heads, P_SIZE), axis=1),
        g_norm_gain,
    )
    if lines.shards == 4:
        row_parts = {}
        turn = d_value
        for name, blocks in (("rows_far", (6, 7)), ("rows_near", (2, 5)), ("rows_next", (3, 4)), ("rows_own", (0, 1))):
            row_parts[name] = run_rows(blocks, d_gate, turn, small, w_gate_full, w_cat, piece_rows // 2, 512)
            turn, *row_parts[name] = tied(turn, *row_parts[name])
            if name == "rows_far":
                far_came = lines.scatter_far(*row_parts[name])
            elif name == "rows_near":
                near_came = lines.scatter_near(*row_parts[name])
            elif name == "rows_next":
                sent = lines.scatter_add(*row_parts[name], far_came)
                turn, *sent = tied(turn, *sent)
        own = row_parts["rows_own"]
        own[0], normal_in, g_gate_part, g_value_part, *early_near = tied(
            own[0], normal_in, g_gate_part, g_value_part, *early_near
        )
        d_rows = lines.scatter_end(sent, own, near_came)
        branch_out = lines.scatter_end(early_sent, out_parts[:2], early_near)
    else:
        d_cat = jnp.concatenate([d_value, small], axis=1)
        d_rows = lines.scatter_whole((nt_dot(d_gate, w_gate_full) + nt_dot(d_cat, w_cat)).astype(BF16))
    result = (hidden.astype(F32) + branch_out).astype(BF16)
    g_small_part = tn_dot(normal_in, small)
    g_small = row_scatter_small(g_small_part)
    tokens = hidden.astype(F32)
    scale = lax.rsqrt(jnp.mean(tokens * tokens, axis=1, keepdims=True) + EPSILON)
    scaled_rows = d_rows * full_gain
    grad_hidden = grad_out.astype(F32) + scale * (
        scaled_rows - tokens * (scale * scale * jnp.mean(tokens * scaled_rows, axis=1, keepdims=True))
    )

    g_in_gain = gain_sums(w_gate_full, g_gate_part, w_cat, g_value_part, g_small_part) / full_gain
    packed = row_sum(jnp.concatenate([part.reshape(-1) for part in parts] + [g_in_gain]))
    summed = []
    at = 0
    for part in parts:
        summed.append(packed[at : at + part.size].reshape(part.shape))
        at += part.size
    g_in_gain = lines.own_slice(lines.total(packed[at:]))
    return (
        result,
        grad_hidden,
        g_in_gain,
        g_gate.astype(F32),
        g_value[:, :channels].astype(F32),
        g_small[:, :bc_width],
        g_small[:, bc_width : bc_width + heads],
        *summed,
        g_out_t.T.astype(F32),
    )


def gain_sums(w_gate, g_gate, w_cat, g_value, g_small):
    wide = g_value.shape[1]
    return (
        jnp.sum(w_gate.astype(F32) * g_gate.astype(F32), axis=1)
        + jnp.sum(w_cat[:, :wide].astype(F32) * g_value.astype(F32), axis=1)
        + jnp.sum(w_cat[:, wide:].astype(F32) * g_small, axis=1)
    )


def solution(mesh):
    over_tokens = P(("row", "col"), None)
    square = P("row", "col")
    across = P(None, "col")
    vector = P("col")
    return jax.shard_map(
        body,
        mesh=mesh,
        in_specs=(
            over_tokens, vector, square, square, square, square, across, vector, across, vector,
            vector, vector, vector, vector, P("col", "row"), over_tokens,
        ),
        out_specs=(
            over_tokens, over_tokens, vector, square, square, square, square, across, vector, across,
            vector, vector, vector, vector, vector, P("col", "row"),
        ),
        check_vma=False,
    )
```

```python
import functools
import jax
import jax.numpy as jnp
from jax import lax
from jax.experimental import pallas as pl
from jax.experimental.pallas import tpu as pltpu
from jax.sharding import PartitionSpec as P


P_SIZE = 64
N = 128
Q = 128
LANES = 128
NEG = -1e30
HIGH = lax.Precision.HIGHEST
F32 = jnp.float32
BF16 = jnp.bfloat16


def sigmoid(v):
    return 0.5 * jnp.tanh(0.5 * v) + 0.5


def nt_dot(a, b):
    return lax.dot_general(a, b, (((1,), (1,)), ((), ())), preferred_element_type=F32)


def mm(a, b):
    return jnp.dot(a, b, preferred_element_type=F32)


def mm_exact(a, b):
    return jnp.dot(a, b, precision=HIGH, preferred_element_type=F32)


def turned(m):
    return m.astype(F32).T.astype(BF16)


def pair_cols(low_half, cols, first):
    return jnp.where(low_half, cols[:, first : first + 1], cols[:, first + 1 : first + 2])


def halves(low_half, v):
    zero = jnp.zeros_like(v)
    return jnp.concatenate([jnp.where(low_half, v, zero), jnp.where(low_half, zero, v)], axis=0)


def shifts(first_row, count, step):
    rows = lax.broadcasted_iota(jnp.int32, (count * Q, Q + 16), 0)
    lanes = lax.broadcasted_iota(jnp.int32, (count * Q, Q + 16), 1)
    part = lax.div(rows, Q)
    return (lanes == first_row + step * part + lax.rem(rows, Q)).astype(F32).astype(BF16)


def open_chunk(taps_ref, back_ref, prior, vp_ref, cols):
    now = vp_ref[:, cols]
    moved = mm(back_ref[...], jnp.concatenate([prior[:, cols], now], axis=0))
    seen = [moved[k * Q : (k + 1) * Q] for k in range(3)] + [now.astype(F32)]
    half = taps_ref[4:5, cols] + taps_ref[0:1, cols] * seen[0]
    for k in range(1, 4):
        half = half + taps_ref[k : k + 1, cols] * seen[k]
    return seen, half, jnp.tanh(half)


def scan_forward(
    seat_ref, vp_ref, bc_ref, st_ref, taps_ref, rate_ref, skip_ref,
    y_ref, hold_ref, state, halo, shut, *, pairs
):
    rows = lax.broadcasted_iota(jnp.int32, (Q, Q), 0)
    lanes = lax.broadcasted_iota(jnp.int32, (Q, Q), 1)

    @pl.when(pl.program_id(0) == 0)
    def _():
        state[...] = jnp.zeros_like(state)
        halo[0:8, :] = jnp.zeros_like(halo[0:8, :])
        shut[...] = jnp.where(rows >= lanes, 0.0, NEG)

    halo[8 : 8 + Q, :] = vp_ref[...].astype(F32)
    low_half = lanes < P_SIZE
    steps = st_ref[...]
    lam = mm_exact((rows >= lanes).astype(F32), steps * rate_ref[...])
    source_t = (lam - jnp.log(steps)).T
    grown = jnp.exp(lam)
    last = lam[Q - 1 : Q, :]
    weight = jnp.exp(last - lam) * steps
    fade = jnp.exp(last)
    b_rows = bc_ref[:, :N]
    c_rows = bc_ref[:, N:]
    b_t = turned(b_rows)
    scores = nt_dot(c_rows, b_rows)
    for pair in range(pairs):
        cols = slice(pair * LANES, (pair + 1) * LANES)
        first = 2 * pair
        half = taps_ref[4:5, cols] + taps_ref[0:1, cols] * halo[5 : 5 + Q, cols]
        for k in range(1, 4):
            half = half + taps_ref[k : k + 1, cols] * halo[5 + k : 5 + k + Q, cols]
        x = half * jnp.tanh(half) + half
        mixing = []
        for h in (first, first + 1):
            gap = lam[:, h : h + 1] - source_t[h : h + 1, :] + shut[...]
            mixing.append((scores * jnp.exp(gap)).astype(BF16))
        y = mm(jnp.concatenate(mixing, axis=1), halves(low_half, x).astype(BF16))
        held = state[:, cols]
        held_low = held.astype(BF16)
        y = y + mm(c_rows, held_low) * pair_cols(low_half, grown, first)
        y = y + skip_ref[:, cols] * x
        y_ref[:, cols] = y.astype(y_ref.dtype)
        hold_ref[0, :, cols] = held_low
        fed = (x * pair_cols(low_half, weight, first)).astype(BF16)
        state[:, cols] = held * pair_cols(low_half[0:1], fade, first) + mm(b_t, fed)
    halo[0:8, :] = halo[Q : Q + 8, :]


def scan_backward(
    seat_ref, vp_ref, before_ref, dy_ref, bc_ref, st_ref, hold_ref, taps_ref, rate_ref, skip_ref, pick_ref,
    dvp_ref, dbc_ref, dst_ref, gconv_ref, gdecay_ref,
    prior, g_next, back, ahead, shut, ds, ds_low, across, w_cols, w_rows, state_terms, inter_terms, fed_all, dyl_all,
    e_rows, *, pairs, blocks
):
    step_id = pl.program_id(0)
    rows = lax.broadcasted_iota(jnp.int32, (Q, Q), 0)
    lanes = lax.broadcasted_iota(jnp.int32, (Q, Q), 1)

    @pl.when(step_id == 0)
    def _():
        ds[...] = jnp.zeros_like(ds)
        g_next[...] = jnp.zeros_like(g_next)
        gconv_ref[...] = jnp.zeros_like(gconv_ref)
        gdecay_ref[...] = jnp.zeros_like(gdecay_ref)
        w_cols[...] = jnp.zeros_like(w_cols)
        w_rows[...] = jnp.zeros_like(w_rows)
        e_rows[...] = jnp.zeros_like(e_rows)
        back[...] = shifts(13, 3, 1)
        ahead[...] = shifts(1, 3, 1)
        shut[...] = jnp.where(lanes >= rows, 0.0, NEG)

    @pl.when(step_id < blocks - 1)
    def _():
        prior[...] = before_ref[...]

    @pl.when(step_id == blocks - 1)
    def _():
        prior[...] = jnp.zeros_like(prior)

    low_half = lanes < P_SIZE
    steps = st_ref[...]
    rate = rate_ref[...]
    lam = mm_exact((rows >= lanes).astype(F32), steps * rate)
    lam_t = lam.T
    source = lam - jnp.log(steps)
    grown = jnp.exp(lam)
    last = lam[Q - 1 : Q, :]
    weight = jnp.exp(last - lam) * steps
    fade = jnp.exp(last)
    b_rows = bc_ref[:, :N]
    c_rows = bc_ref[:, N:]
    c_t = turned(c_rows)
    scores_t = nt_dot(b_rows, c_rows)
    for pair in range(pairs):
        cols = slice(pair * LANES, (pair + 1) * LANES)
        first = 2 * pair
        seen, half, bend = open_chunk(taps_ref, back, prior, vp_ref, cols)
        x = half * bend + half
        dy = dy_ref[:, cols]
        dy_wide = dy.astype(F32)
        q_t = nt_dot(halves(low_half, x).astype(BF16), dy)
        mixing = []
        crossed = None
        for at, h in enumerate((first, first + 1)):
            decay = jnp.exp(lam_t[h : h + 1, :] - source[:, h : h + 1] + shut[...])
            stepped = decay * q_t[at * Q : (at + 1) * Q]
            crossed = stepped if crossed is None else crossed + stepped
            both = stepped * scores_t
            w_cols[:, h : h + 1] = jnp.sum(both, axis=1, keepdims=True)
            w_rows[h : h + 1, :] = jnp.sum(both, axis=0, keepdims=True)
            mixing.append((decay * scores_t).astype(BF16))
        if pair == 0:
            across[...] = crossed
        else:
            across[...] += crossed
        dx = mm(jnp.concatenate(mixing, axis=1), halves(low_half, dy_wide).astype(BF16))
        d_state = ds[:, cols]
        d_state_low = d_state.astype(BF16)
        ds_low[:, cols] = d_state_low
        weight_pair = pair_cols(low_half, weight, first)
        carried = weight_pair * mm(b_rows, d_state_low)
        dx = dx + carried + skip_ref[:, cols] * dy_wide
        state_terms[:, cols] = (x * carried).astype(BF16)
        fed_all[:, cols] = (x * weight_pair).astype(BF16)
        held = hold_ref[0, :, cols]
        dyl = dy_wide * pair_cols(low_half, grown, first)
        dyl_low = dyl.astype(BF16)
        dyl_all[:, cols] = dyl_low
        inter_terms[:, cols] = (dyl * mm(c_rows, held)).astype(BF16)
        e_rows[0:1, cols] = jnp.sum(d_state * held.astype(F32), axis=0, keepdims=True)
        ds[:, cols] = d_state * pair_cols(low_half[0:1], fade, first) + mm(c_t, dyl_low)
        g = dx * ((0.5 + 0.5 * bend) * (1.0 + half * (1.0 - bend)))
        for k in range(4):
            gconv_ref[k : k + 1, cols] += jnp.sum(g * seen[k], axis=0, keepdims=True)
        gconv_ref[4:5, cols] += jnp.sum(g, axis=0, keepdims=True)
        gconv_ref[5:6, cols] += jnp.sum(dy_wide * x, axis=0, keepdims=True)
        g_low = g.astype(BF16)
        moved = mm(ahead[...], jnp.concatenate([g_low, g_next[:, cols]], axis=0))
        d_pre = taps_ref[3:4, cols] * g
        for k in range(3):
            d_pre = d_pre + taps_ref[2 - k : 3 - k, cols] * moved[k * Q : (k + 1) * Q]
        dvp_ref[:, cols] = (2.0 * d_pre).astype(dvp_ref.dtype)
        g_next[:, cols] = g_low[0:16]
    cross = across[...]
    d_b = mm(cross.astype(BF16), c_rows) + nt_dot(fed_all[...], ds_low[...])
    d_c = mm(turned(cross), b_rows) + nt_dot(dyl_all[...], hold_ref[0])
    dbc_ref[:, :N] = d_b.astype(dbc_ref.dtype)
    dbc_ref[:, N:] = d_c.astype(dbc_ref.dtype)
    pick = pick_ref[...]
    from_state = mm(state_terms[...], pick)
    from_carry = mm(inter_terms[...], pick)
    e_high = e_rows[...].astype(BF16)
    e_rest = (e_rows[...] - e_high.astype(F32)).astype(BF16)
    through = (mm(e_high, pick) + mm(e_rest, pick))[0:1]
    w_all = w_cols[...]
    d_lam = w_rows[...].T - w_all + from_carry
    d_log = (
        mm_exact((lanes >= rows).astype(F32), d_lam)
        + mm_exact((rows > lanes).astype(F32), from_state)
        + fade * through
    )
    dst_ref[...] = (w_all + from_state) / jnp.maximum(steps, 1e-37) + rate * d_log
    gdecay_ref[...] += jnp.sum(steps * d_log, axis=0, keepdims=True)


def chunk_of(i, seat, per):
    return (lax.div(i, per) ^ seat[0]) * per + lax.rem(i, per)


def run_forward(seat, pre, states_in, steps, taps, rate, skip, shards):
    tokens = steps.shape[0]
    width = taps.shape[1]
    blocks = tokens // Q
    per = blocks // shards
    fixed = lambda i, seat: (0, 0)
    plain = lambda i, seat: (i, 0)
    moved = lambda i, seat: (chunk_of(i, seat, per), 0)
    return pl.pallas_call(
        functools.partial(scan_forward, pairs=width // LANES),
        out_shape=(
            jax.ShapeDtypeStruct((tokens, width), BF16),
            jax.ShapeDtypeStruct((blocks, N, width), BF16),
        ),
        grid_spec=pltpu.PrefetchScalarGridSpec(
            num_scalar_prefetch=1,
            grid=(blocks,),
            in_specs=[
                pl.BlockSpec((Q, width), moved),
                pl.BlockSpec((Q, 2 * N), plain),
                pl.BlockSpec((Q, LANES), plain),
                pl.BlockSpec((8, width), fixed),
                pl.BlockSpec((1, LANES), fixed),
                pl.BlockSpec((1, width), fixed),
            ],
            out_specs=[
                pl.BlockSpec((Q, width), moved),
                pl.BlockSpec((1, N, width), lambda i, seat: (i, 0, 0)),
            ],
            scratch_shapes=[
                pltpu.VMEM((N, width), F32),
                pltpu.VMEM((Q + 8, width), F32),
                pltpu.VMEM((Q, Q), F32),
            ],
        ),
        cost_estimate=pl.CostEstimate(
            flops=tokens * width * 1200, bytes_accessed=tokens * width * 10, transcendentals=tokens * width * 3
        ),
        name="scan_forward",
    )(seat, pre, states_in, steps, taps, rate, skip)


def run_backward(seat, pre, dy, states_in, steps, held, taps, rate, skip, pick, shards):
    tokens = steps.shape[0]
    width = taps.shape[1]
    blocks = tokens // Q
    per = blocks // shards
    fixed = lambda i, seat: (0, 0)
    plain = lambda i, seat: (blocks - 1 - i, 0)
    moved = lambda i, seat: (chunk_of(blocks - 1 - i, seat, per), 0)

    def before(i, seat):
        chunk = jnp.maximum(blocks - 2 - i, 0)
        return (chunk_of(chunk, seat, per) * (Q // 16) + Q // 16 - 1, 0)

    return pl.pallas_call(
        functools.partial(scan_backward, pairs=width // LANES, blocks=blocks),
        out_shape=(
            jax.ShapeDtypeStruct((tokens, width), BF16),
            jax.ShapeDtypeStruct((tokens, 2 * N), BF16),
            jax.ShapeDtypeStruct((tokens, LANES), F32),
            jax.ShapeDtypeStruct((8, width), F32),
            jax.ShapeDtypeStruct((1, LANES), F32),
        ),
        grid_spec=pltpu.PrefetchScalarGridSpec(
            num_scalar_prefetch=1,
            grid=(blocks,),
            in_specs=[
                pl.BlockSpec((Q, width), moved),
                pl.BlockSpec((16, width), before),
                pl.BlockSpec((Q, width), moved),
                pl.BlockSpec((Q, 2 * N), plain),
                pl.BlockSpec((Q, LANES), plain),
                pl.BlockSpec((1, N, width), lambda i, seat: (blocks - 1 - i, 0, 0)),
                pl.BlockSpec((8, width), fixed),
                pl.BlockSpec((1, LANES), fixed),
                pl.BlockSpec((1, width), fixed),
                pl.BlockSpec((width, LANES), fixed),
            ],
            out_specs=[
                pl.BlockSpec((Q, width), moved),
                pl.BlockSpec((Q, 2 * N), plain),
                pl.BlockSpec((Q, LANES), plain),
                pl.BlockSpec((8, width), fixed),
                pl.BlockSpec((1, LANES), fixed),
            ],
            scratch_shapes=[
                pltpu.VMEM((16, width), BF16),
                pltpu.VMEM((16, width), BF16),
                pltpu.VMEM((3 * Q, Q + 16), BF16),
                pltpu.VMEM((3 * Q, Q + 16), BF16),
                pltpu.VMEM((Q, Q), F32),
                pltpu.VMEM((N, width), F32),
                pltpu.VMEM((N, width), BF16),
                pltpu.VMEM((Q, Q), F32),
                pltpu.VMEM((Q, LANES), F32),
                pltpu.VMEM((LANES, Q), F32),
                pltpu.VMEM((Q, width), BF16),
                pltpu.VMEM((Q, width), BF16),
                pltpu.VMEM((Q, width), BF16),
                pltpu.VMEM((Q, width), BF16),
                pltpu.VMEM((8, width), F32),
            ],
        ),
        cost_estimate=pl.CostEstimate(
            flops=tokens * width * 3000, bytes_accessed=tokens * width * 14, transcendentals=tokens * width * 4
        ),
        name="scan_backward",
    )(seat, pre, pre, dy, states_in, steps, held, taps, rate, skip, pick)


EPSILON = 1e-05


def swish(v):
    return v * sigmoid(v)


def tn_dot(a, b):
    return lax.dot_general(a, b, (((0,), (0,)), ((), ())), preferred_element_type=F32)


def fill_kernel(*refs, spans):
    gain_ref, w_ref = refs[len(spans) : len(spans) + 2]
    normal_ref, value_ref, small_ref = refs[-3:]
    step_id = pl.program_id(0)
    wide = value_ref.shape[1]
    for (start, stop), piece_ref in zip(spans, refs):

        @pl.when((step_id >= start) & (step_id < stop))
        def _(piece_ref=piece_ref):
            rows = piece_ref[...].astype(F32)
            scale = lax.rsqrt(jnp.mean(rows * rows, axis=1, keepdims=True) + EPSILON)
            normal_ref[...] = (rows * scale * gain_ref[...]).astype(BF16)

    small_ref[...] = mm(normal_ref[...], w_ref[:, wide:])
    value_ref[...] = mm(normal_ref[...], w_ref[:, :wide]).astype(BF16)


def run_fill(pieces, gain, w, into, rows, first, block):
    depth, width = w.shape
    wide = width - LANES
    place = lambda i: (i + first, 0)
    spans = []
    specs = []
    at = 0
    for piece in pieces:
        blocks = piece.shape[0] // block
        spans.append((at, at + blocks))
        specs.append(pl.BlockSpec((block, depth), lambda i, at=at, blocks=blocks: (jnp.clip(i - at, 0, blocks - 1), 0)))
        at += blocks
    return pl.pallas_call(
        functools.partial(fill_kernel, spans=spans),
        out_shape=(
            jax.ShapeDtypeStruct((rows, depth), BF16),
            jax.ShapeDtypeStruct((rows, wide), BF16),
            jax.ShapeDtypeStruct((rows, LANES), F32),
        ),
        grid=(at,),
        in_specs=specs
        + [
            pl.BlockSpec((1, depth), lambda i: (0, 0)),
            pl.BlockSpec((depth, width), lambda i: (0, 0), pipeline_mode=pl.Buffered(1)),
        ]
        + [pl.BlockSpec(memory_space=pl.ANY)] * len(into),
        out_specs=(
            pl.BlockSpec((block, depth), place), pl.BlockSpec((block, wide), place), pl.BlockSpec((block, LANES), place)
        ),
        input_output_aliases={len(pieces) + 2 + k: k for k in range(len(into))},
        cost_estimate=pl.CostEstimate(
            flops=2 * at * block * depth * width,
            bytes_accessed=2 * (at * block + width) * (depth + width),
            transcendentals=0,
        ),
        name="values",
    )(*pieces, gain, w, *into)


def split_kernel(x_ref, w_ref, *out_refs):
    rows = out_refs[0].shape[0]
    for at, out_ref in enumerate(out_refs):
        out_ref[...] = nt_dot(x_ref[at * rows : (at + 1) * rows], w_ref[...]).astype(BF16)


def run_split(x, w, parts, block):
    tokens, depth = x.shape
    width = w.shape[0]
    rows = tokens // parts
    return pl.pallas_call(
        split_kernel,
        out_shape=[jax.ShapeDtypeStruct((rows, width), BF16)] * parts,
        grid=(width // block,),
        in_specs=[
            pl.BlockSpec((tokens, depth), lambda i: (0, 0), pipeline_mode=pl.Buffered(1)),
            pl.BlockSpec((block, depth), lambda i: (i, 0)),
        ],
        out_specs=[pl.BlockSpec((rows, block), lambda i: (0, i))] * parts,
        cost_estimate=pl.CostEstimate(
            flops=2 * tokens * depth * width, bytes_accessed=2 * (tokens + width) * depth + 2 * tokens * width, transcendentals=0
        ),
        name="split",
    )(x, w)


def rows_kernel(*refs):
    w_gate_ref, w_cat_ref = refs[6:8]
    wide = refs[2].shape[1]
    for at in range(2):
        gate_ref, value_ref, small_ref = refs[at:6:2]
        total = nt_dot(gate_ref[...], w_gate_ref[...])
        total = total + nt_dot(value_ref[...], w_cat_ref[:, :wide])
        total = total + nt_dot(small_ref[...], w_cat_ref[:, wide:])
        refs[8 + at][...] = total.astype(BF16)


def run_rows(blocks, d_gate, d_value, d_small, w_gate, w_cat, rows, block):
    width = w_gate.shape[0]
    depth = w_gate.shape[1] + w_cat.shape[1]
    given = [v for v in (d_gate, d_value, d_small) for _ in blocks]
    specs = [
        pl.BlockSpec((rows, v.shape[1]), lambda i, at=at: (at, 0), pipeline_mode=pl.Buffered(1))
        for v in (d_gate, d_value, d_small)
        for at in blocks
    ]
    return pl.pallas_call(
        rows_kernel,
        out_shape=[jax.ShapeDtypeStruct((rows, width), BF16)] * 2,
        grid=(width // block,),
        in_specs=specs
        + [
            pl.BlockSpec((block, w_gate.shape[1]), lambda i: (i, 0)),
            pl.BlockSpec((block, w_cat.shape[1]), lambda i: (i, 0)),
        ],
        out_specs=[pl.BlockSpec((rows, block), lambda i: (0, i))] * 2,
        cost_estimate=pl.CostEstimate(
            flops=4 * rows * depth * width, bytes_accessed=2 * (2 * rows + width) * depth + 4 * rows * width, transcendentals=0
        ),
        name="rows",
    )(*given, w_gate, w_cat)


def turned_kernel(a_ref, b_ref, out_ref):
    out_ref[...] = tn_dot(a_ref[...], b_ref[...]).astype(BF16)


def run_turned(a, b, block):
    tokens, depth = a.shape
    width = b.shape[1]
    return pl.pallas_call(
        turned_kernel,
        out_shape=jax.ShapeDtypeStruct((depth, width), BF16),
        grid=(depth // block,),
        in_specs=[
            pl.BlockSpec((tokens, block), lambda i: (0, i)),
            pl.BlockSpec((tokens, width), lambda i: (0, 0), pipeline_mode=pl.Buffered(1)),
        ],
        out_specs=pl.BlockSpec((block, width), lambda i: (i, 0)),
        cost_estimate=pl.CostEstimate(
            flops=2 * tokens * depth * width, bytes_accessed=2 * (tokens * (depth + width) + depth * width), transcendentals=0
        ),
        name="weights",
    )(a, b)


def joined_kernel(*refs):
    b_ref, out_ref, full_ref = refs[-3:]
    at = 0
    for piece_ref in refs[:-3]:
        rows = piece_ref.shape[0]
        full_ref[at : at + rows] = piece_ref[...]
        at += rows
    out_ref[...] = tn_dot(full_ref[...], b_ref[...]).astype(BF16)


def run_joined(pieces, b, block):
    tokens, width = b.shape
    depth = pieces[0].shape[1]
    return pl.pallas_call(
        joined_kernel,
        out_shape=(jax.ShapeDtypeStruct((depth, width), BF16), jax.ShapeDtypeStruct((tokens, depth), BF16)),
        grid=(depth // block,),
        in_specs=[pl.BlockSpec((piece.shape[0], block), lambda i: (0, i)) for piece in pieces]
        + [pl.BlockSpec((tokens, width), lambda i: (0, 0), pipeline_mode=pl.Buffered(1))],
        out_specs=(pl.BlockSpec((block, width), lambda i: (i, 0)), pl.BlockSpec((tokens, block), lambda i: (0, i))),
        cost_estimate=pl.CostEstimate(
            flops=2 * tokens * depth * width, bytes_accessed=2 * (tokens * (2 * depth + width) + depth * width), transcendentals=0
        ),
        name="joined",
    )(*pieces, b)


def causal_conv(values, taps, offsets):
    tap_count = taps.shape[0]
    length = values.shape[0]
    padded = jnp.pad(values, ((tap_count - 1, 0), (0, 0)))
    summed = offsets[None, :] + taps[0][None, :] * padded[0:length]
    for offset in range(1, tap_count):
        summed = summed + taps[offset][None, :] * padded[offset : offset + length]
    return summed


def swap(v, bit, axis="col"):
    size = lax.axis_size(axis)
    return lax.ppermute(v, axis, [(i, i ^ bit) for i in range(size)])


def row_sum(v):
    bit = 1
    while bit < lax.axis_size("row"):
        v = v + swap(v, bit, "row")
        bit *= 2
    return v


class Square:
    shards = 4

    def __init__(self):
        self.place = lax.axis_index("col")
        self.x = lax.rem(self.place, 2) == 1
        self.y = lax.div(self.place, 2) == 1
        self.seat = jnp.reshape(self.place, (1,)).astype(jnp.int32)

    def settle(self, v):
        parts = v.reshape((2, 2, v.shape[0] // 4) + v.shape[1:])
        parts = jnp.where(self.y, parts[::-1], parts)
        parts = jnp.where(self.x, parts[:, ::-1], parts)
        return parts.reshape(v.shape)

    def gather_whole(self, v):
        from_x, from_y = swap(v, 1), swap(v, 2)
        half = v.shape[0] // 2
        relay_y = swap(from_x[:half], 2)
        relay_x = swap(from_y[half:], 1)
        return [v, from_x, from_y, relay_y, relay_x]

    def gather_top(self, v):
        first, rest = v[: v.shape[0] // 4], v[v.shape[0] // 4 :]
        return [v, rest, swap(first, 1), swap(first, 2)]

    def gather_low(self, parts):
        v, rest, x_first, y_first = parts
        quarter = x_first.shape[0]
        x_rest, y_rest = swap(rest, 1), swap(rest, 2)
        far_first = swap(y_first, 1)
        far_middle = swap(x_rest[: 2 * quarter], 2)
        far_last = swap(y_rest[2 * quarter :], 1)
        return [v, x_first, x_rest, y_first, y_rest, far_first, far_middle, far_last]

    def gather_flat(self, v):
        others = [swap(v, bit) for bit in (1, 2, 3)]
        return self.settle(jnp.concatenate([v] + others))

    def token_sum(self, v):
        parts = v.reshape(2, 2, -1)
        parts = parts + swap(parts, 1)[:, ::-1]
        parts = parts + swap(parts, 2)[::-1]
        return parts.reshape(v.shape)

    def total(self, v):
        v = v + swap(v, 1)
        return v + swap(v, 2)

    def scatter_far(self, far_top, far_low):
        return swap(far_top, 1), swap(far_low, 2)

    def scatter_near(self, x_top, y_low):
        return swap(x_top, 1), swap(y_low, 2)

    def scatter_add(self, x_low, y_top, far_came):
        across_x, across_y = far_came
        return [
            (x_low.astype(F32) + across_y.astype(F32)).astype(BF16),
            (y_top.astype(F32) + across_x.astype(F32)).astype(BF16),
        ]

    def scatter_end(self, sent, own, near_came):
        x_low, y_top = swap(sent[0], 1), swap(sent[1], 2)
        top, low, x_top, y_low = (v.astype(F32) for v in (*own, *near_came))
        return jnp.concatenate([top + x_top + y_top.astype(F32), low + x_low.astype(F32) + y_low])

    def dense_swap(self, v, bit):
        half, width = v.shape[0] // 2, v.shape[1]
        came = swap(jnp.concatenate([v[:half], v[half:]], axis=1), bit)
        return jnp.concatenate([came[:, :width], came[:, width:]])

    def gather_states(self, s):
        pair = jnp.concatenate([s, self.dense_swap(s, 1)], axis=1)
        other = jnp.concatenate([self.dense_swap(s, 2), self.dense_swap(s, 3)], axis=1)
        return jnp.concatenate([jnp.where(self.y, other, pair), jnp.where(self.y, pair, other)], axis=1)

    def split_states(self, d):
        first, second = d[:, :N], d[:, N:]
        kept = jnp.where(self.y, second, first)
        given = jnp.where(self.y, first, second)
        half = N // 2
        return [kept[:, :half], kept[:, half:], given[:, :half], given[:, half:]]

    def scatter_states(self, parts):
        own = parts[0].astype(F32)
        for bit in (1, 2, 3):
            own = own + self.dense_swap(parts[bit], bit).astype(F32)
        return own

    def own_slice(self, v):
        width = v.shape[0] // 4
        return lax.dynamic_slice(v, (self.place * width,), (width,))


class Line:
    shards = 1

    def __init__(self):
        self.seat = jnp.zeros((1,), jnp.int32)

    def settle(self, v):
        return v

    def gather_whole(self, v):
        return [lax.all_gather(v, "col", axis=0, tiled=True)]

    def gather_top(self, v):
        return self.gather_whole(v)

    def gather_low(self, parts):
        return parts

    def gather_flat(self, v):
        return lax.all_gather(v, "col", axis=0, tiled=True)

    def token_sum(self, v):
        return lax.psum(v, "col")

    def total(self, v):
        return lax.psum(v, "col")

    def scatter_whole(self, v):
        return lax.psum_scatter(v, "col", scatter_dimension=0, tiled=True).astype(F32)

    def gather_states(self, s):
        return lax.all_gather(s, "col", axis=1, tiled=True)

    def split_states(self, d):
        return [d]

    def scatter_states(self, parts):
        return lax.psum_scatter(parts[0].astype(BF16), "col", scatter_dimension=1, tiled=True).astype(F32)

    def own_slice(self, v):
        width = v.shape[0] // lax.axis_size("col")
        return lax.dynamic_slice(v, (lax.axis_index("col") * width,), (width,))


def widened(v, width):
    return v if v.shape[-1] == width else jnp.pad(v, [(0, 0)] * (v.ndim - 1) + [(0, width - v.shape[-1])])


def tied(*values):
    return lax.optimization_barrier(values)


def row_scatter_small(v):
    bit = lax.axis_size("row") // 2
    place = lax.axis_index("row")
    while bit:
        half = v.shape[0] // 2
        upper = lax.rem(lax.div(place, bit), 2) == 1
        kept = jnp.where(upper, v[half:], v[:half])
        given = jnp.where(upper, v[:half], v[half:])
        v = kept + swap(given.astype(BF16), bit, "row").astype(F32)
        bit //= 2
    return v


def row_scatter(v):
    return lax.psum_scatter(v, "row", scatter_dimension=0, tiled=True)


def body(
    hidden,
    in_gain,
    w_gate,
    w_value,
    w_bc,
    w_step,
    conv_value,
    conv_value_bias,
    conv_bc,
    conv_bc_bias,
    step_bias,
    decay_log,
    skip_gain,
    norm_gain,
    w_out,
    grad_out,
):
    lines = Square() if lax.axis_size("col") == 4 else Line()
    heads = step_bias.shape[0]
    channels = w_value.shape[1]
    inner_width = lax.axis_size("col") * channels
    bc_width = w_bc.shape[1]
    wide = -(-channels // LANES) * LANES
    full_width = wide + LANES
    piece_rows = hidden.shape[0]

    w_cat = lax.all_gather(
        widened(jnp.concatenate([widened(w_value, wide), w_bc, w_step], axis=1), full_width),
        "row", axis=0, tiled=True,
    )
    w_gate_full = lax.all_gather(w_gate, "row", axis=0, tiled=True)
    w_out_t = lax.all_gather(w_out.T, "row", axis=0, tiled=True)
    full_gain = lines.gather_flat(in_gain).astype(F32)

    def weight_grad(a, b):
        return run_turned(a, b, 256) if lines.shards == 4 else tn_dot(a, b).astype(BF16)

    def normalized(rows):
        rows = rows.astype(F32)
        scale = lax.rsqrt(jnp.mean(rows * rows, axis=1, keepdims=True) + EPSILON)
        return (rows * scale * full_gain).astype(BF16)

    hidden_pieces = lines.gather_whole(hidden)
    grad_source, hidden_pieces[-1] = tied(grad_out, hidden_pieces[-1])
    grad_pieces = lines.gather_top(grad_source)
    near, far = hidden_pieces[:3], hidden_pieces[3:]

    if far:
        tokens_here = 4 * piece_rows
        half_rows = piece_rows // 2
        filled = run_fill(near, full_gain[None], w_cat, (), tokens_here, 0, half_rows)
        filled = run_fill(far, full_gain[None], w_cat, filled, tokens_here, 6, half_rows)
        normal_in, pre, pre_small = filled
    else:
        normal_in = normalized(near[0])
        pre = mm(normal_in, w_cat[:, :wide]).astype(BF16)
        pre_small = mm(normal_in, w_cat[:, wide:])
    bc_pre = lines.settle(pre_small[:, :bc_width])
    step_sum = lines.settle(pre_small[:, bc_width : bc_width + heads]) + step_bias

    def state_branch(pre_vals, conv_weight, conv_offset):
        return swish(causal_conv(pre_vals, conv_weight, conv_offset))

    state_local, state_back = jax.vjp(state_branch, bc_pre, conv_bc, conv_bc_bias)
    states = lines.gather_states(state_local.astype(BF16))
    steps = widened(jax.nn.softplus(step_sum), LANES)
    rate = widened(-jnp.exp(decay_log), LANES)[None]
    skip = widened(jnp.repeat(skip_gain, P_SIZE), wide)[None]
    taps = 0.5 * jnp.concatenate([conv_value, conv_value_bias[None], jnp.zeros((3, channels), F32)])
    taps = widened(taps, wide)
    pick = (jnp.arange(wide)[:, None] // P_SIZE == jnp.arange(LANES)[None]).astype(BF16)
    states, *grad_pieces[:2] = tied(states, *grad_pieces[:2])
    grad_pieces = lines.gather_low(grad_pieces)
    heads_out, held = run_forward(lines.seat, pre, states, steps, taps, rate, skip, lines.shards)

    gate_pre = mm(normal_in, w_gate_full).astype(BF16)
    ho = heads_out[:, :channels].astype(F32)
    gate = gate_pre.astype(F32)
    gated = ho * swish(gate)
    squares = jnp.sum(gated * gated, axis=1)
    squares = lines.token_sum(squares)
    mix = lax.rsqrt(squares / inner_width + EPSILON)[:, None]
    normed = (gated * mix * norm_gain).astype(BF16)

    if lines.shards == 4:
        g_out_part, grad_full = run_joined(grad_pieces, normed, 256)
    else:
        grad_full = grad_pieces[0]
        g_out_part = weight_grad(grad_full, normed)
    w_out_t, g_out_part = tied(w_out_t, g_out_part)
    g_out_t = row_scatter(g_out_part)
    d_normed = mm(grad_full, w_out_t).astype(BF16).astype(F32)
    scaled = d_normed * norm_gain
    dots = jnp.sum(gated * scaled, axis=1)
    w_out_t, dots = tied(w_out_t, dots)
    if lines.shards == 4:
        out_parts = run_split(normed, w_out_t, 8, 512)
        early_far = lines.scatter_far(*out_parts[6:])
        early_near = lines.scatter_near(out_parts[2], out_parts[5])
    else:
        branch_out = lines.scatter_whole(nt_dot(normed, w_out_t).astype(BF16))
    dots = lines.token_sum(dots)[:, None]
    d_gated = mix * scaled - gated * (mix * mix * mix * dots / inner_width)
    g_norm_gain = jnp.sum(d_normed * gated * mix, axis=0)
    open_gate = sigmoid(gate)
    d_heads = (d_gated * gate * open_gate).astype(BF16)
    d_gate = (d_gated * ho * (open_gate * (1.0 + gate * (1.0 - open_gate)))).astype(BF16)
    g_gate_part = weight_grad(normal_in, d_gate)
    if lines.shards == 4:
        early_sent = lines.scatter_add(out_parts[3], out_parts[4], early_far)
        d_heads, g_gate_part, *early_sent = tied(d_heads, g_gate_part, *early_sent)
    g_gate_sent, g_out_t = tied(g_gate_part, g_out_t)
    g_gate = row_scatter(g_gate_sent)

    d_value, d_states, d_steps, g_conv, g_decay = run_backward(
        lines.seat, pre, widened(d_heads, wide), states, steps, held, taps, rate, skip, pick, lines.shards
    )
    state_parts = lines.split_states(d_states)
    normal_in, *state_parts = tied(normal_in, *state_parts)
    g_value_part = weight_grad(normal_in, d_value)
    g_value_sent, g_gate = tied(g_value_part, g_gate)
    g_value = row_scatter(g_value_sent)
    d_state_local, g_value_part = tied(lines.scatter_states(state_parts), g_value_part)
    d_bc_pre, g_conv_bc, g_conv_bc_bias = state_back(d_state_local)
    d_step = d_steps[:, :heads] * sigmoid(step_sum)
    small = lines.settle(widened(jnp.concatenate([d_bc_pre, d_step], axis=1), LANES)).astype(BF16)
    small, d_value, g_value_part = tied(small, d_value, g_value_part)
    parts = (
        g_conv[:4, :channels],
        g_conv[4, :channels],
        g_conv_bc,
        g_conv_bc_bias,
        jnp.sum(d_step, axis=0),
        (g_decay * rate)[0, :heads],
        jnp.sum(g_conv[5, :channels].reshape(heads, P_SIZE), axis=1),
        g_norm_gain,
    )

    def small_and_gain(normal, from_gate, from_value):
        from_small = tn_dot(normal, small)
        return from_small, gain_sums(w_gate_full, from_gate, w_cat, from_value, from_small) / full_gain

    if lines.shards == 4:
        row_parts = {}
        turn = d_value
        for name, blocks in (("rows_far", (6, 7)), ("rows_near", (2, 5)), ("rows_next", (3, 4)), ("rows_own", (0, 1))):
            row_parts[name] = run_rows(blocks, d_gate, turn, small, w_gate_full, w_cat, piece_rows // 2, 512)
            turn, *row_parts[name] = tied(turn, *row_parts[name])
            if name == "rows_far":
                far_came = lines.scatter_far(*row_parts[name])
            elif name == "rows_near":
                near_came = lines.scatter_near(*row_parts[name])
                turn, normal_in, g_gate_part, g_value_part = tied(turn, normal_in, g_gate_part, g_value_part)
                g_small_part, g_in_gain = small_and_gain(normal_in, g_gate_part, g_value_part)
                turn, g_small_part, g_in_gain = tied(turn, g_small_part, g_in_gain)
            elif name == "rows_next":
                sent = lines.scatter_add(*row_parts[name], far_came)
                turn, g_small_part, g_in_gain, *sent = tied(turn, g_small_part, g_in_gain, *sent)
        own = row_parts["rows_own"]
        own[0], *early_near = tied(own[0], *early_near)
        d_rows = lines.scatter_end(sent, own, near_came)
        branch_out = lines.scatter_end(early_sent, out_parts[:2], early_near)
    else:
        g_small_part, g_in_gain = small_and_gain(normal_in, g_gate_part, g_value_part)
        d_cat = jnp.concatenate([d_value, small], axis=1)
        d_rows = lines.scatter_whole((nt_dot(d_gate, w_gate_full) + nt_dot(d_cat, w_cat)).astype(BF16))
    result = (hidden.astype(F32) + branch_out).astype(BF16)
    g_small = row_scatter_small(g_small_part)

    tokens = hidden.astype(F32)
    scale = lax.rsqrt(jnp.mean(tokens * tokens, axis=1, keepdims=True) + EPSILON)
    scaled_rows = d_rows * full_gain
    grad_hidden = grad_out.astype(F32) + scale * (
        scaled_rows - tokens * (scale * scale * jnp.mean(tokens * scaled_rows, axis=1, keepdims=True))
    )

    packed = row_sum(jnp.concatenate([part.reshape(-1) for part in parts] + [g_in_gain]))
    summed = []
    at = 0
    for part in parts:
        summed.append(packed[at : at + part.size].reshape(part.shape))
        at += part.size
    g_in_gain = lines.own_slice(lines.total(packed[at:]))
    return (
        result,
        grad_hidden,
        g_in_gain,
        g_gate.astype(F32),
        g_value[:, :channels].astype(F32),
        g_small[:, :bc_width],
        g_small[:, bc_width : bc_width + heads],
        *summed,
        g_out_t.T.astype(F32),
    )


def gain_sums(w_gate, g_gate, w_cat, g_value, g_small):
    wide = g_value.shape[1]
    return (
        jnp.sum(w_gate.astype(F32) * g_gate.astype(F32), axis=1)
        + jnp.sum(w_cat[:, :wide].astype(F32) * g_value.astype(F32), axis=1)
        + jnp.sum(w_cat[:, wide:].astype(F32) * g_small, axis=1)
    )


def solution(mesh):
    over_tokens = P(("row", "col"), None)
    square = P("row", "col")
    across = P(None, "col")
    vector = P("col")
    return jax.shard_map(
        body,
        mesh=mesh,
        in_specs=(
            over_tokens, vector, square, square, square, square, across, vector, across, vector,
            vector, vector, vector, vector, P("col", "row"), over_tokens,
        ),
        out_specs=(
            over_tokens, over_tokens, vector, square, square, square, square, across, vector, across,
            vector, vector, vector, vector, vector, P("col", "row"),
        ),
        check_vma=False,
    )
```

```python
import functools
import jax
import jax.numpy as jnp
from jax import lax
from jax.experimental import pallas as pl
from jax.experimental.pallas import tpu as pltpu
from jax.sharding import PartitionSpec as P


P_SIZE = 64
N = 128
Q = 128
LANES = 128
NEG = -1e30
HIGH = lax.Precision.HIGHEST
F32 = jnp.float32
BF16 = jnp.bfloat16


def sigmoid(v):
    return 0.5 * jnp.tanh(0.5 * v) + 0.5


def nt_dot(a, b):
    return lax.dot_general(a, b, (((1,), (1,)), ((), ())), preferred_element_type=F32)


def mm(a, b):
    return jnp.dot(a, b, preferred_element_type=F32)


def mm_exact(a, b):
    return jnp.dot(a, b, precision=HIGH, preferred_element_type=F32)


def turned(m):
    return m.astype(F32).T.astype(BF16)


def pair_cols(low_half, cols, first):
    return jnp.where(low_half, cols[:, first : first + 1], cols[:, first + 1 : first + 2])


def halves(low_half, v):
    zero = jnp.zeros_like(v)
    return jnp.concatenate([jnp.where(low_half, v, zero), jnp.where(low_half, zero, v)], axis=0)


def shifts(first_row, count, step):
    rows = lax.broadcasted_iota(jnp.int32, (count * Q, Q + 16), 0)
    lanes = lax.broadcasted_iota(jnp.int32, (count * Q, Q + 16), 1)
    part = lax.div(rows, Q)
    return (lanes == first_row + step * part + lax.rem(rows, Q)).astype(F32).astype(BF16)


def open_chunk(taps_ref, back_ref, prior, vp_ref, cols):
    now = vp_ref[:, cols]
    moved = mm(back_ref[...], jnp.concatenate([prior[:, cols], now], axis=0))
    seen = [moved[k * Q : (k + 1) * Q] for k in range(3)] + [now.astype(F32)]
    half = taps_ref[4:5, cols] + taps_ref[0:1, cols] * seen[0]
    for k in range(1, 4):
        half = half + taps_ref[k : k + 1, cols] * seen[k]
    return seen, half, jnp.tanh(half)


def scan_forward(
    seat_ref, vp_ref, bc_ref, st_ref, taps_ref, rate_ref, skip_ref,
    y_ref, hold_ref, state, halo, shut, *, pairs
):
    rows = lax.broadcasted_iota(jnp.int32, (Q, Q), 0)
    lanes = lax.broadcasted_iota(jnp.int32, (Q, Q), 1)

    @pl.when(pl.program_id(0) == 0)
    def _():
        state[...] = jnp.zeros_like(state)
        halo[0:8, :] = jnp.zeros_like(halo[0:8, :])
        shut[...] = jnp.where(rows >= lanes, 0.0, NEG)

    halo[8 : 8 + Q, :] = vp_ref[...].astype(F32)
    low_half = lanes < P_SIZE
    steps = st_ref[...]
    lam = mm_exact((rows >= lanes).astype(F32), steps * rate_ref[...])
    source_t = (lam - jnp.log(steps)).T
    grown = jnp.exp(lam)
    last = lam[Q - 1 : Q, :]
    weight = jnp.exp(last - lam) * steps
    fade = jnp.exp(last)
    b_rows = bc_ref[:, :N]
    c_rows = bc_ref[:, N:]
    b_t = turned(b_rows)
    scores = nt_dot(c_rows, b_rows)
    for pair in range(pairs):
        cols = slice(pair * LANES, (pair + 1) * LANES)
        first = 2 * pair
        half = taps_ref[4:5, cols] + taps_ref[0:1, cols] * halo[5 : 5 + Q, cols]
        for k in range(1, 4):
            half = half + taps_ref[k : k + 1, cols] * halo[5 + k : 5 + k + Q, cols]
        x = half * jnp.tanh(half) + half
        mixing = []
        for h in (first, first + 1):
            gap = lam[:, h : h + 1] - source_t[h : h + 1, :] + shut[...]
            mixing.append((scores * jnp.exp(gap)).astype(BF16))
        y = mm(jnp.concatenate(mixing, axis=1), halves(low_half, x).astype(BF16))
        held = state[:, cols]
        held_low = held.astype(BF16)
        y = y + mm(c_rows, held_low) * pair_cols(low_half, grown, first)
        y = y + skip_ref[:, cols] * x
        y_ref[:, cols] = y.astype(y_ref.dtype)
        hold_ref[0, :, cols] = held_low
        fed = (x * pair_cols(low_half, weight, first)).astype(BF16)
        state[:, cols] = held * pair_cols(low_half[0:1], fade, first) + mm(b_t, fed)
    halo[0:8, :] = halo[Q : Q + 8, :]


def scan_backward(
    seat_ref, vp_ref, before_ref, dy_ref, bc_ref, st_ref, hold_ref, taps_ref, rate_ref, skip_ref, pick_ref,
    dvp_ref, dbc_ref, dst_ref, gconv_ref, gdecay_ref,
    prior, g_next, back, ahead, shut, ds, ds_low, across, w_cols, w_rows, state_terms, inter_terms, fed_all, dyl_all,
    e_rows, *, pairs, blocks
):
    step_id = pl.program_id(0)
    rows = lax.broadcasted_iota(jnp.int32, (Q, Q), 0)
    lanes = lax.broadcasted_iota(jnp.int32, (Q, Q), 1)

    @pl.when(step_id == 0)
    def _():
        ds[...] = jnp.zeros_like(ds)
        g_next[...] = jnp.zeros_like(g_next)
        gconv_ref[...] = jnp.zeros_like(gconv_ref)
        gdecay_ref[...] = jnp.zeros_like(gdecay_ref)
        w_cols[...] = jnp.zeros_like(w_cols)
        w_rows[...] = jnp.zeros_like(w_rows)
        e_rows[...] = jnp.zeros_like(e_rows)
        back[...] = shifts(13, 3, 1)
        ahead[...] = shifts(1, 3, 1)
        shut[...] = jnp.where(lanes >= rows, 0.0, NEG)

    @pl.when(step_id < blocks - 1)
    def _():
        prior[...] = before_ref[...]

    @pl.when(step_id == blocks - 1)
    def _():
        prior[...] = jnp.zeros_like(prior)

    low_half = lanes < P_SIZE
    steps = st_ref[...]
    rate = rate_ref[...]
    lam = mm_exact((rows >= lanes).astype(F32), steps * rate)
    lam_t = lam.T
    source = lam - jnp.log(steps)
    grown = jnp.exp(lam)
    last = lam[Q - 1 : Q, :]
    weight = jnp.exp(last - lam) * steps
    fade = jnp.exp(last)
    b_rows = bc_ref[:, :N]
    c_rows = bc_ref[:, N:]
    c_t = turned(c_rows)
    scores_t = nt_dot(b_rows, c_rows)
    for pair in range(pairs):
        cols = slice(pair * LANES, (pair + 1) * LANES)
        first = 2 * pair
        seen, half, bend = open_chunk(taps_ref, back, prior, vp_ref, cols)
        x = half * bend + half
        dy = dy_ref[:, cols]
        dy_wide = dy.astype(F32)
        q_t = nt_dot(halves(low_half, x).astype(BF16), dy)
        mixing = []
        crossed = None
        for at, h in enumerate((first, first + 1)):
            decay = jnp.exp(lam_t[h : h + 1, :] - source[:, h : h + 1] + shut[...])
            stepped = decay * q_t[at * Q : (at + 1) * Q]
            crossed = stepped if crossed is None else crossed + stepped
            both = stepped * scores_t
            w_cols[:, h : h + 1] = jnp.sum(both, axis=1, keepdims=True)
            w_rows[h : h + 1, :] = jnp.sum(both, axis=0, keepdims=True)
            mixing.append((decay * scores_t).astype(BF16))
        if pair == 0:
            across[...] = crossed
        else:
            across[...] += crossed
        dx = mm(jnp.concatenate(mixing, axis=1), halves(low_half, dy_wide).astype(BF16))
        d_state = ds[:, cols]
        d_state_low = d_state.astype(BF16)
        ds_low[:, cols] = d_state_low
        weight_pair = pair_cols(low_half, weight, first)
        carried = weight_pair * mm(b_rows, d_state_low)
        dx = dx + carried + skip_ref[:, cols] * dy_wide
        state_terms[:, cols] = (x * carried).astype(BF16)
        fed_all[:, cols] = (x * weight_pair).astype(BF16)
        held = hold_ref[0, :, cols]
        dyl = dy_wide * pair_cols(low_half, grown, first)
        dyl_low = dyl.astype(BF16)
        dyl_all[:, cols] = dyl_low
        inter_terms[:, cols] = (dyl * mm(c_rows, held)).astype(BF16)
        e_rows[0:1, cols] = jnp.sum(d_state * held.astype(F32), axis=0, keepdims=True)
        ds[:, cols] = d_state * pair_cols(low_half[0:1], fade, first) + mm(c_t, dyl_low)
        g = dx * ((0.5 + 0.5 * bend) * (1.0 + half * (1.0 - bend)))
        for k in range(4):
            gconv_ref[k : k + 1, cols] += jnp.sum(g * seen[k], axis=0, keepdims=True)
        gconv_ref[4:5, cols] += jnp.sum(g, axis=0, keepdims=True)
        gconv_ref[5:6, cols] += jnp.sum(dy_wide * x, axis=0, keepdims=True)
        g_low = g.astype(BF16)
        moved = mm(ahead[...], jnp.concatenate([g_low, g_next[:, cols]], axis=0))
        d_pre = taps_ref[3:4, cols] * g
        for k in range(3):
            d_pre = d_pre + taps_ref[2 - k : 3 - k, cols] * moved[k * Q : (k + 1) * Q]
        dvp_ref[:, cols] = (2.0 * d_pre).astype(dvp_ref.dtype)
        g_next[:, cols] = g_low[0:16]
    cross = across[...]
    d_b = mm(cross.astype(BF16), c_rows) + nt_dot(fed_all[...], ds_low[...])
    d_c = mm(turned(cross), b_rows) + nt_dot(dyl_all[...], hold_ref[0])
    dbc_ref[:, :N] = d_b.astype(dbc_ref.dtype)
    dbc_ref[:, N:] = d_c.astype(dbc_ref.dtype)
    pick = pick_ref[...]
    from_state = mm(state_terms[...], pick)
    from_carry = mm(inter_terms[...], pick)
    e_high = e_rows[...].astype(BF16)
    e_rest = (e_rows[...] - e_high.astype(F32)).astype(BF16)
    through = (mm(e_high, pick) + mm(e_rest, pick))[0:1]
    w_all = w_cols[...]
    d_lam = w_rows[...].T - w_all + from_carry
    d_log = (
        mm_exact((lanes >= rows).astype(F32), d_lam)
        + mm_exact((rows > lanes).astype(F32), from_state)
        + fade * through
    )
    dst_ref[...] = (w_all + from_state) / jnp.maximum(steps, 1e-37) + rate * d_log
    gdecay_ref[...] += jnp.sum(steps * d_log, axis=0, keepdims=True)


def chunk_of(i, seat, per):
    return (lax.div(i, per) ^ seat[0]) * per + lax.rem(i, per)


def run_forward(seat, pre, states_in, steps, taps, rate, skip, shards):
    tokens = steps.shape[0]
    width = taps.shape[1]
    blocks = tokens // Q
    per = blocks // shards
    fixed = lambda i, seat: (0, 0)
    plain = lambda i, seat: (i, 0)
    moved = lambda i, seat: (chunk_of(i, seat, per), 0)
    return pl.pallas_call(
        functools.partial(scan_forward, pairs=width // LANES),
        out_shape=(
            jax.ShapeDtypeStruct((tokens, width), BF16),
            jax.ShapeDtypeStruct((blocks, N, width), BF16),
        ),
        grid_spec=pltpu.PrefetchScalarGridSpec(
            num_scalar_prefetch=1,
            grid=(blocks,),
            in_specs=[
                pl.BlockSpec((Q, width), moved),
                pl.BlockSpec((Q, 2 * N), plain),
                pl.BlockSpec((Q, LANES), plain),
                pl.BlockSpec((8, width), fixed),
                pl.BlockSpec((1, LANES), fixed),
                pl.BlockSpec((1, width), fixed),
            ],
            out_specs=[
                pl.BlockSpec((Q, width), moved),
                pl.BlockSpec((1, N, width), lambda i, seat: (i, 0, 0)),
            ],
            scratch_shapes=[
                pltpu.VMEM((N, width), F32),
                pltpu.VMEM((Q + 8, width), F32),
                pltpu.VMEM((Q, Q), F32),
            ],
        ),
        cost_estimate=pl.CostEstimate(
            flops=tokens * width * 1200, bytes_accessed=tokens * width * 10, transcendentals=tokens * width * 3
        ),
        name="scan_forward",
    )(seat, pre, states_in, steps, taps, rate, skip)


def run_backward(seat, pre, dy, states_in, steps, held, taps, rate, skip, pick, shards):
    tokens = steps.shape[0]
    width = taps.shape[1]
    blocks = tokens // Q
    per = blocks // shards
    fixed = lambda i, seat: (0, 0)
    plain = lambda i, seat: (blocks - 1 - i, 0)
    moved = lambda i, seat: (chunk_of(blocks - 1 - i, seat, per), 0)

    def before(i, seat):
        chunk = jnp.maximum(blocks - 2 - i, 0)
        return (chunk_of(chunk, seat, per) * (Q // 16) + Q // 16 - 1, 0)

    return pl.pallas_call(
        functools.partial(scan_backward, pairs=width // LANES, blocks=blocks),
        out_shape=(
            jax.ShapeDtypeStruct((tokens, width), BF16),
            jax.ShapeDtypeStruct((tokens, 2 * N), BF16),
            jax.ShapeDtypeStruct((tokens, LANES), F32),
            jax.ShapeDtypeStruct((8, width), F32),
            jax.ShapeDtypeStruct((1, LANES), F32),
        ),
        grid_spec=pltpu.PrefetchScalarGridSpec(
            num_scalar_prefetch=1,
            grid=(blocks,),
            in_specs=[
                pl.BlockSpec((Q, width), moved),
                pl.BlockSpec((16, width), before),
                pl.BlockSpec((Q, width), moved),
                pl.BlockSpec((Q, 2 * N), plain),
                pl.BlockSpec((Q, LANES), plain),
                pl.BlockSpec((1, N, width), lambda i, seat: (blocks - 1 - i, 0, 0)),
                pl.BlockSpec((8, width), fixed),
                pl.BlockSpec((1, LANES), fixed),
                pl.BlockSpec((1, width), fixed),
                pl.BlockSpec((width, LANES), fixed),
            ],
            out_specs=[
                pl.BlockSpec((Q, width), moved),
                pl.BlockSpec((Q, 2 * N), plain),
                pl.BlockSpec((Q, LANES), plain),
                pl.BlockSpec((8, width), fixed),
                pl.BlockSpec((1, LANES), fixed),
            ],
            scratch_shapes=[
                pltpu.VMEM((16, width), BF16),
                pltpu.VMEM((16, width), BF16),
                pltpu.VMEM((3 * Q, Q + 16), BF16),
                pltpu.VMEM((3 * Q, Q + 16), BF16),
                pltpu.VMEM((Q, Q), F32),
                pltpu.VMEM((N, width), F32),
                pltpu.VMEM((N, width), BF16),
                pltpu.VMEM((Q, Q), F32),
                pltpu.VMEM((Q, LANES), F32),
                pltpu.VMEM((LANES, Q), F32),
                pltpu.VMEM((Q, width), BF16),
                pltpu.VMEM((Q, width), BF16),
                pltpu.VMEM((Q, width), BF16),
                pltpu.VMEM((Q, width), BF16),
                pltpu.VMEM((8, width), F32),
            ],
        ),
        cost_estimate=pl.CostEstimate(
            flops=tokens * width * 3000, bytes_accessed=tokens * width * 14, transcendentals=tokens * width * 4
        ),
        name="scan_backward",
    )(seat, pre, pre, dy, states_in, steps, held, taps, rate, skip, pick)


EPSILON = 1e-05


def swish(v):
    return v * sigmoid(v)


def tn_dot(a, b):
    return lax.dot_general(a, b, (((0,), (0,)), ((), ())), preferred_element_type=F32)


def fill_kernel(*refs, spans):
    gain_ref, w_ref = refs[len(spans) : len(spans) + 2]
    normal_ref, value_ref, small_ref = refs[-3:]
    step_id = pl.program_id(0)
    wide = value_ref.shape[1]
    for (start, stop), piece_ref in zip(spans, refs):

        @pl.when((step_id >= start) & (step_id < stop))
        def _(piece_ref=piece_ref):
            rows = piece_ref[...].astype(F32)
            scale = lax.rsqrt(jnp.mean(rows * rows, axis=1, keepdims=True) + EPSILON)
            normal_ref[...] = (rows * scale * gain_ref[...]).astype(BF16)

    small_ref[...] = mm(normal_ref[...], w_ref[:, wide:])
    value_ref[...] = mm(normal_ref[...], w_ref[:, :wide]).astype(BF16)


def run_fill(pieces, gain, w, into, rows, first, block):
    depth, width = w.shape
    wide = width - LANES
    place = lambda i: (i + first, 0)
    spans = []
    specs = []
    at = 0
    for piece in pieces:
        blocks = piece.shape[0] // block
        spans.append((at, at + blocks))
        specs.append(pl.BlockSpec((block, depth), lambda i, at=at, blocks=blocks: (jnp.clip(i - at, 0, blocks - 1), 0)))
        at += blocks
    return pl.pallas_call(
        functools.partial(fill_kernel, spans=spans),
        out_shape=(
            jax.ShapeDtypeStruct((rows, depth), BF16),
            jax.ShapeDtypeStruct((rows, wide), BF16),
            jax.ShapeDtypeStruct((rows, LANES), F32),
        ),
        grid=(at,),
        in_specs=specs
        + [
            pl.BlockSpec((1, depth), lambda i: (0, 0)),
            pl.BlockSpec((depth, width), lambda i: (0, 0), pipeline_mode=pl.Buffered(1)),
        ]
        + [pl.BlockSpec(memory_space=pl.ANY)] * len(into),
        out_specs=(
            pl.BlockSpec((block, depth), place), pl.BlockSpec((block, wide), place), pl.BlockSpec((block, LANES), place)
        ),
        input_output_aliases={len(pieces) + 2 + k: k for k in range(len(into))},
        cost_estimate=pl.CostEstimate(
            flops=2 * at * block * depth * width,
            bytes_accessed=2 * (at * block + width) * (depth + width),
            transcendentals=0,
        ),
        name="values",
    )(*pieces, gain, w, *into)


def split_kernel(x_ref, w_ref, *out_refs):
    rows = out_refs[0].shape[0]
    for at, out_ref in enumerate(out_refs):
        out_ref[...] = nt_dot(x_ref[at * rows : (at + 1) * rows], w_ref[...]).astype(BF16)


def run_split(x, w, parts, block):
    tokens, depth = x.shape
    width = w.shape[0]
    rows = tokens // parts
    return pl.pallas_call(
        split_kernel,
        out_shape=[jax.ShapeDtypeStruct((rows, width), BF16)] * parts,
        grid=(width // block,),
        in_specs=[
            pl.BlockSpec((tokens, depth), lambda i: (0, 0), pipeline_mode=pl.Buffered(1)),
            pl.BlockSpec((block, depth), lambda i: (i, 0)),
        ],
        out_specs=[pl.BlockSpec((rows, block), lambda i: (0, i))] * parts,
        cost_estimate=pl.CostEstimate(
            flops=2 * tokens * depth * width, bytes_accessed=2 * (tokens + width) * depth + 2 * tokens * width, transcendentals=0
        ),
        name="split",
    )(x, w)


def rows_kernel(*refs):
    w_gate_ref, w_cat_ref = refs[6:8]
    wide = refs[2].shape[1]
    for at in range(2):
        gate_ref, value_ref, small_ref = refs[at:6:2]
        total = nt_dot(gate_ref[...], w_gate_ref[...])
        total = total + nt_dot(value_ref[...], w_cat_ref[:, :wide])
        total = total + nt_dot(small_ref[...], w_cat_ref[:, wide:])
        refs[8 + at][...] = total.astype(BF16)


def run_rows(blocks, d_gate, d_value, d_small, w_gate, w_cat, rows, block):
    width = w_gate.shape[0]
    depth = w_gate.shape[1] + w_cat.shape[1]
    given = [v for v in (d_gate, d_value, d_small) for _ in blocks]
    specs = [
        pl.BlockSpec((rows, v.shape[1]), lambda i, at=at: (at, 0), pipeline_mode=pl.Buffered(1))
        for v in (d_gate, d_value, d_small)
        for at in blocks
    ]
    return pl.pallas_call(
        rows_kernel,
        out_shape=[jax.ShapeDtypeStruct((rows, width), BF16)] * 2,
        grid=(width // block,),
        in_specs=specs
        + [
            pl.BlockSpec((block, w_gate.shape[1]), lambda i: (i, 0)),
            pl.BlockSpec((block, w_cat.shape[1]), lambda i: (i, 0)),
        ],
        out_specs=[pl.BlockSpec((rows, block), lambda i: (0, i))] * 2,
        cost_estimate=pl.CostEstimate(
            flops=4 * rows * depth * width, bytes_accessed=2 * (2 * rows + width) * depth + 4 * rows * width, transcendentals=0
        ),
        name="rows",
    )(*given, w_gate, w_cat)


def turned_kernel(a_ref, b_ref, out_ref):
    out_ref[...] = tn_dot(a_ref[...], b_ref[...]).astype(BF16)


def run_turned(a, b, block):
    tokens, depth = a.shape
    width = b.shape[1]
    return pl.pallas_call(
        turned_kernel,
        out_shape=jax.ShapeDtypeStruct((depth, width), BF16),
        grid=(depth // block,),
        in_specs=[
            pl.BlockSpec((tokens, block), lambda i: (0, i)),
            pl.BlockSpec((tokens, width), lambda i: (0, 0), pipeline_mode=pl.Buffered(1)),
        ],
        out_specs=pl.BlockSpec((block, width), lambda i: (i, 0)),
        cost_estimate=pl.CostEstimate(
            flops=2 * tokens * depth * width, bytes_accessed=2 * (tokens * (depth + width) + depth * width), transcendentals=0
        ),
        name="weights",
    )(a, b)


def joined_kernel(*refs):
    b_ref, out_ref, full_ref = refs[-3:]
    at = 0
    for piece_ref in refs[:-3]:
        rows = piece_ref.shape[0]
        full_ref[at : at + rows] = piece_ref[...]
        at += rows
    out_ref[...] = tn_dot(full_ref[...], b_ref[...]).astype(BF16)


def run_joined(pieces, b, block):
    tokens, width = b.shape
    depth = pieces[0].shape[1]
    return pl.pallas_call(
        joined_kernel,
        out_shape=(jax.ShapeDtypeStruct((depth, width), BF16), jax.ShapeDtypeStruct((tokens, depth), BF16)),
        grid=(depth // block,),
        in_specs=[pl.BlockSpec((piece.shape[0], block), lambda i: (0, i)) for piece in pieces]
        + [pl.BlockSpec((tokens, width), lambda i: (0, 0), pipeline_mode=pl.Buffered(1))],
        out_specs=(pl.BlockSpec((block, width), lambda i: (i, 0)), pl.BlockSpec((tokens, block), lambda i: (0, i))),
        cost_estimate=pl.CostEstimate(
            flops=2 * tokens * depth * width, bytes_accessed=2 * (tokens * (2 * depth + width) + depth * width), transcendentals=0
        ),
        name="joined",
    )(*pieces, b)


def causal_conv(values, taps, offsets):
    tap_count = taps.shape[0]
    length = values.shape[0]
    padded = jnp.pad(values, ((tap_count - 1, 0), (0, 0)))
    summed = offsets[None, :] + taps[0][None, :] * padded[0:length]
    for offset in range(1, tap_count):
        summed = summed + taps[offset][None, :] * padded[offset : offset + length]
    return summed


def swap(v, bit, axis="col"):
    size = lax.axis_size(axis)
    return lax.ppermute(v, axis, [(i, i ^ bit) for i in range(size)])


def row_sum(v):
    bit = 1
    while bit < lax.axis_size("row"):
        v = v + swap(v, bit, "row")
        bit *= 2
    return v


class Square:
    shards = 4

    def __init__(self):
        self.place = lax.axis_index("col")
        self.x = lax.rem(self.place, 2) == 1
        self.y = lax.div(self.place, 2) == 1
        self.seat = jnp.reshape(self.place, (1,)).astype(jnp.int32)

    def settle(self, v):
        parts = v.reshape((2, 2, v.shape[0] // 4) + v.shape[1:])
        parts = jnp.where(self.y, parts[::-1], parts)
        parts = jnp.where(self.x, parts[:, ::-1], parts)
        return parts.reshape(v.shape)

    def gather_whole(self, v):
        from_x, from_y = swap(v, 1), swap(v, 2)
        half = v.shape[0] // 2
        relay_y = swap(from_x[:half], 2)
        relay_x = swap(from_y[half:], 1)
        return [v, from_x, from_y, relay_y, relay_x]

    def gather_top(self, v):
        first, rest = v[: v.shape[0] // 4], v[v.shape[0] // 4 :]
        return [v, rest, swap(first, 1), swap(first, 2)]

    def gather_low(self, parts):
        v, rest, x_first, y_first = parts
        x_rest, y_rest = swap(rest, 1), swap(rest, 2)
        far_first = swap(y_first, 1)
        return [v, x_first, x_rest, y_first, y_rest, far_first]

    def gather_far(self, pieces):
        quarter = pieces[1].shape[0]
        far_middle = swap(pieces[2][: 2 * quarter], 2)
        far_last = swap(pieces[4][2 * quarter :], 1)
        return pieces + [far_middle, far_last]

    def gather_flat(self, v):
        others = [swap(v, bit) for bit in (1, 2, 3)]
        return self.settle(jnp.concatenate([v] + others))

    def token_sum(self, v):
        parts = v.reshape(2, 2, -1)
        parts = parts + swap(parts, 1)[:, ::-1]
        parts = parts + swap(parts, 2)[::-1]
        return parts.reshape(v.shape)

    def total(self, v):
        v = v + swap(v, 1)
        return v + swap(v, 2)

    def scatter_far(self, far_top, far_low):
        return swap(far_top, 1), swap(far_low, 2)

    def scatter_near(self, x_top, y_low):
        return swap(x_top, 1), swap(y_low, 2)

    def scatter_add(self, x_low, y_top, far_came):
        across_x, across_y = far_came
        return [
            (x_low.astype(F32) + across_y.astype(F32)).astype(BF16),
            (y_top.astype(F32) + across_x.astype(F32)).astype(BF16),
        ]

    def scatter_end(self, sent, own, near_came):
        x_low, y_top = swap(sent[0], 1), swap(sent[1], 2)
        top, low, x_top, y_low = (v.astype(F32) for v in (*own, *near_came))
        return jnp.concatenate([top + x_top + y_top.astype(F32), low + x_low.astype(F32) + y_low])

    def dense_swap(self, v, bit):
        half, width = v.shape[0] // 2, v.shape[1]
        came = swap(jnp.concatenate([v[:half], v[half:]], axis=1), bit)
        return jnp.concatenate([came[:, :width], came[:, width:]])

    def gather_states(self, s):
        pair = jnp.concatenate([s, self.dense_swap(s, 1)], axis=1)
        other = jnp.concatenate([self.dense_swap(s, 2), self.dense_swap(s, 3)], axis=1)
        return jnp.concatenate([jnp.where(self.y, other, pair), jnp.where(self.y, pair, other)], axis=1)

    def split_states(self, d):
        first, second = d[:, :N], d[:, N:]
        kept = jnp.where(self.y, second, first)
        given = jnp.where(self.y, first, second)
        half = N // 2
        return [kept[:, :half], kept[:, half:], given[:, :half], given[:, half:]]

    def scatter_states(self, parts):
        own = parts[0].astype(F32)
        for bit in (1, 2, 3):
            own = own + self.dense_swap(parts[bit], bit).astype(F32)
        return own

    def own_slice(self, v):
        width = v.shape[0] // 4
        return lax.dynamic_slice(v, (self.place * width,), (width,))


class Line:
    shards = 1

    def __init__(self):
        self.seat = jnp.zeros((1,), jnp.int32)

    def settle(self, v):
        return v

    def gather_whole(self, v):
        return [lax.all_gather(v, "col", axis=0, tiled=True)]

    def gather_top(self, v):
        return self.gather_whole(v)

    def gather_low(self, parts):
        return parts

    def gather_far(self, pieces):
        return pieces

    def gather_flat(self, v):
        return lax.all_gather(v, "col", axis=0, tiled=True)

    def token_sum(self, v):
        return lax.psum(v, "col")

    def total(self, v):
        return lax.psum(v, "col")

    def scatter_whole(self, v):
        return lax.psum_scatter(v, "col", scatter_dimension=0, tiled=True).astype(F32)

    def gather_states(self, s):
        return lax.all_gather(s, "col", axis=1, tiled=True)

    def split_states(self, d):
        return [d]

    def scatter_states(self, parts):
        return lax.psum_scatter(parts[0].astype(BF16), "col", scatter_dimension=1, tiled=True).astype(F32)

    def own_slice(self, v):
        width = v.shape[0] // lax.axis_size("col")
        return lax.dynamic_slice(v, (lax.axis_index("col") * width,), (width,))


def widened(v, width):
    return v if v.shape[-1] == width else jnp.pad(v, [(0, 0)] * (v.ndim - 1) + [(0, width - v.shape[-1])])


def tied(*values):
    return lax.optimization_barrier(values)


def row_scatter_small(v):
    bit = lax.axis_size("row") // 2
    place = lax.axis_index("row")
    while bit:
        half = v.shape[0] // 2
        upper = lax.rem(lax.div(place, bit), 2) == 1
        kept = jnp.where(upper, v[half:], v[:half])
        given = jnp.where(upper, v[:half], v[half:])
        v = kept + swap(given.astype(BF16), bit, "row").astype(F32)
        bit //= 2
    return v


def row_scatter(v):
    return lax.psum_scatter(v, "row", scatter_dimension=0, tiled=True)


def body(
    hidden,
    in_gain,
    w_gate,
    w_value,
    w_bc,
    w_step,
    conv_value,
    conv_value_bias,
    conv_bc,
    conv_bc_bias,
    step_bias,
    decay_log,
    skip_gain,
    norm_gain,
    w_out,
    grad_out,
):
    lines = Square() if lax.axis_size("col") == 4 else Line()
    heads = step_bias.shape[0]
    channels = w_value.shape[1]
    inner_width = lax.axis_size("col") * channels
    bc_width = w_bc.shape[1]
    wide = -(-channels // LANES) * LANES
    full_width = wide + LANES
    piece_rows = hidden.shape[0]

    w_cat = lax.all_gather(
        widened(jnp.concatenate([widened(w_value, wide), w_bc, w_step], axis=1), full_width),
        "row", axis=0, tiled=True,
    )
    w_gate_full = lax.all_gather(w_gate, "row", axis=0, tiled=True)
    w_out_t = lax.all_gather(w_out.T, "row", axis=0, tiled=True)
    full_gain = lines.gather_flat(in_gain).astype(F32)

    def weight_grad(a, b):
        return run_turned(a, b, 256) if lines.shards == 4 else tn_dot(a, b).astype(BF16)

    def normalized(rows):
        rows = rows.astype(F32)
        scale = lax.rsqrt(jnp.mean(rows * rows, axis=1, keepdims=True) + EPSILON)
        return (rows * scale * full_gain).astype(BF16)

    hidden_pieces = lines.gather_whole(hidden)
    grad_source, hidden_pieces[-1] = tied(grad_out, hidden_pieces[-1])
    grad_pieces = lines.gather_top(grad_source)
    near, far = hidden_pieces[:3], hidden_pieces[3:]

    if far:
        tokens_here = 4 * piece_rows
        half_rows = piece_rows // 2
        filled = run_fill(near, full_gain[None], w_cat, (), tokens_here, 0, half_rows)
        filled = run_fill(far, full_gain[None], w_cat, filled, tokens_here, 6, half_rows)
        normal_in, pre, pre_small = filled
    else:
        normal_in = normalized(near[0])
        pre = mm(normal_in, w_cat[:, :wide]).astype(BF16)
        pre_small = mm(normal_in, w_cat[:, wide:])
    bc_pre = lines.settle(pre_small[:, :bc_width])
    step_sum = lines.settle(pre_small[:, bc_width : bc_width + heads]) + step_bias

    def state_branch(pre_vals, conv_weight, conv_offset):
        return swish(causal_conv(pre_vals, conv_weight, conv_offset))

    state_local, state_back = jax.vjp(state_branch, bc_pre, conv_bc, conv_bc_bias)
    states = lines.gather_states(state_local.astype(BF16))
    steps = widened(jax.nn.softplus(step_sum), LANES)
    rate = widened(-jnp.exp(decay_log), LANES)[None]
    skip = widened(jnp.repeat(skip_gain, P_SIZE), wide)[None]
    taps = 0.5 * jnp.concatenate([conv_value, conv_value_bias[None], jnp.zeros((3, channels), F32)])
    taps = widened(taps, wide)
    pick = (jnp.arange(wide)[:, None] // P_SIZE == jnp.arange(LANES)[None]).astype(BF16)
    states, *grad_pieces[:2] = tied(states, *grad_pieces[:2])
    grad_pieces = lines.gather_low(grad_pieces)
    heads_out, held = run_forward(lines.seat, pre, states, steps, taps, rate, skip, lines.shards)

    gate_pre = mm(normal_in, w_gate_full).astype(BF16)
    ho = heads_out[:, :channels].astype(F32)
    gate = gate_pre.astype(F32)
    gated = ho * swish(gate)
    squares = jnp.sum(gated * gated, axis=1)
    squares, *grad_pieces = tied(squares, *grad_pieces)
    grad_pieces = lines.gather_far(grad_pieces)
    squares = lines.token_sum(squares)
    mix = lax.rsqrt(squares / inner_width + EPSILON)[:, None]
    normed = (gated * mix * norm_gain).astype(BF16)

    if lines.shards == 4:
        g_out_part, grad_full = run_joined(grad_pieces, normed, 256)
    else:
        grad_full = grad_pieces[0]
        g_out_part = weight_grad(grad_full, normed)
    w_out_t, g_out_part = tied(w_out_t, g_out_part)
    g_out_t = row_scatter(g_out_part)
    d_normed = mm(grad_full, w_out_t).astype(BF16).astype(F32)
    scaled = d_normed * norm_gain
    dots = jnp.sum(gated * scaled, axis=1)
    w_out_t, dots = tied(w_out_t, dots)
    if lines.shards == 4:
        out_parts = run_split(normed, w_out_t, 8, 512)
        early_far = lines.scatter_far(*out_parts[6:])
        early_near = lines.scatter_near(out_parts[2], out_parts[5])
    else:
        branch_out = lines.scatter_whole(nt_dot(normed, w_out_t).astype(BF16))
    dots = lines.token_sum(dots)[:, None]
    d_gated = mix * scaled - gated * (mix * mix * mix * dots / inner_width)
    g_norm_gain = jnp.sum(d_normed * gated * mix, axis=0)
    open_gate = sigmoid(gate)
    d_heads = (d_gated * gate * open_gate).astype(BF16)
    d_gate = (d_gated * ho * (open_gate * (1.0 + gate * (1.0 - open_gate)))).astype(BF16)
    g_gate_part = weight_grad(normal_in, d_gate)
    if lines.shards == 4:
        early_sent = lines.scatter_add(out_parts[3], out_parts[4], early_far)
        d_heads, g_gate_part, *early_sent = tied(d_heads, g_gate_part, *early_sent)
    g_gate_sent, g_out_t = tied(g_gate_part, g_out_t)
    g_gate = row_scatter(g_gate_sent)

    d_value, d_states, d_steps, g_conv, g_decay = run_backward(
        lines.seat, pre, widened(d_heads, wide), states, steps, held, taps, rate, skip, pick, lines.shards
    )
    state_parts = lines.split_states(d_states)
    normal_in, *state_parts = tied(normal_in, *state_parts)
    g_value_part = weight_grad(normal_in, d_value)
    g_value_sent, g_gate = tied(g_value_part, g_gate)
    g_value = row_scatter(g_value_sent)
    d_state_local, g_value_part = tied(lines.scatter_states(state_parts), g_value_part)
    d_bc_pre, g_conv_bc, g_conv_bc_bias = state_back(d_state_local)
    d_step = d_steps[:, :heads] * sigmoid(step_sum)
    small = lines.settle(widened(jnp.concatenate([d_bc_pre, d_step], axis=1), LANES)).astype(BF16)
    small, d_value, g_value_part = tied(small, d_value, g_value_part)
    parts = (
        g_conv[:4, :channels],
        g_conv[4, :channels],
        g_conv_bc,
        g_conv_bc_bias,
        jnp.sum(d_step, axis=0),
        (g_decay * rate)[0, :heads],
        jnp.sum(g_conv[5, :channels].reshape(heads, P_SIZE), axis=1),
        g_norm_gain,
    )

    def small_and_gain(normal, from_gate, from_value):
        from_small = tn_dot(normal, small)
        return from_small, gain_sums(w_gate_full, from_gate, w_cat, from_value, from_small) / full_gain

    if lines.shards == 4:
        row_parts = {}
        turn = d_value
        for name, blocks in (("rows_far", (6, 7)), ("rows_near", (2, 5)), ("rows_next", (3, 4)), ("rows_own", (0, 1))):
            row_parts[name] = run_rows(blocks, d_gate, turn, small, w_gate_full, w_cat, piece_rows // 2, 512)
            turn, *row_parts[name] = tied(turn, *row_parts[name])
            if name == "rows_far":
                far_came = lines.scatter_far(*row_parts[name])
            elif name == "rows_near":
                near_came = lines.scatter_near(*row_parts[name])
                turn, normal_in, g_gate_part, g_value_part = tied(turn, normal_in, g_gate_part, g_value_part)
                g_small_part, g_in_gain = small_and_gain(normal_in, g_gate_part, g_value_part)
                turn, g_small_part, g_in_gain = tied(turn, g_small_part, g_in_gain)
            elif name == "rows_next":
                sent = lines.scatter_add(*row_parts[name], far_came)
                turn, g_small_part, g_in_gain, *sent = tied(turn, g_small_part, g_in_gain, *sent)
        own = row_parts["rows_own"]
        own[0], *early_near = tied(own[0], *early_near)
        d_rows = lines.scatter_end(sent, own, near_came)
        branch_out = lines.scatter_end(early_sent, out_parts[:2], early_near)
    else:
        g_small_part, g_in_gain = small_and_gain(normal_in, g_gate_part, g_value_part)
        d_cat = jnp.concatenate([d_value, small], axis=1)
        d_rows = lines.scatter_whole((nt_dot(d_gate, w_gate_full) + nt_dot(d_cat, w_cat)).astype(BF16))
    result = (hidden.astype(F32) + branch_out).astype(BF16)
    g_small = row_scatter_small(g_small_part)

    tokens = hidden.astype(F32)
    scale = lax.rsqrt(jnp.mean(tokens * tokens, axis=1, keepdims=True) + EPSILON)
    scaled_rows = d_rows * full_gain
    grad_hidden = grad_out.astype(F32) + scale * (
        scaled_rows - tokens * (scale * scale * jnp.mean(tokens * scaled_rows, axis=1, keepdims=True))
    )

    packed = row_sum(jnp.concatenate([part.reshape(-1) for part in parts] + [g_in_gain]))
    summed = []
    at = 0
    for part in parts:
        summed.append(packed[at : at + part.size].reshape(part.shape))
        at += part.size
    g_in_gain = lines.own_slice(lines.total(packed[at:]))
    return (
        result,
        grad_hidden,
        g_in_gain,
        g_gate.astype(F32),
        g_value[:, :channels].astype(F32),
        g_small[:, :bc_width],
        g_small[:, bc_width : bc_width + heads],
        *summed,
        g_out_t.T.astype(F32),
    )


def gain_sums(w_gate, g_gate, w_cat, g_value, g_small):
    wide = g_value.shape[1]
    return (
        jnp.sum(w_gate.astype(F32) * g_gate.astype(F32), axis=1)
        + jnp.sum(w_cat[:, :wide].astype(F32) * g_value.astype(F32), axis=1)
        + jnp.sum(w_cat[:, wide:].astype(F32) * g_small, axis=1)
    )


def solution(mesh):
    over_tokens = P(("row", "col"), None)
    square = P("row", "col")
    across = P(None, "col")
    vector = P("col")
    return jax.shard_map(
        body,
        mesh=mesh,
        in_specs=(
            over_tokens, vector, square, square, square, square, across, vector, across, vector,
            vector, vector, vector, vector, P("col", "row"), over_tokens,
        ),
        out_specs=(
            over_tokens, over_tokens, vector, square, square, square, square, across, vector, across,
            vector, vector, vector, vector, vector, P("col", "row"),
        ),
        check_vma=False,
    )
```
